32 devices in a mesh: ra: 8 (over z, y), dec: 4 (over x, core).
Axes of the slice: x: 2, y: 2, z: 4, core: 2. Of those that a mesh axis runs over, the one named last changes fastest.
Arguments:
- exposures: float32 [2, 1280, 3072], P(None, 'dec', 'ra'), may hold values from -6 to 6
- inv_variance: float32 [2, 1280, 3072], P(None, 'dec', 'ra'), may hold values from 0.25 to 4
- pixel_valid: int32 [2, 1280, 3072], P(None, 'dec', 'ra'), may hold values 0 or 1
- correlation: int32 [4, 8, 2], P('dec', 'ra'), may hold values 0 or 1
- pixel_offset: int32 [4, 8, 2, 2], P('dec', 'ra'), may hold values from -3 to 3
- subpixel: float32 [4, 8, 2, 2], P('dec', 'ra'), may hold values from -0.5 to 0.5
- psf_match: bfloat16 [63, 63], replicated, may hold values from -0.09375 to 0.09375
Outputs:
- matched: float32 [768, 2048], P('dec', 'ra')
- weight_map: float32 [768, 2048], P('dec', 'ra')
The draws below stay inside these ranges and needn't reach their ends.
All inputs are finite; a program needn't handle non-finite values. No bound on the sum of `pixel_valid` or of `correlation` on one device may be relied on, other than what follows from the above.
Results may differ from the reference program's by a relative error of at most 0.007.
Values may be sent and summed in bfloat16 or wider, within the bound.
A program may use at most 128 MiB of HBM per device.

```python
import math
import jax
import jax.numpy as jnp
from jax import lax

MARGIN = 64
KERNEL = 63
EPOCHS = 2
HALF = 31
PROWS = 320
PCOLS = 384
STRIPS = 4
TILES = 8
NROWS = 768
NCOLS = 2048
SROWS = 1280
SCOLS = 3072


def with_ends(drawn, own_key, least, high):
    place = [jax.random.randint(jax.random.fold_in(own_key, axis), (), 0, length) for axis, length in enumerate(drawn.shape)]
    longest = drawn.shape.index(max(drawn.shape))
    neighbour = place[:longest] + [(place[longest] + 1) % drawn.shape[longest]] + place[longest + 1:]
    return drawn.at[tuple(place)].set(least).at[tuple(neighbour)].set(high)


def levels(rng, extent, pieces, low, high):
    loudness = 1.0
    for position, shards_of in pieces:
        steps = jax.random.uniform(jax.random.fold_in(jax.random.fold_in(rng, 6), position), (shards_of,), jnp.float32, low / len(pieces), high / len(pieces))
        loudness = loudness * jnp.repeat(jnp.exp(steps), extent[position] // shards_of).reshape((-1,) + (1,) * (len(extent) - 1 - position))
    return loudness


def centred(stream_key, extent, width, bound, shards=(), kind=jnp.bfloat16):
    values = width * jax.random.normal(stream_key, extent, jnp.float32)
    if shards:
        values = values * levels(stream_key, extent, shards, -0.22, 0.18)
    return jnp.clip(values, -bound, bound).astype(kind)


def setup_inputs(seed: int = 0) -> dict:
    arg_keys = jax.random.split(jax.random.key(seed), 8)
    return {
        "exposures": centred(arg_keys[0], (EPOCHS, SROWS, SCOLS), 1.0, 6.0, ((1, 4), (2, 8)), jnp.float32),
        "inv_variance": jnp.clip(jnp.exp(math.log(4.0) - 2.7725887 * jax.random.uniform(arg_keys[1], (EPOCHS, SROWS, SCOLS), jnp.float32) ** levels(arg_keys[1], (EPOCHS, SROWS, SCOLS), ((1, 4), (2, 8)), -0.2, 0.2)), 0.25, 4.0),
        "pixel_valid": with_ends((jax.random.randint(arg_keys[2], (EPOCHS, SROWS, SCOLS), 0, 8) < 7).astype(jnp.int32), jax.random.fold_in(arg_keys[2], 1), 0, 1),
        "correlation": with_ends((jax.random.randint(arg_keys[3], (STRIPS, TILES, EPOCHS), 0, 4) < 3).astype(jnp.int32), jax.random.fold_in(arg_keys[3], 1), 0, 1),
        "pixel_offset": with_ends(jax.random.randint(arg_keys[4], (STRIPS, TILES, EPOCHS, 2), -3, 4), jax.random.fold_in(arg_keys[4], 1), -3, 3).astype(jnp.int32),
        "subpixel": jnp.clip(jax.random.uniform(arg_keys[5], (STRIPS, TILES, EPOCHS, 2), jnp.float32, -0.5, 0.5) * levels(arg_keys[5], (STRIPS, TILES, EPOCHS, 2), ((0, 4), (1, 8)), -0.4, 0.0), -0.5, 0.5),
        "psf_match": centred(arg_keys[6], (KERNEL, KERNEL), (KERNEL * KERNEL) ** -0.5, 0.09375),
    }


HIGHEST_PRECISION = lax.Precision.HIGHEST


def lanczos_matrix(size_count, shift_value):
    row_ids = jnp.arange(size_count, dtype=jnp.int32)[:, None]
    col_ids = jnp.arange(size_count, dtype=jnp.int32)[None, :]
    where_at = (row_ids - col_ids).astype(shift_value.dtype) + shift_value
    kernel_value = jnp.sinc(where_at) * jnp.sinc(where_at / 3.0)
    return jnp.where(jnp.abs(where_at) < 3.0, kernel_value, jnp.zeros_like(kernel_value))


def warp_tile(images, weights, valid_bits, offsets, fractions, covered):
    row_count, col_count = images.shape[1], images.shape[2]
    numerator = jnp.zeros((row_count, col_count), images.dtype)
    denominator = jnp.zeros((row_count, col_count), images.dtype)
    for which_epoch in range(images.shape[0]):
        shifts = offsets[which_epoch].astype(fractions.dtype) + fractions[which_epoch]
        row_map = lanczos_matrix(row_count, shifts[0])
        col_map = lanczos_matrix(col_count, shifts[1])
        masked = weights[which_epoch] * valid_bits[which_epoch].astype(weights.dtype) * covered[which_epoch].astype(weights.dtype)
        stacked = jnp.concatenate([masked * images[which_epoch], masked], axis=1)
        half_done = jnp.dot(row_map, stacked, precision=HIGHEST_PRECISION)
        numerator = numerator + jnp.dot(half_done[:, :col_count], col_map.T, precision=HIGHEST_PRECISION)
        denominator = denominator + jnp.dot(half_done[:, col_count:], col_map.T, precision=HIGHEST_PRECISION)
    return numerator, denominator


def shift_tiles(values, grid_axis, offset_by, wrapping):
    if wrapping:
        return jnp.roll(values, offset_by, axis=grid_axis)
    size_count = values.shape[grid_axis]
    empty_slab = jnp.zeros_like(lax.slice_in_dim(values, 0, 1, axis=grid_axis))
    if offset_by > 0:
        return jnp.concatenate([empty_slab, lax.slice_in_dim(values, 0, size_count - 1, axis=grid_axis)], axis=grid_axis)
    return jnp.concatenate([lax.slice_in_dim(values, 1, size_count, axis=grid_axis), empty_slab], axis=grid_axis)


def place_margins(values, pixel_axis, grid_axis, wrapping):
    inner_size = values.shape[pixel_axis] - 2 * MARGIN
    summed = lax.slice_in_dim(values, MARGIN, MARGIN + inner_size, axis=pixel_axis)
    from_lower = shift_tiles(lax.slice_in_dim(values, MARGIN + inner_size, inner_size + 2 * MARGIN, axis=pixel_axis), grid_axis, 1, wrapping)
    from_upper = shift_tiles(lax.slice_in_dim(values, 0, MARGIN, axis=pixel_axis), grid_axis, -1, wrapping)
    pad_lower = [(0, 0)] * values.ndim
    pad_lower[pixel_axis] = (0, inner_size - MARGIN)
    pad_upper = [(0, 0)] * values.ndim
    pad_upper[pixel_axis] = (inner_size - MARGIN, 0)
    return summed + jnp.pad(from_lower, pad_lower) + jnp.pad(from_upper, pad_upper)


def reference(exposures, inv_variance, pixel_valid, correlation, pixel_offset, subpixel, psf_match):
    tile_count = STRIPS * TILES

    def one_tile(flat_index):
        strip_index = flat_index // TILES
        tile_index = flat_index - strip_index * TILES

        def tile_block(source):
            starts = (jnp.zeros((), jnp.int32), (strip_index * PROWS).astype(jnp.int32), (tile_index * PCOLS).astype(jnp.int32))
            return lax.dynamic_slice(source, starts, (EPOCHS, PROWS, PCOLS))

        return warp_tile(tile_block(exposures), tile_block(inv_variance), tile_block(pixel_valid), pixel_offset[strip_index, tile_index], subpixel[strip_index, tile_index], correlation[strip_index, tile_index])

    numerator, denominator = lax.map(one_tile, jnp.arange(tile_count, dtype=jnp.int32))
    planes = jnp.stack([numerator, denominator]).reshape(2, STRIPS, TILES, PROWS, PCOLS)
    planes = place_margins(planes, 4, 2, True)
    planes = place_margins(planes, 3, 1, False)
    planes = planes.transpose(0, 1, 3, 2, 4).reshape(2, NROWS, NCOLS)
    weight_map = planes[1]
    coadded = (planes[0] / jnp.maximum(planes[1], 1.0)).astype(jnp.bfloat16)
    wrapped = jnp.concatenate([coadded[:, NCOLS - HALF:], coadded, coadded[:, :HALF]], axis=1)
    padded = jnp.pad(wrapped, ((HALF, HALF), (0, 0)))
    matched = lax.conv_general_dilated(padded.astype(jnp.float32)[None, None], psf_match.astype(jnp.float32)[None, None], (1, 1), "VALID", precision=HIGHEST_PRECISION)[0, 0]
    return matched, weight_map
```

```python
import functools
import math

import jax
import jax.numpy as jnp
from jax import lax
from jax.experimental import pallas as pl
from jax.experimental.pallas import tpu as pltpu
from jax.sharding import PartitionSpec as P

MARGIN = 64
HALF = 31
LANES = 128
BAND = 96
GROUP = 16
F32 = jnp.float32
BF16 = jnp.bfloat16
MESH = pl.DeviceIdType.MESH
SERIES = tuple((-1.0) ** k / math.factorial(2 * k + 1) for k in range(12))


def dot(a, b):
    return jnp.dot(a, b, preferred_element_type=F32)


def dot_t(a, b):
    return lax.dot_general(a, b, (((1,), (1,)), ((), ())), preferred_element_type=F32)


def lanczos(x):
    angle = (jnp.pi / 3.0) * x
    square = angle * angle
    ratio = jnp.full_like(x, SERIES[-1])
    for term in SERIES[-2::-1]:
        ratio = ratio * square + term
    both = ratio * ratio
    return jnp.where(jnp.abs(x) < 3.0, both * (1.0 - (4.0 / 3.0) * square * both), 0.0)


def cyclic(row, shift):
    spread = jnp.broadcast_to(row, (LANES, LANES))
    return pltpu.roll(spread, shift, 1, stride=1, stride_axis=0)


def skewed(row, count, width, shift):
    spread = jnp.broadcast_to(row, (count, row.shape[1]))
    return pltpu.roll(spread, shift, 1, stride=1, stride_axis=0)[:, :width]


def lane_ids(value):
    return lax.broadcasted_iota(jnp.int32, value.shape, 1)


def packed(planes, way):
    first, second = planes[0], planes[1]
    if way:
        first, second = pltpu.roll(first, BAND, 1), pltpu.roll(second, BAND, 1)
    half = first.shape[0] // 2
    upper = jnp.where(lane_ids(first) < BAND, first, pltpu.roll(second, LANES - BAND, 1))
    low, high = second[:half], second[half:]
    lower = jnp.where(lane_ids(low) < LANES // 2, low, pltpu.roll(high, LANES // 2, 1))
    return jnp.concatenate([upper, lower], axis=0).astype(BF16)


def unpacked(value, way):
    value = value.astype(F32)
    half = value.shape[0] // 3
    upper, lower = value[: 2 * half], value[2 * half :]
    lanes = lane_ids(upper)
    first = jnp.where(lanes < BAND, upper, 0.0)
    low = jnp.concatenate([lower, pltpu.roll(lower, LANES // 2, 1)], axis=0)
    high = jnp.where(lanes < BAND, pltpu.roll(upper, BAND, 1), 0.0)
    second = jnp.where(lanes < LANES // 2, low, high)
    if way:
        first, second = pltpu.roll(first, LANES - BAND, 1), pltpu.roll(second, LANES - BAND, 1)
    return first, second


def kernel(
    dims,
    exp_hbm,
    inv_hbm,
    val_hbm,
    cor_hbm,
    off_hbm,
    sub_hbm,
    psf_hbm,
    matched_ref,
    weight_ref,
    exp_ref,
    inv_ref,
    val_ref,
    cor_ref,
    off_ref,
    sub_ref,
    psf_ref,
    tile,
    slab,
    dec_out,
    dec_in,
    dec_core_out,
    dec_core_in,
    mid_out,
    mid_in,
    edge_out,
    edge_in,
    taps,
    bands,
    coadd,
    shifts,
    inner_sum,
    small_sem,
    load_sem,
    dec_send,
    dec_recv,
    dec_core_send,
    dec_core_recv,
    mid_send,
    mid_recv,
    edge_send,
    edge_recv,
    ready,
):
    epochs, prows, pcols, n_ra, n_dec = dims
    rows, cols = prows - 2 * MARGIN, pcols - 2 * MARGIN
    me_ra, me_dec = lax.axis_index("ra"), lax.axis_index("dec")
    prev_ra, next_ra = lax.rem(me_ra + n_ra - 1, n_ra), lax.rem(me_ra + 1, n_ra)
    has_prev, has_next = me_dec > 0, me_dec < n_dec - 1
    is_first, not_first, not_last = me_ra == 0, me_ra > 0, me_ra < n_ra - 1

    small = [
        pltpu.make_async_copy(src, dst, small_sem.at[i])
        for i, (src, dst) in enumerate(
            ((off_hbm, off_ref), (sub_hbm, sub_ref), (cor_hbm, cor_ref), (psf_hbm, psf_ref))
        )
    ]
    segments = (
        slice(0, LANES),
        slice(prows - LANES, prows),
        slice(LANES, prows - LANES),
    )

    def load(e, segment, which):
        src, dst = ((inv_hbm, inv_ref), (val_hbm, val_ref), (exp_hbm, exp_ref))[which]
        return pltpu.make_async_copy(
            src.at[e, segments[segment]], dst.at[e, segments[segment]], load_sem.at[e, segment, which]
        )

    order = [(e, segment) for e in range(epochs) for segment in range(2)]
    order += [(e, 2) for e in range(epochs)]
    loads = [load(e, segment, which) for e, segment in order for which in range(3)]
    for copy in small + loads:
        copy.start()

    barrier = pltpu.get_barrier_semaphore()
    pl.semaphore_signal(barrier, inc=1, device_id=(prev_ra, me_dec), device_id_type=MESH)

    @pl.when(not_last)
    def _():
        pl.semaphore_signal(barrier, inc=1, device_id=(next_ra, me_dec), device_id_type=MESH)

    @pl.when(has_prev)
    def _():
        pl.semaphore_signal(barrier, inc=1, device_id=(me_ra, me_dec - 1), device_id_type=MESH)

    @pl.when(has_next)
    def _():
        pl.semaphore_signal(barrier, inc=1, device_id=(me_ra, me_dec + 1), device_id_type=MESH)

    for copy in small[:3]:
        copy.wait()
    inner = prows - 2 * BAND
    side = 2 * LANES
    start = (prows - side) // 2
    with jax.named_scope("maps"):
        lane = lax.broadcasted_iota(jnp.int32, (8, LANES), 1).astype(F32) - LANES // 2
        which_map = lax.broadcasted_iota(jnp.int32, (8, LANES), 0)
        place = lane
        for e in range(epochs):
            shift_r = off_ref[0, 0, e, 0].astype(F32) + sub_ref[0, 0, e, 0]
            shift_c = off_ref[0, 0, e, 1].astype(F32) + sub_ref[0, 0, e, 1]
            place = jnp.where(which_map == 2 * e, shift_r - lane, place)
            place = jnp.where(which_map == 2 * e + 1, shift_c + lane, place)
        wave = lanczos(place)
        kept = wave.astype(BF16).astype(F32)
        scale = jnp.sum(wave, axis=1, keepdims=True) / jnp.sum(kept, axis=1, keepdims=True)
        across = lax.broadcasted_iota(jnp.int32, (LANES, LANES), 1)
        down = lax.broadcasted_iota(jnp.int32, (LANES, LANES), 0)
        apart = across - down
        near = jnp.abs(apart) < LANES // 2
        ahead, behind = apart <= -LANES // 2, apart >= LANES // 2
        zero = jnp.zeros((LANES, LANES), BF16)

        def masked_map(mask, value):
            return jnp.where(mask, value, 0.0).astype(BF16)

        row_maps, lefts, rights, gains = [], [], [], []
        for e in range(epochs):
            row, col = kept[2 * e : 2 * e + 1], kept[2 * e + 1 : 2 * e + 2]
            gains.append(
                scale[2 * e : 2 * e + 1] * scale[2 * e + 1 : 2 * e + 2] * cor_ref[0, 0, e].astype(F32)
            )
            diagonal = masked_map(near, cyclic(row, LANES // 2))
            straight = cyclic(row, 0)
            middle = jnp.concatenate(
                [masked_map(apart >= 0, straight), masked_map(apart < 0, straight)], axis=1
            )
            row_maps.append((diagonal[:BAND], diagonal[LANES - BAND :], middle))
            turned = cyclic(col, LANES // 2)
            same, up, down_map = (masked_map(m, turned) for m in (near, ahead, behind))
            lefts.append(
                jnp.concatenate(
                    [jnp.concatenate([same, up], axis=1), jnp.concatenate([down_map, same], axis=1)],
                    axis=0,
                )
            )
            rights.append(
                jnp.concatenate(
                    [jnp.concatenate([zero, up], axis=1), jnp.concatenate([down_map, same], axis=1)],
                    axis=0,
                )
            )
        left_map, right_map = jnp.concatenate(lefts, axis=0), jnp.concatenate(rights, axis=0)

    def column_pass(pieces):
        stacked = [jnp.concatenate([p[:, :pcols], p[:, pcols:]], axis=0) for p in pieces]
        left = dot(jnp.concatenate([p[:, :side] for p in stacked], axis=1), left_map)
        right = dot(jnp.concatenate([p[:, pcols - side :] for p in stacked], axis=1), right_map)
        return left[:, :LANES], left[:, LANES:] + right[:, :LANES], right[:, LANES:]

    rim_rows, inner_rows = [], []

    def pixels(e, segment):
        for which in range(3):
            load(e, segment, which).wait()
        at = segments[segment]
        masked = inv_ref[e, at] * val_ref[e, at].astype(F32) * gains[e]
        return jnp.concatenate([(masked * exp_ref[e, at]).astype(BF16), masked.astype(BF16)], axis=1)

    reach = LANES - start
    with jax.named_scope("rim_rows"):
        for e in range(epochs):
            rims = []
            for segment in range(2):
                part = pixels(e, segment)
                rims.append(dot(row_maps[e][segment], part).astype(BF16))
                if segment:
                    slab[e, side - reach : side] = part[:reach]
                else:
                    slab[e, 0:reach] = part[start:]
            rim_rows.append(jnp.concatenate(rims, axis=0))

    with jax.named_scope("rim_columns"):
        for block, value in enumerate(column_pass(rim_rows)):
            where = slice(block * LANES, (block + 1) * LANES)
            for plane in range(2):
                for way in range(2):
                    part = value[(2 * plane + way) * BAND : (2 * plane + way + 1) * BAND]
                    tile[plane, way * (prows - BAND) : way * (prows - BAND) + BAND, where] = part
                    if block == 1:
                        dec_core_out[way, plane] = part.astype(BF16)
                    else:
                        dec_out[way, plane, :, block // 2 * LANES : (block // 2 + 1) * LANES] = (
                            part.astype(BF16)
                        )
    with jax.named_scope("barrier"):
        pl.semaphore_wait(
            barrier,
            1 + not_first.astype(jnp.int32) + has_prev.astype(jnp.int32) + has_next.astype(jnp.int32),
        )

    def dec_copy(way):
        return pltpu.make_async_remote_copy(
            src_ref=dec_out.at[way],
            dst_ref=dec_in.at[way],
            send_sem=dec_send.at[way],
            recv_sem=dec_recv.at[way],
            device_id=(me_ra, me_dec + (1 if way else -1)),
            device_id_type=MESH,
        )

    def dec_core_copy(way):
        return pltpu.make_async_remote_copy(
            src_ref=dec_core_out.at[way],
            dst_ref=dec_core_in.at[way],
            send_sem=dec_core_send.at[way],
            recv_sem=dec_core_recv.at[way],
            device_id=(me_ra, me_dec + (1 if way else -1)),
            device_id_type=MESH,
        )

    def mid_copy(way):
        return pltpu.make_async_remote_copy(
            src_ref=mid_out.at[way],
            dst_ref=mid_in.at[way],
            send_sem=mid_send.at[way],
            recv_sem=mid_recv.at[way],
            device_id=(next_ra if way else prev_ra, me_dec),
            device_id_type=MESH,
        )

    def edge_copy(way, part):
        return pltpu.make_async_remote_copy(
            src_ref=edge_out.at[way, part],
            dst_ref=edge_in.at[way, part],
            send_sem=edge_send.at[way, part],
            recv_sem=edge_recv.at[way, part],
            device_id=(next_ra if way else prev_ra, me_dec),
            device_id_type=MESH,
        )

    @pl.when(has_prev)
    def _():
        dec_copy(0).start()
        dec_core_copy(0).start()

    @pl.when(has_next)
    def _():
        dec_copy(1).start()
        dec_core_copy(1).start()

    @pl.when(jnp.logical_not(not_last))
    def _():
        pl.semaphore_signal(ready, inc=1, device_id=(next_ra, me_dec), device_id_type=MESH)

    with jax.named_scope("inner"):
        for e in range(epochs):
            slab[e, reach : side - reach] = pixels(e, 2)
            inner_rows.append(dot(row_maps[e][2], slab[e]).astype(BF16))
        for block, value in enumerate(column_pass(inner_rows)):
            where = slice(block * LANES, (block + 1) * LANES)
            for plane in range(2):
                tile[plane, BAND : BAND + inner, where] = value[plane * inner : (plane + 1) * inner]

    ends = (slice(0, LANES), slice(pcols - LANES, pcols))
    core = slice(2 * MARGIN, prows - 2 * MARGIN)
    with jax.named_scope("mid_send"):
        for way in range(2):
            mid_out[way] = packed(tile[:, core, ends[way]], way)
        mid_copy(1).start()

        @pl.when(not_first)
        def _():
            mid_copy(0).start()

    edges = (
        slice(2 * MARGIN - BAND, 2 * MARGIN),
        slice(prows - 2 * MARGIN, prows - 2 * MARGIN + BAND),
    )
    with jax.named_scope("edges"):
        for part, present in ((0, has_prev), (1, has_next)):

            @pl.when(present)
            def _():
                dec_copy(1 - part).wait_recv()
                for end in range(2):
                    tile[:, edges[part], ends[end]] += dec_in[
                        1 - part, :, :, end * LANES : (end + 1) * LANES
                    ].astype(F32)

            for way in range(2):
                edge_out[way, part] = packed(tile[:, edges[part], ends[way]], way)
            edge_copy(1, part).start()

            @pl.when(not_first)
            def _():
                edge_copy(0, part).start()

    small[3].wait()
    side_k = psf_ref.shape[0]
    taps[...] = jnp.zeros_like(taps)
    taps[0:side_k, 0 : psf_ref.shape[1]] = psf_ref[...].astype(F32)
    offset = MARGIN - HALF

    def build(k, carry):
        for s in range(GROUP // 2):
            for parity in range(2):
                row = taps[pl.ds(k * GROUP + 2 * s + parity, 1), :]
                matrix = skewed(row, LANES, 2 * LANES, offset).astype(BF16)
                for end in range(2):
                    first = (2 * end + parity) * LANES
                    bands[k, first : first + LANES, s * LANES : (s + 1) * LANES] = matrix[
                        :, (1 - end) * LANES : (2 - end) * LANES
                    ]
        return carry

    with jax.named_scope("bands"):
        lax.fori_loop(0, bands.shape[0], build, 0)

    span = coadd.shape[0]
    row_id = lax.broadcasted_iota(jnp.int32, (span, 1), 0) - HALF + me_dec * rows
    inside = (row_id >= 0) & (row_id < n_dec * rows)
    deep, tall = shifts.shape[1], rows + GROUP

    def spread(slot, where):
        numer = tile[0, offset : offset + span, where]
        denom = tile[1, offset : offset + span, where]
        coadd[:, where] = jnp.where(inside, numer / jnp.maximum(denom, 1.0), 0.0).astype(BF16)
        for s in range(GROUP // 2):
            shifts[slot, :, s * LANES : (s + 1) * LANES] = coadd[2 * s : 2 * s + deep, where]

    def product(slot, k, chosen):
        return dot_t(shifts[slot, k * GROUP : k * GROUP + tall, :], bands[k, chosen, :])

    for part, present in ((0, has_prev), (1, has_next)):

        @pl.when(present)
        def _():
            dec_core_copy(1 - part).wait_recv()
            tile[:, edges[part], LANES : 2 * LANES] += dec_core_in[1 - part].astype(F32)

    with jax.named_scope("middle"):
        spread(2, slice(LANES, 2 * LANES))
        total = product(2, 0, slice(None))
        for k in range(1, bands.shape[0]):
            total = total + product(2, k, slice(None))
        inner_sum[...] = total

    @pl.when(is_first)
    def _():
        pl.semaphore_wait(ready, 1)
        mid_copy(0).start()
        for part in range(2):
            edge_copy(0, part).start()

    with jax.named_scope("mid_receive"):
        for way in range(2):
            mid_copy(way).wait_recv()
            for plane, part in enumerate(unpacked(mid_in[way], way)):
                tile[plane, core, ends[1 - way]] += part
    with jax.named_scope("edge_receive"):
        for part in range(2):
            for way in range(2):
                edge_copy(way, part).wait_recv()
                for plane, value in enumerate(unpacked(edge_in[way, part], way)):
                    tile[plane, edges[part], ends[1 - way]] += value
    with jax.named_scope("ends_spread"):
        for end in range(2):
            spread(end, ends[end])
    with jax.named_scope("ends_product"):
        totals = [
            inner_sum[:, end * 2 * LANES : (end + 1) * 2 * LANES] for end in range(2)
        ]
        for k in range(bands.shape[0]):
            for end in range(2):
                totals[end] = totals[end] + product(
                    end, k, slice((1 - end) * 2 * LANES, (2 - end) * 2 * LANES)
                )
        for end in range(2):
            matched_ref[:, end * LANES : (end + 1) * LANES] = (
                totals[end][:rows, :LANES] + totals[end][1 : rows + 1, LANES:]
            )
    weight_ref[...] = tile[1, MARGIN : MARGIN + rows, MARGIN : MARGIN + cols]

    @pl.when(has_prev)
    def _():
        dec_copy(0).wait_send()
        dec_core_copy(0).wait_send()

    @pl.when(has_next)
    def _():
        dec_copy(1).wait_send()
        dec_core_copy(1).wait_send()

    for way in range(2):
        mid_copy(way).wait_send()
        for part in range(2):
            edge_copy(way, part).wait_send()


def finish(matched_in, weight_in, matched_out, weight_out, sems):
    copies = [
        pltpu.make_async_copy(matched_in, matched_out, sems.at[0]),
        pltpu.make_async_copy(weight_in, weight_out, sems.at[1]),
    ]
    for copy in copies:
        copy.start()
    for copy in copies:
        copy.wait()


def solution(mesh):
    n_ra, n_dec = mesh.shape["ra"], mesh.shape["dec"]

    def shards(exposures, inv_variance, pixel_valid, correlation, pixel_offset, subpixel, psf_match):
        epochs, prows, pcols = exposures.shape
        rows, cols = prows - 2 * MARGIN, pcols - 2 * MARGIN
        groups = -(-psf_match.shape[0] // GROUP)
        deep = rows + GROUP * groups
        result = jax.ShapeDtypeStruct((rows, cols), F32)
        hbm = pl.BlockSpec(memory_space=pltpu.HBM)
        vmem = pl.BlockSpec(memory_space=pltpu.VMEM)
        sums = pl.pallas_call(
            functools.partial(kernel, (epochs, prows, pcols, n_ra, n_dec)),
            out_shape=(result, result),
            in_specs=[hbm] * 7,
            out_specs=(vmem, vmem),
            scratch_shapes=[
                pltpu.VMEM((epochs, prows, pcols), F32),
                pltpu.VMEM((epochs, prows, pcols), F32),
                pltpu.VMEM((epochs, prows, pcols), jnp.int32),
                pltpu.SMEM(correlation.shape, jnp.int32),
                pltpu.SMEM(pixel_offset.shape, jnp.int32),
                pltpu.SMEM(subpixel.shape, F32),
                pltpu.VMEM(psf_match.shape, BF16),
                pltpu.VMEM((2, prows, pcols), F32),
                pltpu.VMEM((epochs, 2 * LANES, 2 * pcols), BF16),
                pltpu.VMEM((2, 2, BAND, 2 * LANES), BF16),
                pltpu.VMEM((2, 2, BAND, 2 * LANES), BF16),
                pltpu.VMEM((2, 2, BAND, LANES), BF16),
                pltpu.VMEM((2, 2, BAND, LANES), BF16),
                pltpu.VMEM((2, (prows - 4 * MARGIN) * 3 // 2, LANES), BF16),
                pltpu.VMEM((2, (prows - 4 * MARGIN) * 3 // 2, LANES), BF16),
                pltpu.VMEM((2, 2, BAND * 3 // 2, LANES), BF16),
                pltpu.VMEM((2, 2, BAND * 3 // 2, LANES), BF16),
                pltpu.VMEM((groups * GROUP, 2 * LANES), F32),
                pltpu.VMEM((groups, 4 * LANES, GROUP // 2 * LANES), BF16),
                pltpu.VMEM((deep + GROUP, pcols), BF16),
                pltpu.VMEM((3, deep, GROUP // 2 * LANES), BF16),
                pltpu.VMEM((rows + GROUP, 4 * LANES), F32),
                pltpu.SemaphoreType.DMA((4,)),
                pltpu.SemaphoreType.DMA((epochs, 3, 3)),
                pltpu.SemaphoreType.DMA((2,)),
                pltpu.SemaphoreType.DMA((2,)),
                pltpu.SemaphoreType.DMA((2,)),
                pltpu.SemaphoreType.DMA((2,)),
                pltpu.SemaphoreType.DMA((2,)),
                pltpu.SemaphoreType.DMA((2,)),
                pltpu.SemaphoreType.DMA((2, 2)),
                pltpu.SemaphoreType.DMA((2, 2)),
                pltpu.SemaphoreType.REGULAR,
            ],
            compiler_params=pltpu.CompilerParams(
                collective_id=0, has_side_effects=True, vmem_limit_bytes=48 * 1024 * 1024
            ),
            name="coadd",
        )(*[pltpu.with_memory_space_constraint(x, pltpu.HBM) for x in (exposures, inv_variance, pixel_valid, correlation, pixel_offset, subpixel, psf_match)])
        return pl.pallas_call(
            finish,
            out_shape=(result, result),
            in_specs=[vmem, vmem],
            out_specs=(hbm, hbm),
            scratch_shapes=[pltpu.SemaphoreType.DMA((2,))],
            compiler_params=pltpu.CompilerParams(vmem_limit_bytes=1024 * 1024),
            name="finish",
        )(*sums)

    return jax.shard_map(
        shards,
        mesh=mesh,
        in_specs=(
            P(None, "dec", "ra"),
            P(None, "dec", "ra"),
            P(None, "dec", "ra"),
            P("dec", "ra", None),
            P("dec", "ra", None, None),
            P("dec", "ra", None, None),
            P(),
        ),
        out_specs=(P("dec", "ra"), P("dec", "ra")),
        check_vma=False,
    )
```

```python
import functools
import math

import jax
import jax.numpy as jnp
from jax import lax
from jax.experimental import pallas as pl
from jax.experimental.pallas import tpu as pltpu
from jax.sharding import PartitionSpec as P

MARGIN = 64
HALF = 31
LANES = 128
BAND = 96
GROUP = 16
RIM = 112
OWN = 160
F32 = jnp.float32
BF16 = jnp.bfloat16
MESH = pl.DeviceIdType.MESH
SERIES = tuple((-1.0) ** k / math.factorial(2 * k + 1) for k in range(12))


def dot(a, b):
    return jnp.dot(a, b, preferred_element_type=F32)


def lanczos(x):
    angle = (jnp.pi / 3.0) * x
    square = angle * angle
    ratio = jnp.full_like(x, SERIES[-1])
    for term in SERIES[-2::-1]:
        ratio = ratio * square + term
    both = ratio * ratio
    return jnp.where(jnp.abs(x) < 3.0, both * (1.0 - (4.0 / 3.0) * square * both), 0.0)


def toeplitz(row, count, width, shift, first, last):
    spread = jnp.broadcast_to(row, (count, LANES))
    turned = pltpu.roll(spread, (LANES // 2 - shift) % LANES, 1, stride=1, stride_axis=0)
    lanes = lax.broadcasted_iota(jnp.int32, (count, LANES), 1)
    down = lax.broadcasted_iota(jnp.int32, (count, LANES), 0)
    blocks = []
    for block in range(width // LANES):
        lane = lanes + block * LANES
        inside = jnp.abs(lane - down + shift) < LANES // 2
        inside = inside & (lane >= first) & (lane < last)
        blocks.append(jnp.where(inside, turned, 0.0))
    return blocks[0] if len(blocks) == 1 else jnp.concatenate(blocks, axis=1)


def lane_ids(value):
    return lax.broadcasted_iota(jnp.int32, value.shape, 1)


def packed(planes, way):
    first, second = planes[0], planes[1]
    if way:
        first, second = pltpu.roll(first, BAND, 1), pltpu.roll(second, BAND, 1)
    half = first.shape[0] // 2
    upper = jnp.where(lane_ids(first) < BAND, first, pltpu.roll(second, LANES - BAND, 1))
    low, high = second[:half], second[half:]
    lower = jnp.where(lane_ids(low) < LANES // 2, low, pltpu.roll(high, LANES // 2, 1))
    return jnp.concatenate([upper, lower], axis=0).astype(BF16)


def unpacked(value, way):
    value = value.astype(F32)
    half = value.shape[0] // 3
    upper, lower = value[: 2 * half], value[2 * half :]
    lanes = lane_ids(upper)
    first = jnp.where(lanes < BAND, upper, 0.0)
    low = jnp.concatenate([lower, pltpu.roll(lower, LANES // 2, 1)], axis=0)
    high = jnp.where(lanes < BAND, pltpu.roll(upper, BAND, 1), 0.0)
    second = jnp.where(lanes < LANES // 2, low, high)
    if way:
        first, second = pltpu.roll(first, LANES - BAND, 1), pltpu.roll(second, LANES - BAND, 1)
    return first, second


def kernel(
    dims,
    exp_hbm,
    inv_hbm,
    val_hbm,
    cor_hbm,
    off_hbm,
    sub_hbm,
    psf_hbm,
    matched_ref,
    weight_ref,
    exp_ref,
    inv_ref,
    val_ref,
    cor_ref,
    off_ref,
    sub_ref,
    psf_ref,
    tile,
    dec_out,
    dec_in,
    dec_core_out,
    dec_core_in,
    own_out,
    own_in,
    near_out,
    near_in,
    corner_out,
    corner_in,
    taps,
    bands,
    coadd,
    shifts,
    inner_sum,
    small_sem,
    load_sem,
    dec_send,
    dec_recv,
    dec_core_send,
    dec_core_recv,
    own_send,
    own_recv,
    near_send,
    near_recv,
    corner_send,
    corner_recv,
    ready_wrap,
    ready_corner,
):
    epochs, prows, pcols, n_ra, n_dec = dims
    rows, cols = prows - 2 * MARGIN, pcols - 2 * MARGIN
    me_ra, me_dec = lax.axis_index("ra"), lax.axis_index("dec")
    prev_ra, next_ra = lax.rem(me_ra + n_ra - 1, n_ra), lax.rem(me_ra + 1, n_ra)
    has_prev, has_next = me_dec > 0, me_dec < n_dec - 1
    is_first, not_first = me_ra == 0, me_ra > 0
    is_last, not_last = me_ra == n_ra - 1, me_ra < n_ra - 1
    odd = lax.rem(me_dec, 2)
    is_odd, is_even = odd == 1, odd == 0
    far = me_dec - 1 + 2 * odd
    has_far = (far >= 0) & (far < n_dec)
    has_near = jnp.where(is_odd, has_prev, has_next)

    small = [
        pltpu.make_async_copy(src, dst, small_sem.at[i])
        for i, (src, dst) in enumerate(
            ((off_hbm, off_ref), (sub_hbm, sub_ref), (cor_hbm, cor_ref), (psf_hbm, psf_ref))
        )
    ]
    segments = (
        slice(0, RIM),
        slice(prows - RIM, prows),
        slice(RIM, prows - RIM),
    )

    def load(e, segment, which):
        src, dst = ((inv_hbm, inv_ref), (val_hbm, val_ref), (exp_hbm, exp_ref))[which]
        return pltpu.make_async_copy(
            src.at[e, segments[segment]], dst.at[e, segments[segment]], load_sem.at[e, segment, which]
        )

    order = [(e, segment) for segment in range(3) for e in range(epochs)]
    loads = [load(e, segment, which) for e, segment in order for which in range(3)]
    for copy in small[:3] + loads + small[3:]:
        copy.start()

    barrier = pltpu.get_barrier_semaphore()
    pl.semaphore_signal(barrier, inc=1, device_id=(prev_ra, me_dec), device_id_type=MESH)

    @pl.when(not_last)
    def _():
        pl.semaphore_signal(barrier, inc=1, device_id=(next_ra, me_dec), device_id_type=MESH)

    @pl.when(has_far & (is_odd | is_first))
    def _():
        pl.semaphore_signal(barrier, inc=1, device_id=(prev_ra, far), device_id_type=MESH)

    @pl.when(has_far & is_odd & not_last)
    def _():
        pl.semaphore_signal(barrier, inc=1, device_id=(next_ra, far), device_id_type=MESH)

    @pl.when(has_prev)
    def _():
        pl.semaphore_signal(barrier, inc=1, device_id=(me_ra, me_dec - 1), device_id_type=MESH)

    @pl.when(has_next)
    def _():
        pl.semaphore_signal(barrier, inc=1, device_id=(me_ra, me_dec + 1), device_id_type=MESH)

    for copy in small[:3]:
        copy.wait()
    inner = prows - 2 * BAND
    groups = taps.shape[0] // GROUP
    side = 2 * LANES
    reach = RIM - (OWN - (prows - 2 * RIM)) // 2
    with jax.named_scope("maps"):
        lane = lax.broadcasted_iota(jnp.int32, (8, LANES), 1).astype(F32) - LANES // 2
        which_map = lax.broadcasted_iota(jnp.int32, (8, LANES), 0)
        place = lane
        for e in range(epochs):
            shift_r = off_ref[0, 0, e, 0].astype(F32) + sub_ref[0, 0, e, 0]
            shift_c = off_ref[0, 0, e, 1].astype(F32) + sub_ref[0, 0, e, 1]
            place = jnp.where(which_map == 2 * e, shift_r - lane, place)
            place = jnp.where(which_map == 2 * e + 1, shift_c + lane, place)
        wave = lanczos(place)
        kept = wave.astype(BF16).astype(F32)
        scale = jnp.sum(wave, axis=1, keepdims=True) / jnp.sum(kept, axis=1, keepdims=True)
        def scaled_map(line, count, width, spans):
            parts = [toeplitz(kept[line(e)], count, width, *span) for e, span in spans]
            return functools.reduce(jnp.add, parts).astype(BF16)

        def row_line(e):
            return slice(2 * e, 2 * e + 1)

        def col_line(e):
            return slice(2 * e + 1, 2 * e + 2)

        width = -(-epochs * RIM // LANES) * LANES
        rim_maps = [
            scaled_map(
                row_line,
                BAND,
                width,
                [(e, (shift - e * RIM, e * RIM, (e + 1) * RIM)) for e in range(epochs)],
            )[:, : epochs * RIM]
            for shift in (0, BAND - RIM)
        ]
        inner_maps, lefts, rights, gains = [], [], [], []
        for e in range(epochs):
            gains.append(scale[row_line(e)] * scale[col_line(e)] * cor_ref[0, 0, e].astype(F32))
            inner_maps.append(
                scaled_map(row_line, inner, side, [(e, (reach - BAND, 0, OWN))])[:, :OWN]
            )
            turned = kept[col_line(e)]
            same, behind, ahead = (
                toeplitz(turned, LANES, LANES, shift, 0, LANES).astype(BF16)
                for shift in (0, -LANES, LANES)
            )
            zero = jnp.zeros_like(same)
            lower = jnp.concatenate([behind, same], axis=1)
            lefts.append(jnp.concatenate([jnp.concatenate([same, ahead], axis=1), lower], axis=0))
            rights.append(jnp.concatenate([jnp.concatenate([zero, ahead], axis=1), lower], axis=0))

    def pixels(e, segment):
        for which in range(3):
            load(e, segment, which).wait()
        at = segments[segment]
        masked = inv_ref[e, at] * val_ref[e, at].astype(F32) * gains[e]
        return jnp.concatenate([(masked * exp_ref[e, at]).astype(BF16), masked.astype(BF16)], axis=0)

    def columns(e, segment):
        part = pixels(e, segment)
        left = dot(part[:, :side], lefts[e])
        right = dot(part[:, pcols - side :], rights[e])
        wide = jnp.concatenate(
            [left[:, :LANES], left[:, LANES:] + right[:, :LANES], right[:, LANES:]], axis=1
        ).astype(BF16)
        half = wide.shape[0] // 2
        return jnp.concatenate([wide[:half], wide[half:]], axis=1)

    warped = []
    ends = (slice(0, LANES), slice(pcols - LANES, pcols))
    for way in range(2):
        with jax.named_scope("rim_columns"):
            warped.append([columns(e, way) for e in range(epochs)])
        with jax.named_scope("rim_rows"):
            value = dot(rim_maps[way], jnp.concatenate(warped[way], axis=0))
            for plane in range(2):
                part = value[:, plane * pcols : (plane + 1) * pcols]
                tile[plane, way * (prows - BAND) : way * (prows - BAND) + BAND, :] = part
                dec_core_out[way, plane] = part[:, LANES : 2 * LANES].astype(BF16)
                for end in range(2):
                    dec_out[way, plane, :, end * LANES : (end + 1) * LANES] = part[
                        :, ends[end]
                    ].astype(BF16)
    with jax.named_scope("barrier"):
        pl.semaphore_wait(
            barrier,
            1
            + not_first.astype(jnp.int32)
            + has_prev.astype(jnp.int32)
            + has_next.astype(jnp.int32)
            + (has_far & (is_even | is_last)).astype(jnp.int32)
            + (has_far & is_even & not_first).astype(jnp.int32),
        )

    def dec_copy(way):
        return pltpu.make_async_remote_copy(
            src_ref=dec_out.at[way],
            dst_ref=dec_in.at[way],
            send_sem=dec_send.at[way],
            recv_sem=dec_recv.at[way],
            device_id=(me_ra, me_dec + (1 if way else -1)),
            device_id_type=MESH,
        )

    def dec_core_copy(way):
        return pltpu.make_async_remote_copy(
            src_ref=dec_core_out.at[way],
            dst_ref=dec_core_in.at[way],
            send_sem=dec_core_send.at[way],
            recv_sem=dec_core_recv.at[way],
            device_id=(me_ra, me_dec + (1 if way else -1)),
            device_id_type=MESH,
        )

    def ra_copy(out, into, send, recv, way, to_dec):
        return pltpu.make_async_remote_copy(
            src_ref=out.at[way],
            dst_ref=into.at[way],
            send_sem=send.at[way],
            recv_sem=recv.at[way],
            device_id=(next_ra if way else prev_ra, to_dec),
            device_id_type=MESH,
        )

    def own_copy(way):
        return ra_copy(own_out, own_in, own_send, own_recv, way, me_dec)

    def near_copy(way):
        return ra_copy(near_out, near_in, near_send, near_recv, way, me_dec)

    def corner_copy(way):
        return ra_copy(corner_out, corner_in, corner_send, corner_recv, way, far)

    for way, present in ((0, has_prev), (1, has_next)):

        @pl.when(present)
        def _():
            dec_copy(way).start()
            dec_core_copy(way).start()

    def edge_at(part):
        first = 2 * MARGIN - BAND + part * (prows - 4 * MARGIN + BAND)
        return pl.ds(pl.multiple_of(first, 8), BAND)

    far_rim = pl.ds(pl.multiple_of(odd * (prows - BAND), 8), BAND)
    own_at = pl.ds(pl.multiple_of(2 * MARGIN - BAND + odd * BAND, 8), OWN)
    far_at, near_at = edge_at(odd), edge_at(1 - odd)

    @pl.when(has_far)
    def _():
        with jax.named_scope("corner_send"):
            for way in range(2):
                corner_out[way] = packed(tile[:, far_rim, ends[way]], way)

            @pl.when(is_even | is_last)
            def _():
                corner_copy(1).start()

            @pl.when(is_even & not_first)
            def _():
                corner_copy(0).start()

            @pl.when(is_even & not_first)
            def _():
                pl.semaphore_signal(
                    ready_corner, inc=1, device_id=(prev_ra, far), device_id_type=MESH
                )

            @pl.when(is_even & not_last)
            def _():
                pl.semaphore_signal(
                    ready_corner, inc=1, device_id=(next_ra, far), device_id_type=MESH
                )

    @pl.when(is_last)
    def _():
        pl.semaphore_signal(ready_wrap, inc=1, device_id=(next_ra, me_dec), device_id_type=MESH)

    @pl.when(is_last & has_far)
    def _():
        pl.semaphore_signal(ready_wrap, inc=1, device_id=(next_ra, far), device_id_type=MESH)

    with jax.named_scope("inner"):
        value = None
        for e in range(epochs):
            rows_in = jnp.concatenate(
                [warped[0][e][reach:], columns(e, 2), warped[1][e][: RIM - reach]], axis=0
            )
            part = dot(inner_maps[e], rows_in)
            value = part if value is None else value + part
        for plane in range(2):
            tile[plane, BAND : BAND + inner, :] = value[:, plane * pcols : (plane + 1) * pcols]

    with jax.named_scope("own_send"):
        for way in (1, 0):
            own_out[way] = packed(tile[:, own_at, ends[way]], way)
        own_copy(1).start()

        @pl.when(not_first)
        def _():
            own_copy(0).start()

    def add_band(way, at):
        for end in range(2):
            tile[:, at, ends[end]] += dec_in[way, :, :, end * LANES : (end + 1) * LANES].astype(F32)

    with jax.named_scope("near_send"):
        for part, present in ((0, has_prev & is_odd), (1, has_next & is_even)):

            @pl.when(present)
            def _():
                dec_copy(1 - part).wait_recv()
                add_band(1 - part, edge_at(part))

        for way in (1, 0):
            near_out[way] = packed(tile[:, near_at, ends[way]], way)
        near_copy(1).start()

        @pl.when(not_first)
        def _():
            near_copy(0).start()

    small[3].wait()
    side_k = psf_ref.shape[0]
    taps[...] = jnp.zeros_like(taps)
    taps[0:side_k, 0:side_k] = psf_ref[...].astype(F32)
    offset = MARGIN - HALF
    across = lax.broadcasted_iota(jnp.int32, (LANES, LANES), 1)
    down = lax.broadcasted_iota(jnp.int32, (LANES, LANES), 0)
    last_tap = taps.shape[0] - 1
    mirror = jnp.where(across + down == last_tap, 1.0, 0.0).astype(BF16)
    taps[...] = dot(taps[...].astype(BF16), mirror)
    turn = LANES - last_tap - offset
    level = across - down >= turn

    def build(k, carry):
        for s in range(GROUP // 2):
            at = pl.ds(pl.multiple_of((k * (GROUP // 2) + s) * LANES, LANES), LANES)
            for parity in range(2):
                row = taps[pl.ds(k * GROUP + 2 * s + parity, 1), :]
                spread_row = jnp.broadcast_to(row, (LANES, LANES))
                turned = pltpu.roll(spread_row, turn, 1, stride=1, stride_axis=0)
                for block in range(2):
                    first = (2 * block + parity) * LANES
                    keep = jnp.logical_not(level) if block else level
                    bands[at, first : first + LANES] = jnp.where(keep, turned, 0.0).astype(BF16)
        return carry

    with jax.named_scope("bands"):
        lax.fori_loop(0, groups, build, 0)

    @pl.when(has_far & is_odd & not_last)
    def _():
        pl.semaphore_wait(ready_corner, 1 + not_first.astype(jnp.int32))
        corner_copy(1).start()

    @pl.when(has_far & is_odd & is_last)
    def _():
        pl.semaphore_wait(ready_corner, 1)

    @pl.when(has_far & is_odd & not_first)
    def _():
        corner_copy(0).start()

    span = coadd.shape[0]
    row_id = lax.broadcasted_iota(jnp.int32, (span, 1), 0) - HALF + me_dec * rows
    inside = (row_id >= 0) & (row_id < n_dec * rows)
    deep, tall = shifts.shape[1], rows + GROUP

    def spread(slot, where):
        numer = tile[0, offset : offset + span, where]
        denom = tile[1, offset : offset + span, where]
        coadd[:, where] = jnp.where(inside, numer / jnp.maximum(denom, 1.0), 0.0).astype(BF16)
        for s in range(GROUP // 2):
            shifts[slot, :, s * LANES : (s + 1) * LANES] = coadd[2 * s : 2 * s + deep, where]

    def product(slot, chosen):
        stacked = jnp.concatenate(
            [shifts[slot, k * GROUP : k * GROUP + tall, :] for k in range(groups)], axis=1
        )
        return dot(stacked, bands[:, chosen])

    with jax.named_scope("far_receive"):
        for part, present in ((0, has_prev), (1, has_next)):

            @pl.when(present)
            def _():
                dec_core_copy(1 - part).wait_recv()
                tile[:, edge_at(part), LANES : 2 * LANES] += dec_core_in[1 - part].astype(F32)

    with jax.named_scope("middle"):
        spread(2, slice(LANES, 2 * LANES))
        inner_sum[...] = product(2, slice(None))

    @pl.when(is_first)
    def _():
        pl.semaphore_wait(ready_wrap, 1 + has_far.astype(jnp.int32))
        own_copy(0).start()
        near_copy(0).start()

    @pl.when(is_first & has_far)
    def _():
        corner_copy(0).start()

    for part, present in ((0, has_prev & is_even), (1, has_next & is_odd)):

        @pl.when(present)
        def _():
            dec_copy(1 - part).wait_recv()
            add_band(1 - part, edge_at(part))

    for end in (1, 0):
        way = 1 - end
        with jax.named_scope("receive%d" % end):

            @pl.when(has_far)
            def _():
                corner_copy(way).wait_recv()
                for plane, value in enumerate(unpacked(corner_in[way], way)):
                    tile[plane, far_at, ends[end]] += value

            own_copy(way).wait_recv()
            for plane, value in enumerate(unpacked(own_in[way], way)):
                tile[plane, own_at, ends[end]] += value
            near_copy(way).wait_recv()
            for plane, value in enumerate(unpacked(near_in[way], way)):
                tile[plane, near_at, ends[end]] += value
    with jax.named_scope("ends_spread"):
        for end in range(2):
            spread(end, ends[end])
    with jax.named_scope("ends_product"):
        for end in range(2):
            total = inner_sum[:, end * 2 * LANES : (end + 1) * 2 * LANES] + product(
                end, slice((1 - end) * 2 * LANES, (2 - end) * 2 * LANES)
            )
            matched_ref[:, end * LANES : (end + 1) * LANES] = (
                total[:rows, :LANES] + total[1 : rows + 1, LANES:]
            )
    weight_ref[...] = tile[1, MARGIN : MARGIN + rows, MARGIN : MARGIN + cols]

    @pl.when(has_prev)
    def _():
        dec_copy(0).wait_send()
        dec_core_copy(0).wait_send()

    @pl.when(has_next)
    def _():
        dec_copy(1).wait_send()
        dec_core_copy(1).wait_send()

    for way in range(2):
        own_copy(way).wait_send()
        near_copy(way).wait_send()

    @pl.when(has_far)
    def _():
        for way in range(2):
            corner_copy(way).wait_send()


def finish(matched_in, weight_in, matched_out, weight_out, sems):
    copies = [
        pltpu.make_async_copy(matched_in, matched_out, sems.at[0]),
        pltpu.make_async_copy(weight_in, weight_out, sems.at[1]),
    ]
    for copy in copies:
        copy.start()
    for copy in copies:
        copy.wait()


def solution(mesh):
    n_ra, n_dec = mesh.shape["ra"], mesh.shape["dec"]

    def shards(exposures, inv_variance, pixel_valid, correlation, pixel_offset, subpixel, psf_match):
        epochs, prows, pcols = exposures.shape
        rows, cols = prows - 2 * MARGIN, pcols - 2 * MARGIN
        groups = -(-psf_match.shape[0] // GROUP)
        deep = rows + GROUP * groups
        result = jax.ShapeDtypeStruct((rows, cols), F32)
        hbm = pl.BlockSpec(memory_space=pltpu.HBM)
        vmem = pl.BlockSpec(memory_space=pltpu.VMEM)
        sums = pl.pallas_call(
            functools.partial(kernel, (epochs, prows, pcols, n_ra, n_dec)),
            out_shape=(result, result),
            in_specs=[hbm] * 7,
            out_specs=(vmem, vmem),
            scratch_shapes=[
                pltpu.VMEM((epochs, prows, pcols), F32),
                pltpu.VMEM((epochs, prows, pcols), F32),
                pltpu.VMEM((epochs, prows, pcols), jnp.int32),
                pltpu.SMEM(correlation.shape, jnp.int32),
                pltpu.SMEM(pixel_offset.shape, jnp.int32),
                pltpu.SMEM(subpixel.shape, F32),
                pltpu.VMEM(psf_match.shape, BF16),
                pltpu.VMEM((2, prows, pcols), F32),
                pltpu.VMEM((2, 2, BAND, 2 * LANES), BF16),
                pltpu.VMEM((2, 2, BAND, 2 * LANES), BF16),
                pltpu.VMEM((2, 2, BAND, LANES), BF16),
                pltpu.VMEM((2, 2, BAND, LANES), BF16),
                pltpu.VMEM((2, OWN * 3 // 2, LANES), BF16),
                pltpu.VMEM((2, OWN * 3 // 2, LANES), BF16),
                pltpu.VMEM((2, BAND * 3 // 2, LANES), BF16),
                pltpu.VMEM((2, BAND * 3 // 2, LANES), BF16),
                pltpu.VMEM((2, BAND * 3 // 2, LANES), BF16),
                pltpu.VMEM((2, BAND * 3 // 2, LANES), BF16),
                pltpu.VMEM((groups * GROUP, LANES), F32),
                pltpu.VMEM((groups * GROUP // 2 * LANES, 4 * LANES), BF16),
                pltpu.VMEM((deep + GROUP, pcols), BF16),
                pltpu.VMEM((3, deep, GROUP // 2 * LANES), BF16),
                pltpu.VMEM((rows + GROUP, 4 * LANES), F32),
                pltpu.SemaphoreType.DMA((4,)),
                pltpu.SemaphoreType.DMA((epochs, 3, 3)),
                pltpu.SemaphoreType.DMA((2,)),
                pltpu.SemaphoreType.DMA((2,)),
                pltpu.SemaphoreType.DMA((2,)),
                pltpu.SemaphoreType.DMA((2,)),
                pltpu.SemaphoreType.DMA((2,)),
                pltpu.SemaphoreType.DMA((2,)),
                pltpu.SemaphoreType.DMA((2,)),
                pltpu.SemaphoreType.DMA((2,)),
                pltpu.SemaphoreType.DMA((2,)),
                pltpu.SemaphoreType.DMA((2,)),
                pltpu.SemaphoreType.REGULAR,
                pltpu.SemaphoreType.REGULAR,
            ],
            compiler_params=pltpu.CompilerParams(
                collective_id=0, has_side_effects=True, vmem_limit_bytes=48 * 1024 * 1024
            ),
            name="coadd",
        )(*[pltpu.with_memory_space_constraint(x, pltpu.HBM) for x in (exposures, inv_variance, pixel_valid, correlation, pixel_offset, subpixel, psf_match)])
        return pl.pallas_call(
            finish,
            out_shape=(result, result),
            in_specs=[vmem, vmem],
            out_specs=(hbm, hbm),
            scratch_shapes=[pltpu.SemaphoreType.DMA((2,))],
            compiler_params=pltpu.CompilerParams(vmem_limit_bytes=1024 * 1024),
            name="finish",
        )(*sums)

    return jax.shard_map(
        shards,
        mesh=mesh,
        in_specs=(
            P(None, "dec", "ra"),
            P(None, "dec", "ra"),
            P(None, "dec", "ra"),
            P("dec", "ra", None),
            P("dec", "ra", None, None),
            P("dec", "ra", None, None),
            P(),
        ),
        out_specs=(P("dec", "ra"), P("dec", "ra")),
        check_vma=False,
    )
```

```python
import functools
import math

import jax
import jax.numpy as jnp
from jax import lax
from jax.experimental import pallas as pl
from jax.experimental.pallas import tpu as pltpu
from jax.sharding import PartitionSpec as P

MARGIN = 64
HALF = 31
LANES = 128
BAND = 96
GROUP = 16
RIM = 112
OWN = 128
HALO = 32
WINDOW = 160
ROW_PAD = 1
F32 = jnp.float32
BF16 = jnp.bfloat16
MESH = pl.DeviceIdType.MESH
SERIES = tuple((-1.0) ** k / math.factorial(2 * k + 1) for k in range(12))


def dot(a, b):
    return jnp.dot(a, b, preferred_element_type=F32)


def lanczos(x):
    angle = (jnp.pi / 3.0) * x
    square = angle * angle
    ratio = jnp.full_like(x, SERIES[-1])
    for term in SERIES[-2::-1]:
        ratio = ratio * square + term
    both = ratio * ratio
    return jnp.where(jnp.abs(x) < 3.0, both * (1.0 - (4.0 / 3.0) * square * both), 0.0)


def toeplitz(row, count, width, shift, first, last):
    spread = jnp.broadcast_to(row, (count, LANES))
    turned = pltpu.roll(spread, (LANES // 2 - shift) % LANES, 1, stride=1, stride_axis=0)
    lanes = lax.broadcasted_iota(jnp.int32, (count, LANES), 1)
    down = lax.broadcasted_iota(jnp.int32, (count, LANES), 0)
    blocks = []
    for block in range(width // LANES):
        lane = lanes + block * LANES
        inside = jnp.abs(lane - down + shift) < LANES // 2
        inside = inside & (lane >= first) & (lane < last)
        blocks.append(jnp.where(inside, turned, 0.0))
    return blocks[0] if len(blocks) == 1 else jnp.concatenate(blocks, axis=1)


def lane_ids(value):
    return lax.broadcasted_iota(jnp.int32, value.shape, 1)


def packed(planes, way):
    first, second = planes[0], planes[1]
    if way:
        first, second = pltpu.roll(first, BAND, 1), pltpu.roll(second, BAND, 1)
    half = first.shape[0] // 2
    upper = jnp.where(lane_ids(first) < BAND, first, pltpu.roll(second, LANES - BAND, 1))
    low, high = second[:half], second[half:]
    lower = jnp.where(lane_ids(low) < LANES // 2, low, pltpu.roll(high, LANES // 2, 1))
    return jnp.concatenate([upper, lower], axis=0).astype(BF16)


def unpacked(value, way):
    value = value.astype(F32)
    half = value.shape[0] // 3
    upper, lower = value[: 2 * half], value[2 * half :]
    lanes = lane_ids(upper)
    first = jnp.where(lanes < BAND, upper, 0.0)
    low = jnp.concatenate([lower, pltpu.roll(lower, LANES // 2, 1)], axis=0)
    high = jnp.where(lanes < BAND, pltpu.roll(upper, BAND, 1), 0.0)
    second = jnp.where(lanes < LANES // 2, low, high)
    if way:
        first, second = pltpu.roll(first, LANES - BAND, 1), pltpu.roll(second, LANES - BAND, 1)
    return first, second


def product(shifts, bands, tall, chosen):
    groups = bands.shape[0] // shifts.shape[1]
    stacked = jnp.concatenate(
        [shifts[k * GROUP : k * GROUP + tall, :] for k in range(groups)], axis=1
    )
    return dot(stacked, bands[:, chosen])


def end_sums(end, inner_sum, end_shifts, bands, rows):
    picked = slice((1 - end) * 2 * LANES, (2 - end) * 2 * LANES)
    total = inner_sum[:, end * 2 * LANES : (end + 1) * 2 * LANES] + product(
        end_shifts.at[end], bands, inner_sum.shape[0], picked
    )
    return total[:rows, :LANES] + total[1 : rows + 1, LANES:]


def late_end(n_ra):
    me = lax.axis_index("ra")
    left_last = (me == 0) | ((lax.rem(me, 2) == 1) & (me < n_ra - 1))
    return jnp.where(left_last, 0, 1)


def kernel(
    dims,
    exp_hbm,
    inv_hbm,
    val_hbm,
    cor_hbm,
    off_hbm,
    sub_hbm,
    psf_hbm,
    matched_ref,
    weight_ref,
    bands,
    inner_sum,
    end_shifts,
    exp_ref,
    inv_ref,
    val_ref,
    cor_ref,
    off_ref,
    sub_ref,
    psf_ref,
    tile,
    slab,
    dec_out,
    dec_in,
    dec_core_out,
    dec_core_in,
    own_out,
    own_in,
    near_out,
    near_in,
    corner_out,
    corner_in,
    taps,
    coadd,
    shifts,
    local_sem,
    dec_recv,
    dec_core_recv,
    own_recv,
    near_recv,
    corner_recv,
    ready_wrap,
    ready_corner,
):
    epochs, prows, pcols, n_ra, n_dec = dims
    rows, cols = prows - 2 * MARGIN, pcols - 2 * MARGIN
    me_ra, me_dec = lax.axis_index("ra"), lax.axis_index("dec")
    prev_ra, next_ra = lax.rem(me_ra + n_ra - 1, n_ra), lax.rem(me_ra + 1, n_ra)
    has_prev, has_next = me_dec > 0, me_dec < n_dec - 1
    is_first, not_first = me_ra == 0, me_ra > 0
    is_last, not_last = me_ra == n_ra - 1, me_ra < n_ra - 1
    odd = lax.rem(me_dec, 2)
    is_odd, is_even = odd == 1, odd == 0
    far = me_dec - 1 + 2 * odd
    has_far = (far >= 0) & (far < n_dec)
    has_near = jnp.where(is_odd, has_prev, has_next)

    small = [
        pltpu.make_async_copy(src, dst, local_sem.at[i % 3])
        for i, (src, dst) in enumerate(
            ((off_hbm, off_ref), (sub_hbm, sub_ref), (cor_hbm, cor_ref), (psf_hbm, psf_ref))
        )
    ]
    top_first = prows - RIM
    segments = (
        pl.ds(pl.multiple_of((1 - odd) * top_first, GROUP), RIM),
        pl.ds(pl.multiple_of(odd * RIM, GROUP), top_first),
    )

    def load(segment, which):
        src, dst = ((inv_hbm, inv_ref), (val_hbm, val_ref), (exp_hbm, exp_ref))[which]
        return pltpu.make_async_copy(
            src.at[:, segments[segment]], dst.at[:, segments[segment]], local_sem.at[3 + 3 * segment + which]
        )

    loads = [load(segment, which) for segment in range(2) for which in range(3)]
    for copy in small[:3] + loads:
        copy.start()

    barrier = pltpu.get_barrier_semaphore()
    pl.semaphore_signal(barrier, inc=1, device_id=(prev_ra, me_dec), device_id_type=MESH)

    @pl.when(not_last)
    def _():
        pl.semaphore_signal(barrier, inc=1, device_id=(next_ra, me_dec), device_id_type=MESH)

    @pl.when(has_far & (is_odd | is_first))
    def _():
        pl.semaphore_signal(barrier, inc=1, device_id=(prev_ra, far), device_id_type=MESH)

    @pl.when(has_far & is_odd & not_last)
    def _():
        pl.semaphore_signal(barrier, inc=1, device_id=(next_ra, far), device_id_type=MESH)

    @pl.when(has_prev)
    def _():
        pl.semaphore_signal(barrier, inc=1, device_id=(me_ra, me_dec - 1), device_id_type=MESH)

    @pl.when(has_next)
    def _():
        pl.semaphore_signal(barrier, inc=1, device_id=(me_ra, me_dec + 1), device_id_type=MESH)

    for copy in small[:3]:
        copy.wait()
    small[3].start()
    inner = prows - 2 * BAND
    groups = taps.shape[0] // GROUP
    side = 2 * LANES
    reach = RIM - (WINDOW - (prows - 2 * RIM)) // 2
    with jax.named_scope("maps"):
        lane = lax.broadcasted_iota(jnp.int32, (8, LANES), 1).astype(F32) - LANES // 2
        which_map = lax.broadcasted_iota(jnp.int32, (8, LANES), 0)
        place = lane
        for e in range(epochs):
            shift_r = off_ref[0, 0, e, 0].astype(F32) + sub_ref[0, 0, e, 0]
            shift_c = off_ref[0, 0, e, 1].astype(F32) + sub_ref[0, 0, e, 1]
            place = jnp.where(which_map == 2 * e, shift_r - lane, place)
            place = jnp.where(which_map == 2 * e + 1, shift_c + lane, place)
        wave = lanczos(place)
        kept = wave.astype(BF16).astype(F32)
        scale = jnp.sum(wave, axis=1, keepdims=True) / jnp.sum(kept, axis=1, keepdims=True)
        def scaled_map(line, count, width, spans):
            parts = [toeplitz(kept[line(e)], count, width, *span) for e, span in spans]
            return functools.reduce(jnp.add, parts)

        def row_line(e):
            return slice(2 * e, 2 * e + 1)

        def col_line(e):
            return slice(2 * e + 1, 2 * e + 2)

        width = -(-epochs * RIM // LANES) * LANES
        upper, lower = [
            scaled_map(
                row_line,
                BAND,
                width,
                [(e, (shift - e * RIM, e * RIM, (e + 1) * RIM)) for e in range(epochs)],
            )
            for shift in (0, BAND - RIM)
        ]
        rim_maps = [
            jnp.where(is_odd, *pair).astype(BF16)[:, : epochs * RIM]
            for pair in ((upper, lower), (lower, upper))
        ]
        inner_maps, lefts, rights, gains = [], [], [], []
        for e in range(epochs):
            gains.append(scale[row_line(e)] * scale[col_line(e)] * cor_ref[0, 0, e].astype(F32))
            inner_maps.append(
                scaled_map(row_line, inner, side, [(e, (reach - BAND, 0, WINDOW))])
                .astype(BF16)[:, :WINDOW]
            )
            turned = kept[col_line(e)]
            same, behind, ahead = (
                toeplitz(turned, LANES, LANES, shift, 0, LANES).astype(BF16)
                for shift in (0, -LANES, LANES)
            )
            zero = jnp.zeros_like(same)
            lower = jnp.concatenate([behind, same], axis=1)
            lefts.append(jnp.concatenate([jnp.concatenate([same, ahead], axis=1), lower], axis=0))
            rights.append(jnp.concatenate([jnp.concatenate([zero, ahead], axis=1), lower], axis=0))

    def pixels(e, segment):
        at = segments[segment]
        masked = inv_ref[e, at] * val_ref[e, at].astype(F32) * gains[e]
        return jnp.concatenate([(masked * exp_ref[e, at]).astype(BF16), masked.astype(BF16)], axis=0)

    def columns(part, e):
        left = dot(part[:, :side], lefts[e])
        right = dot(part[:, pcols - side :], rights[e])
        wide = jnp.concatenate(
            [left[:, :LANES], left[:, LANES:] + right[:, :LANES], right[:, LANES:]], axis=1
        ).astype(BF16)
        half = wide.shape[0] // 2
        return jnp.concatenate([wide[:half], wide[half:]], axis=1)

    ends = (slice(0, LANES), slice(pcols - LANES, pcols))

    def arrive(segment):
        for which in range(3):
            load(segment, which).wait()

    ways = (1 - odd, odd)

    def warp_columns(segment):
        warped = [columns(pixels(e, segment), e) for e in range(epochs)]
        for e in range(epochs):
            slab[e, segments[segment]] = warped[e]
        return warped

    def warp_rim(slot, warped):
        value = dot(rim_maps[slot], jnp.concatenate(warped, axis=0))
        into = pl.ds(pl.multiple_of(ways[slot] * (prows - BAND), 8), BAND)
        for plane in range(2):
            tile[plane, into, :] = value[:, plane * pcols : (plane + 1) * pcols]

    def dec_give(slot):
        way = ways[slot]
        rim_at = pl.ds(pl.multiple_of(way * (prows - BAND), 8), BAND)
        for plane in range(2):
            for end in range(2):
                dec_out[way, plane, :, end * LANES : (end + 1) * LANES] = tile[
                    plane, rim_at, ends[end]
                ].astype(BF16)
            dec_core_out[way, plane] = tile[plane, rim_at, LANES : 2 * LANES].astype(BF16)

    with jax.named_scope("near_rim"):
        arrive(0)
        warp_rim(0, warp_columns(0))
        dec_give(0)
    with jax.named_scope("barrier"):
        pl.semaphore_wait(
            barrier,
            1
            + not_first.astype(jnp.int32)
            + has_prev.astype(jnp.int32)
            + has_next.astype(jnp.int32)
            + (has_far & (is_even | is_last)).astype(jnp.int32)
            + (has_far & is_even & not_first).astype(jnp.int32),
        )

    def dec_copy(way):
        return pltpu.make_async_remote_copy(
            src_ref=dec_out.at[way],
            dst_ref=dec_in.at[way],
            send_sem=local_sem.at[3 + way],
            recv_sem=dec_recv.at[way],
            device_id=(me_ra, me_dec + (1 if way else -1)),
            device_id_type=MESH,
        )

    def dec_core_copy(way):
        return pltpu.make_async_remote_copy(
            src_ref=dec_core_out.at[way],
            dst_ref=dec_core_in.at[way],
            send_sem=local_sem.at[(5, 1)[way]],
            recv_sem=dec_core_recv.at[way],
            device_id=(me_ra, me_dec + (1 if way else -1)),
            device_id_type=MESH,
        )

    def ra_copy(out, into, send, recv, way, to_dec):
        return pltpu.make_async_remote_copy(
            src_ref=out.at[way],
            dst_ref=into.at[way],
            send_sem=local_sem.at[send[way]],
            recv_sem=recv.at[way],
            device_id=(next_ra if way else prev_ra, to_dec),
            device_id_type=MESH,
        )

    def own_copy(way, size):
        return pltpu.make_async_remote_copy(
            src_ref=own_out.at[way, 0:size],
            dst_ref=own_in.at[way, 0:size],
            send_sem=local_sem.at[7 + way],
            recv_sem=own_recv.at[way],
            device_id=(next_ra if way else prev_ra, me_dec),
            device_id_type=MESH,
        )

    def own_each(action):
        @pl.when(has_far)
        def _():
            action(wide_at, (OWN + HALO) * 3 // 2)

        @pl.when(jnp.logical_not(has_far))
        def _():
            action(own_at, OWN * 3 // 2)

    def own_start(way):
        own_each(lambda at, size: own_copy(way, size).start())

    def own_take(way, end):
        def take(at, size):
            own_copy(way, size).wait_recv()
            for plane, value in enumerate(unpacked(own_in[way, :size], way)):
                tile[plane, at, ends[end]] += value

        own_each(take)

    def near_copy(way):
        return ra_copy(near_out, near_in, (2, 6), near_recv, way, me_dec)

    def corner_copy(way):
        return ra_copy(corner_out, corner_in, (9, 10), corner_recv, way, far)

    def dec_send(way):
        dec_copy(way).start()
        dec_core_copy(way).start()

    pl.when(is_odd)(functools.partial(dec_send, 0))
    pl.when(is_even & has_next)(functools.partial(dec_send, 1))

    def edge_at(part):
        first = 2 * MARGIN - BAND + part * (prows - 4 * MARGIN + BAND)
        return pl.ds(pl.multiple_of(first, 8), BAND)

    far_rim = pl.ds(pl.multiple_of(odd * (prows - BAND), 8), BAND)
    own_at = pl.ds(pl.multiple_of(MARGIN + odd * MARGIN, 8), OWN)
    wide_at = pl.ds(pl.multiple_of(MARGIN - HALO + odd * BAND, 8), OWN + HALO)
    far_at, near_at = edge_at(odd), edge_at(1 - odd)

    @pl.when(has_far & is_even & not_first)
    def _():
        pl.semaphore_signal(ready_corner, inc=1, device_id=(prev_ra, far), device_id_type=MESH)

    @pl.when(has_far & is_even & not_last)
    def _():
        pl.semaphore_signal(ready_corner, inc=1, device_id=(next_ra, far), device_id_type=MESH)

    @pl.when(is_last)
    def _():
        pl.semaphore_signal(ready_wrap, inc=1, device_id=(next_ra, me_dec), device_id_type=MESH)

    @pl.when(is_last & has_far)
    def _():
        pl.semaphore_signal(ready_wrap, inc=1, device_id=(next_ra, far), device_id_type=MESH)

    with jax.named_scope("inner"):
        arrive(1)
        warp_columns(1)
        far_in = pl.ds(pl.multiple_of(odd * top_first, GROUP), RIM)
        warp_rim(1, [slab[e, far_in] for e in range(epochs)])
        value = functools.reduce(
            jnp.add,
            [dot(inner_maps[e], slab[e, reach : reach + WINDOW]) for e in range(epochs)],
        )
        for plane in range(2):
            tile[plane, BAND : BAND + inner, :] = value[:, plane * pcols : (plane + 1) * pcols]

    def corner_give(way):
        corner_out[way] = packed(tile[:, far_rim, ends[way]], way)

    def own_give(way):
        def give(at, size):
            own_out[way, :size] = packed(tile[:, at, ends[way]], way)
            if way:
                own_copy(1, size).start()
            else:

                @pl.when(not_first)
                def _():
                    own_copy(0, size).start()

        own_each(give)

    def add_band(way, at):
        for end in range(2):
            tile[:, at, ends[end]] += dec_in[way, :, :, end * LANES : (end + 1) * LANES].astype(F32)

    with jax.named_scope("corner_send"):

        @pl.when(has_far & is_even)
        def _():
            corner_give(1)
            corner_copy(1).start()
            corner_give(0)

            @pl.when(not_first)
            def _():
                corner_copy(0).start()

    with jax.named_scope("own_send"):
        own_give(1)

    with jax.named_scope("near_send"):
        for part, present in ((0, is_odd), (1, has_next & is_even)):

            @pl.when(present)
            def _():
                dec_copy(1 - part).wait_recv()
                add_band(1 - part, edge_at(part))

        near_out[1] = packed(tile[:, near_at, ends[1]], 1)
        near_copy(1).start()

    with jax.named_scope("far_send"):
        own_give(0)
        near_out[0] = packed(tile[:, near_at, ends[0]], 0)

        @pl.when(not_first)
        def _():
            near_copy(0).start()

        @pl.when(has_far)
        def _():
            dec_give(1)
            pl.when(is_even)(functools.partial(dec_send, 0))
            pl.when(is_odd)(functools.partial(dec_send, 1))

        @pl.when(has_far & is_odd)
        def _():
            for way in (1, 0):
                corner_give(way)

            @pl.when(is_last)
            def _():
                corner_copy(1).start()

    small[3].wait()
    side_k = psf_ref.shape[0]
    taps[...] = jnp.zeros_like(taps)
    taps[ROW_PAD : ROW_PAD + side_k, 0:side_k] = psf_ref[...].astype(F32)
    offset = MARGIN - HALF
    across = lax.broadcasted_iota(jnp.int32, (LANES, LANES), 1)
    down = lax.broadcasted_iota(jnp.int32, (LANES, LANES), 0)
    last_tap = taps.shape[0] - 1
    mirror = jnp.where(across + down == last_tap, 1.0, 0.0).astype(BF16)
    taps[...] = dot(taps[...].astype(BF16), mirror)
    turn = LANES - last_tap - offset
    level = across - down >= turn

    def build(k, carry):
        for s in range(GROUP // 2):
            at = pl.ds(pl.multiple_of((k * (GROUP // 2) + s) * LANES, LANES), LANES)
            for parity in range(2):
                row = taps[pl.ds(k * GROUP + 2 * s + parity, 1), :]
                spread_row = jnp.broadcast_to(row, (LANES, LANES))
                turned = pltpu.roll(spread_row, turn, 1, stride=1, stride_axis=0)
                for block in range(2):
                    first = (2 * block + parity) * LANES
                    keep = jnp.logical_not(level) if block else level
                    bands[at, first : first + LANES] = jnp.where(keep, turned, 0.0).astype(BF16)
        return carry

    with jax.named_scope("bands"):
        lax.fori_loop(0, groups, build, 0)

    @pl.when(has_far & is_odd & not_last)
    def _():
        pl.semaphore_wait(ready_corner, 1 + not_first.astype(jnp.int32))
        corner_copy(1).start()

    @pl.when(has_far & is_odd & is_last)
    def _():
        pl.semaphore_wait(ready_corner, 1)

    @pl.when(has_far & is_odd & not_first)
    def _():
        corner_copy(0).start()

    span = coadd.shape[0]
    above = HALF + ROW_PAD
    row_id = lax.broadcasted_iota(jnp.int32, (span, 1), 0) - above + me_dec * rows
    inside = (row_id >= 0) & (row_id < n_dec * rows)
    deep, tall = shifts.shape[0], rows + GROUP
    top = MARGIN - above

    def spread(into, where):
        numer = tile[0, top : top + span, where]
        denom = tile[1, top : top + span, where]
        coadd[:, where] = jnp.where(inside, numer / jnp.maximum(denom, 1.0), 0.0).astype(BF16)
        for s in range(GROUP // 2):
            into[:, s * LANES : (s + 1) * LANES] = coadd[2 * s : 2 * s + deep, where]

    @pl.when(is_first)
    def _():
        pl.semaphore_wait(ready_wrap, 1 + has_far.astype(jnp.int32))
        own_start(0)
        near_copy(0).start()

    @pl.when(is_first & has_far)
    def _():
        corner_copy(0).start()

    with jax.named_scope("far_receive"):
        for part, present in ((0, has_prev), (1, has_next)):

            @pl.when(present)
            def _():
                dec_core_copy(1 - part).wait_recv()
                tile[:, edge_at(part), LANES : 2 * LANES] += dec_core_in[1 - part].astype(F32)

    with jax.named_scope("middle"):
        spread(shifts, slice(LANES, 2 * LANES))
        inner_sum[...] = product(shifts, bands, tall, slice(None))

    for part, present in ((0, has_prev & is_even), (1, has_next & is_odd)):

        @pl.when(present)
        def _():
            dec_copy(1 - part).wait_recv()
            add_band(1 - part, edge_at(part))

    weight_ref[:, MARGIN : MARGIN + LANES] = tile[1, MARGIN : MARGIN + rows, LANES : 2 * LANES]

    def finish_end(end):
        way = 1 - end

        @pl.when(has_far)
        def _():
            corner_copy(way).wait_recv()
            for plane, value in enumerate(unpacked(corner_in[way], way)):
                tile[plane, far_at, ends[end]] += value

        own_take(way, end)
        near_copy(way).wait_recv()
        for plane, value in enumerate(unpacked(near_in[way], way)):
            tile[plane, near_at, ends[end]] += value
        into = slice(end * (cols - MARGIN), end * (cols - MARGIN) + MARGIN)
        first = pcols - LANES if end else MARGIN
        weight_ref[:, into] = tile[1, MARGIN : MARGIN + rows, first : first + MARGIN]
        spread(end_shifts.at[end], ends[end])

    late = late_end(n_ra)
    with jax.named_scope("early_end"):
        for end in range(2):

            @pl.when(late == 1 - end)
            def _():
                finish_end(end)
                matched_ref[:, end * LANES : (end + 1) * LANES] = end_sums(
                    end, inner_sum, end_shifts, bands, rows
                )

    def way_sent(way):
        own_each(lambda at, size: own_copy(way, size).wait_send())
        near_copy(way).wait_send()

        @pl.when(has_far)
        def _():
            corner_copy(way).wait_send()

    with jax.named_scope("sent"):
        for way, present in ((0, has_prev), (1, has_next)):

            @pl.when(present)
            def _():
                dec_copy(way).wait_send()
                dec_core_copy(way).wait_send()

        way_sent(1)

        @pl.when(not_first)
        def _():
            way_sent(0)

    with jax.named_scope("late_end"):
        for end in range(2):

            @pl.when(late == end)
            def _():
                finish_end(end)

    @pl.when(is_first)
    def _():
        way_sent(0)


def finish(
    n_ra, matched_in, weight_in, bands, inner_sum, end_shifts, matched_out, weight_out, held, sems
):
    weight = pltpu.make_async_copy(weight_in, weight_out, sems.at[0])
    weight.start()
    late = late_end(n_ra)
    for end in range(2):

        @pl.when(late == end)
        def _():
            early_at = slice((1 - end) * LANES, (2 - end) * LANES)
            early = pltpu.make_async_copy(
                matched_in.at[:, early_at], matched_out.at[:, early_at], sems.at[1]
            )
            early.start()
            held[...] = end_sums(end, inner_sum, end_shifts, bands, held.shape[0])
            last = pltpu.make_async_copy(
                held, matched_out.at[:, end * LANES : (end + 1) * LANES], sems.at[2]
            )
            last.start()
            early.wait()
            last.wait()

    weight.wait()


def solution(mesh):
    n_ra, n_dec = mesh.shape["ra"], mesh.shape["dec"]

    def shards(exposures, inv_variance, pixel_valid, correlation, pixel_offset, subpixel, psf_match):
        epochs, prows, pcols = exposures.shape
        rows, cols = prows - 2 * MARGIN, pcols - 2 * MARGIN
        groups = -(-psf_match.shape[0] // GROUP)
        deep = rows + GROUP * groups
        result = jax.ShapeDtypeStruct((rows, cols), F32)
        hbm = pl.BlockSpec(memory_space=pltpu.HBM)
        vmem = pl.BlockSpec(memory_space=pltpu.VMEM)
        sums = pl.pallas_call(
            functools.partial(kernel, (epochs, prows, pcols, n_ra, n_dec)),
            out_shape=(
                result,
                result,
                jax.ShapeDtypeStruct((groups * GROUP // 2 * LANES, 4 * LANES), BF16),
                jax.ShapeDtypeStruct((rows + GROUP, 4 * LANES), F32),
                jax.ShapeDtypeStruct((2, deep, GROUP // 2 * LANES), BF16),
            ),
            in_specs=[hbm] * 7,
            out_specs=(vmem,) * 5,
            scratch_shapes=[
                pltpu.VMEM((epochs, prows, pcols), F32),
                pltpu.VMEM((epochs, prows, pcols), F32),
                pltpu.VMEM((epochs, prows, pcols), jnp.int32),
                pltpu.SMEM(correlation.shape, jnp.int32),
                pltpu.SMEM(pixel_offset.shape, jnp.int32),
                pltpu.SMEM(subpixel.shape, F32),
                pltpu.VMEM(psf_match.shape, BF16),
                pltpu.VMEM((2, prows, pcols), F32),
                pltpu.VMEM((epochs, prows, 2 * pcols), BF16),
                pltpu.VMEM((2, 2, BAND, 2 * LANES), BF16),
                pltpu.VMEM((2, 2, BAND, 2 * LANES), BF16),
                pltpu.VMEM((2, 2, BAND, LANES), BF16),
                pltpu.VMEM((2, 2, BAND, LANES), BF16),
                pltpu.VMEM((2, (OWN + HALO) * 3 // 2, LANES), BF16),
                pltpu.VMEM((2, (OWN + HALO) * 3 // 2, LANES), BF16),
                pltpu.VMEM((2, BAND * 3 // 2, LANES), BF16),
                pltpu.VMEM((2, BAND * 3 // 2, LANES), BF16),
                pltpu.VMEM((2, BAND * 3 // 2, LANES), BF16),
                pltpu.VMEM((2, BAND * 3 // 2, LANES), BF16),
                pltpu.VMEM((groups * GROUP, LANES), F32),
                pltpu.VMEM((deep + GROUP, pcols), BF16),
                pltpu.VMEM((deep, GROUP // 2 * LANES), BF16),
                pltpu.SemaphoreType.DMA((11,)),
                pltpu.SemaphoreType.DMA((2,)),
                pltpu.SemaphoreType.DMA((2,)),
                pltpu.SemaphoreType.DMA((2,)),
                pltpu.SemaphoreType.DMA((2,)),
                pltpu.SemaphoreType.DMA((2,)),
                pltpu.SemaphoreType.REGULAR,
                pltpu.SemaphoreType.REGULAR,
            ],
            compiler_params=pltpu.CompilerParams(
                collective_id=0, has_side_effects=True, vmem_limit_bytes=24 * 1024 * 1024
            ),
            name="coadd",
        )(*[pltpu.with_memory_space_constraint(x, pltpu.HBM) for x in (exposures, inv_variance, pixel_valid, correlation, pixel_offset, subpixel, psf_match)])
        return pl.pallas_call(
            functools.partial(finish, n_ra),
            out_shape=(result, result),
            in_specs=[vmem] * 5,
            out_specs=(hbm, hbm),
            scratch_shapes=[pltpu.VMEM((rows, LANES), F32), pltpu.SemaphoreType.DMA((3,))],
            compiler_params=pltpu.CompilerParams(vmem_limit_bytes=8 * 1024 * 1024),
            name="finish",
        )(*sums)

    return jax.shard_map(
        shards,
        mesh=mesh,
        in_specs=(
            P(None, "dec", "ra"),
            P(None, "dec", "ra"),
            P(None, "dec", "ra"),
            P("dec", "ra", None),
            P("dec", "ra", None, None),
            P("dec", "ra", None, None),
            P(),
        ),
        out_specs=(P("dec", "ra"), P("dec", "ra")),
        check_vma=False,
    )
```

```python
import functools
import math

import jax
import jax.numpy as jnp
from jax import lax
from jax.experimental import pallas as pl
from jax.experimental.pallas import tpu as pltpu
from jax.sharding import PartitionSpec as P

MARGIN = 64
HALF = 31
LANES = 128
BAND = 96
GROUP = 16
RIM = 112
OWN = 128
HALO = 32
WINDOW = 160
ROW_PAD = 1
F32 = jnp.float32
BF16 = jnp.bfloat16
MESH = pl.DeviceIdType.MESH
SERIES = tuple((-1.0) ** k / math.factorial(2 * k + 1) for k in range(12))


def dot(a, b):
    return jnp.dot(a, b, preferred_element_type=F32)


def lanczos(x):
    angle = (jnp.pi / 3.0) * x
    square = angle * angle
    ratio = jnp.full_like(x, SERIES[-1])
    for term in SERIES[-2::-1]:
        ratio = ratio * square + term
    both = ratio * ratio
    return jnp.where(jnp.abs(x) < 3.0, both * (1.0 - (4.0 / 3.0) * square * both), 0.0)


def toeplitz(row, count, width, shift, first, last):
    spread = jnp.broadcast_to(row, (count, LANES))
    turned = pltpu.roll(spread, (LANES // 2 - shift) % LANES, 1, stride=1, stride_axis=0)
    lanes = lax.broadcasted_iota(jnp.int32, (count, LANES), 1)
    down = lax.broadcasted_iota(jnp.int32, (count, LANES), 0)
    blocks = []
    for block in range(width // LANES):
        lane = lanes + block * LANES
        inside = jnp.abs(lane - down + shift) < LANES // 2
        inside = inside & (lane >= first) & (lane < last)
        blocks.append(jnp.where(inside, turned, 0.0))
    return blocks[0] if len(blocks) == 1 else jnp.concatenate(blocks, axis=1)


def lane_ids(value):
    return lax.broadcasted_iota(jnp.int32, value.shape, 1)


def packed(planes, way):
    first, second = planes[0], planes[1]
    if way:
        first, second = pltpu.roll(first, BAND, 1), pltpu.roll(second, BAND, 1)
    half = first.shape[0] // 2
    upper = jnp.where(lane_ids(first) < BAND, first, pltpu.roll(second, LANES - BAND, 1))
    low, high = second[:half], second[half:]
    lower = jnp.where(lane_ids(low) < LANES // 2, low, pltpu.roll(high, LANES // 2, 1))
    return jnp.concatenate([upper, lower], axis=0).astype(BF16)


def unpacked(value, way):
    value = value.astype(F32)
    half = value.shape[0] // 3
    upper, lower = value[: 2 * half], value[2 * half :]
    lanes = lane_ids(upper)
    first = jnp.where(lanes < BAND, upper, 0.0)
    low = jnp.concatenate([lower, pltpu.roll(lower, LANES // 2, 1)], axis=0)
    high = jnp.where(lanes < BAND, pltpu.roll(upper, BAND, 1), 0.0)
    second = jnp.where(lanes < LANES // 2, low, high)
    if way:
        first, second = pltpu.roll(first, LANES - BAND, 1), pltpu.roll(second, LANES - BAND, 1)
    return first, second


def product(shifts, bands, tall, chosen):
    groups = bands.shape[0] // shifts.shape[1]
    stacked = jnp.concatenate(
        [shifts[k * GROUP : k * GROUP + tall, :] for k in range(groups)], axis=1
    )
    return dot(stacked, bands[:, chosen])


def end_sums(end, inner_sum, end_shifts, bands, rows):
    picked = slice((1 - end) * 2 * LANES, (2 - end) * 2 * LANES)
    total = inner_sum[:, end * 2 * LANES : (end + 1) * 2 * LANES] + product(
        end_shifts.at[end], bands, inner_sum.shape[0], picked
    )
    return total[:rows, :LANES] + total[1 : rows + 1, LANES:]


def late_end(n_ra):
    me = lax.axis_index("ra")
    left_last = (me == 0) | ((lax.rem(me, 2) == 1) & (me < n_ra - 1))
    return jnp.where(left_last, 0, 1)


def kernel(
    dims,
    exp_hbm,
    inv_hbm,
    val_hbm,
    cor_hbm,
    off_hbm,
    sub_hbm,
    psf_hbm,
    matched_ref,
    weight_ref,
    bands,
    inner_sum,
    end_shifts,
    exp_ref,
    inv_ref,
    val_ref,
    cor_ref,
    off_ref,
    sub_ref,
    psf_ref,
    tile,
    slab,
    dec_out,
    dec_in,
    dec_core_out,
    dec_core_in,
    own_out,
    own_in,
    near_out,
    near_in,
    corner_out,
    corner_in,
    taps,
    coadd,
    shifts,
    local_sem,
    dec_recv,
    dec_core_recv,
    own_recv,
    near_recv,
    corner_recv,
    ready_wrap,
    ready_corner,
):
    epochs, prows, pcols, n_ra, n_dec = dims
    rows, cols = prows - 2 * MARGIN, pcols - 2 * MARGIN
    me_ra, me_dec = lax.axis_index("ra"), lax.axis_index("dec")
    prev_ra, next_ra = lax.rem(me_ra + n_ra - 1, n_ra), lax.rem(me_ra + 1, n_ra)
    has_prev, has_next = me_dec > 0, me_dec < n_dec - 1
    is_first, not_first = me_ra == 0, me_ra > 0
    is_last, not_last = me_ra == n_ra - 1, me_ra < n_ra - 1
    odd = lax.rem(me_dec, 2)
    is_odd, is_even = odd == 1, odd == 0
    far = me_dec - 1 + 2 * odd
    has_far = (far >= 0) & (far < n_dec)
    has_near = jnp.where(is_odd, has_prev, has_next)

    small = [
        pltpu.make_async_copy(src, dst, local_sem.at[i % 3])
        for i, (src, dst) in enumerate(
            ((off_hbm, off_ref), (sub_hbm, sub_ref), (cor_hbm, cor_ref), (psf_hbm, psf_ref))
        )
    ]
    top_first = prows - RIM
    segments = (
        pl.ds(pl.multiple_of((1 - odd) * top_first, GROUP), RIM),
        pl.ds(pl.multiple_of(odd * RIM, GROUP), top_first),
    )

    def load(segment, which):
        src, dst = ((inv_hbm, inv_ref), (val_hbm, val_ref), (exp_hbm, exp_ref))[which]
        return pltpu.make_async_copy(
            src.at[:, segments[segment]], dst.at[:, segments[segment]], local_sem.at[3 + 3 * segment + which]
        )

    loads = [load(segment, which) for segment in range(2) for which in range(3)]
    for copy in small[:3] + loads:
        copy.start()

    barrier = pltpu.get_barrier_semaphore()
    pl.semaphore_signal(barrier, inc=1, device_id=(prev_ra, me_dec), device_id_type=MESH)

    @pl.when(not_last)
    def _():
        pl.semaphore_signal(barrier, inc=1, device_id=(next_ra, me_dec), device_id_type=MESH)

    @pl.when(has_far & (is_odd | is_first))
    def _():
        pl.semaphore_signal(barrier, inc=1, device_id=(prev_ra, far), device_id_type=MESH)

    @pl.when(has_far & is_odd & not_last)
    def _():
        pl.semaphore_signal(barrier, inc=1, device_id=(next_ra, far), device_id_type=MESH)

    @pl.when(has_prev)
    def _():
        pl.semaphore_signal(barrier, inc=1, device_id=(me_ra, me_dec - 1), device_id_type=MESH)

    @pl.when(has_next)
    def _():
        pl.semaphore_signal(barrier, inc=1, device_id=(me_ra, me_dec + 1), device_id_type=MESH)

    for copy in small[:3]:
        copy.wait()
    small[3].start()
    inner = prows - 2 * BAND
    groups = taps.shape[0] // GROUP
    side = 2 * LANES
    reach = RIM - (WINDOW - (prows - 2 * RIM)) // 2
    with jax.named_scope("maps"):
        lane = lax.broadcasted_iota(jnp.int32, (8, LANES), 1).astype(F32) - LANES // 2
        which_map = lax.broadcasted_iota(jnp.int32, (8, LANES), 0)
        place = lane
        for e in range(epochs):
            shift_r = off_ref[0, 0, e, 0].astype(F32) + sub_ref[0, 0, e, 0]
            shift_c = off_ref[0, 0, e, 1].astype(F32) + sub_ref[0, 0, e, 1]
            place = jnp.where(which_map == 2 * e, shift_r - lane, place)
            place = jnp.where(which_map == 2 * e + 1, shift_c + lane, place)
        wave = lanczos(place)
        kept = wave.astype(BF16).astype(F32)
        scale = jnp.sum(wave, axis=1, keepdims=True) / jnp.sum(kept, axis=1, keepdims=True)
        def scaled_map(line, count, width, spans):
            parts = [toeplitz(kept[line(e)], count, width, *span) for e, span in spans]
            return functools.reduce(jnp.add, parts)

        def row_line(e):
            return slice(2 * e, 2 * e + 1)

        def col_line(e):
            return slice(2 * e + 1, 2 * e + 2)

        width = -(-epochs * RIM // LANES) * LANES
        upper, lower = [
            scaled_map(
                row_line,
                BAND,
                width,
                [(e, (shift - e * RIM, e * RIM, (e + 1) * RIM)) for e in range(epochs)],
            )
            for shift in (0, BAND - RIM)
        ]
        rim_maps = [
            jnp.where(is_odd, *pair).astype(BF16)[:, : epochs * RIM]
            for pair in ((upper, lower), (lower, upper))
        ]
        inner_maps, lefts, rights, gains = [], [], [], []
        for e in range(epochs):
            gains.append(scale[row_line(e)] * scale[col_line(e)] * cor_ref[0, 0, e].astype(F32))
            inner_maps.append(
                scaled_map(row_line, inner, side, [(e, (reach - BAND, 0, WINDOW))])
                .astype(BF16)[:, :WINDOW]
            )
            turned = kept[col_line(e)]
            same, behind, ahead = (
                toeplitz(turned, LANES, LANES, shift, 0, LANES).astype(BF16)
                for shift in (0, -LANES, LANES)
            )
            zero = jnp.zeros_like(same)
            lower = jnp.concatenate([behind, same], axis=1)
            lefts.append(jnp.concatenate([jnp.concatenate([same, ahead], axis=1), lower], axis=0))
            rights.append(jnp.concatenate([jnp.concatenate([zero, ahead], axis=1), lower], axis=0))

    def pixels(e, segment):
        at = segments[segment]
        masked = inv_ref[e, at] * val_ref[e, at].astype(F32) * gains[e]
        return jnp.concatenate([(masked * exp_ref[e, at]).astype(BF16), masked.astype(BF16)], axis=0)

    def columns(part, e):
        left = dot(part[:, :side], lefts[e])
        right = dot(part[:, pcols - side :], rights[e])
        wide = jnp.concatenate(
            [left[:, :LANES], left[:, LANES:] + right[:, :LANES], right[:, LANES:]], axis=1
        ).astype(BF16)
        half = wide.shape[0] // 2
        return jnp.concatenate([wide[:half], wide[half:]], axis=1)

    ends = (slice(0, LANES), slice(pcols - LANES, pcols))

    def arrive(segment):
        for which in range(3):
            load(segment, which).wait()

    ways = (1 - odd, odd)

    def warp_columns(segment):
        warped = [columns(pixels(e, segment), e) for e in range(epochs)]
        for e in range(epochs):
            slab[e, segments[segment]] = warped[e]
        return warped

    def warp_rim(slot, warped):
        value = dot(rim_maps[slot], jnp.concatenate(warped, axis=0))
        into = pl.ds(pl.multiple_of(ways[slot] * (prows - BAND), 8), BAND)
        for plane in range(2):
            tile[plane, into, :] = value[:, plane * pcols : (plane + 1) * pcols]

    def dec_give(slot):
        way = ways[slot]
        rim_at = pl.ds(pl.multiple_of(way * (prows - BAND), 8), BAND)
        for plane in range(2):
            for end in range(2):
                dec_out[way, plane, :, end * LANES : (end + 1) * LANES] = tile[
                    plane, rim_at, ends[end]
                ].astype(BF16)
            dec_core_out[way, plane] = tile[plane, rim_at, LANES : 2 * LANES].astype(BF16)

    with jax.named_scope("near_rim"):
        arrive(0)
        warp_rim(0, warp_columns(0))
        dec_give(0)
    with jax.named_scope("barrier"):
        pl.semaphore_wait(
            barrier,
            1
            + not_first.astype(jnp.int32)
            + has_prev.astype(jnp.int32)
            + has_next.astype(jnp.int32)
            + (has_far & (is_even | is_last)).astype(jnp.int32)
            + (has_far & is_even & not_first).astype(jnp.int32),
        )

    def dec_copy(way):
        return pltpu.make_async_remote_copy(
            src_ref=dec_out.at[way],
            dst_ref=dec_in.at[way],
            send_sem=local_sem.at[3 + way],
            recv_sem=dec_recv.at[way],
            device_id=(me_ra, me_dec + (1 if way else -1)),
            device_id_type=MESH,
        )

    def dec_core_copy(way):
        return pltpu.make_async_remote_copy(
            src_ref=dec_core_out.at[way],
            dst_ref=dec_core_in.at[way],
            send_sem=local_sem.at[(5, 1)[way]],
            recv_sem=dec_core_recv.at[way],
            device_id=(me_ra, me_dec + (1 if way else -1)),
            device_id_type=MESH,
        )

    def ra_copy(out, into, send, recv, way, to_dec):
        return pltpu.make_async_remote_copy(
            src_ref=out.at[way],
            dst_ref=into.at[way],
            send_sem=local_sem.at[send[way]],
            recv_sem=recv.at[way],
            device_id=(next_ra if way else prev_ra, to_dec),
            device_id_type=MESH,
        )

    def own_copy(way, size):
        return pltpu.make_async_remote_copy(
            src_ref=own_out.at[way, 0:size],
            dst_ref=own_in.at[way, 0:size],
            send_sem=local_sem.at[7 + way],
            recv_sem=own_recv.at[way],
            device_id=(next_ra if way else prev_ra, me_dec),
            device_id_type=MESH,
        )

    def own_each(action):
        @pl.when(has_far)
        def _():
            action(wide_at, (OWN + HALO) * 3 // 2)

        @pl.when(jnp.logical_not(has_far))
        def _():
            action(own_at, OWN * 3 // 2)

    def own_start(way):
        own_each(lambda at, size: own_copy(way, size).start())

    def own_take(way, end):
        def take(at, size):
            own_copy(way, size).wait_recv()
            for plane, value in enumerate(unpacked(own_in[way, :size], way)):
                tile[plane, at, ends[end]] += value

        own_each(take)

    def near_copy(way):
        return ra_copy(near_out, near_in, (2, 6), near_recv, way, me_dec)

    def corner_copy(way):
        return ra_copy(corner_out, corner_in, (9, 10), corner_recv, way, far)

    def dec_send(way):
        dec_copy(way).start()
        dec_core_copy(way).start()

    def far_dec_send(way):
        dec_core_copy(way).start()
        dec_copy(way).start()

    pl.when(is_odd)(functools.partial(dec_send, 0))
    pl.when(is_even & has_next)(functools.partial(dec_send, 1))

    def edge_at(part):
        first = 2 * MARGIN - BAND + part * (prows - 4 * MARGIN + BAND)
        return pl.ds(pl.multiple_of(first, 8), BAND)

    far_rim = pl.ds(pl.multiple_of(odd * (prows - BAND), 8), BAND)
    own_at = pl.ds(pl.multiple_of(MARGIN + odd * MARGIN, 8), OWN)
    wide_at = pl.ds(pl.multiple_of(MARGIN - HALO + odd * BAND, 8), OWN + HALO)
    far_at, near_at = edge_at(odd), edge_at(1 - odd)

    @pl.when(has_far & is_even & not_first)
    def _():
        pl.semaphore_signal(ready_corner, inc=1, device_id=(prev_ra, far), device_id_type=MESH)

    @pl.when(has_far & is_even & not_last)
    def _():
        pl.semaphore_signal(ready_corner, inc=1, device_id=(next_ra, far), device_id_type=MESH)

    @pl.when(is_last)
    def _():
        pl.semaphore_signal(ready_wrap, inc=1, device_id=(next_ra, me_dec), device_id_type=MESH)

    @pl.when(is_last & has_far)
    def _():
        pl.semaphore_signal(ready_wrap, inc=1, device_id=(next_ra, far), device_id_type=MESH)

    with jax.named_scope("inner"):
        arrive(1)
        warp_columns(1)
        far_in = pl.ds(pl.multiple_of(odd * top_first, GROUP), RIM)
        warp_rim(1, [slab[e, far_in] for e in range(epochs)])
        value = functools.reduce(
            jnp.add,
            [dot(inner_maps[e], slab[e, reach : reach + WINDOW]) for e in range(epochs)],
        )
        for plane in range(2):
            tile[plane, BAND : BAND + inner, :] = value[:, plane * pcols : (plane + 1) * pcols]

    def corner_give(way):
        corner_out[way] = packed(tile[:, far_rim, ends[way]], way)

    def own_give(way):
        def give(at, size):
            own_out[way, :size] = packed(tile[:, at, ends[way]], way)
            if way:
                own_copy(1, size).start()
            else:

                @pl.when(not_first)
                def _():
                    own_copy(0, size).start()

        own_each(give)

    def add_band(way, at):
        for end in range(2):
            tile[:, at, ends[end]] += dec_in[way, :, :, end * LANES : (end + 1) * LANES].astype(F32)

    with jax.named_scope("corner_send"):

        @pl.when(has_far & is_even)
        def _():
            corner_give(1)
            corner_copy(1).start()
            corner_give(0)

            @pl.when(not_first)
            def _():
                corner_copy(0).start()

    with jax.named_scope("own_send"):
        own_give(1)

    with jax.named_scope("near_send"):
        for part, present in ((0, is_odd), (1, has_next & is_even)):

            @pl.when(present)
            def _():
                dec_copy(1 - part).wait_recv()
                add_band(1 - part, edge_at(part))

        near_out[1] = packed(tile[:, near_at, ends[1]], 1)

        @pl.when(not_last | is_even)
        def _():
            near_copy(1).start()

    with jax.named_scope("far_send"):
        own_give(0)
        near_out[0] = packed(tile[:, near_at, ends[0]], 0)

        @pl.when(not_first)
        def _():
            near_copy(0).start()

        @pl.when(has_far)
        def _():
            dec_give(1)
            pl.when(is_even)(functools.partial(far_dec_send, 0))
            pl.when(is_odd)(functools.partial(far_dec_send, 1))

        @pl.when(has_far & is_odd)
        def _():
            for way in (1, 0):
                corner_give(way)

        @pl.when(is_last & is_odd)
        def _():
            near_copy(1).start()

    small[3].wait()
    side_k = psf_ref.shape[0]
    taps[...] = jnp.zeros_like(taps)
    taps[ROW_PAD : ROW_PAD + side_k, 0:side_k] = psf_ref[...].astype(F32)
    offset = MARGIN - HALF
    across = lax.broadcasted_iota(jnp.int32, (LANES, LANES), 1)
    down = lax.broadcasted_iota(jnp.int32, (LANES, LANES), 0)
    last_tap = taps.shape[0] - 1
    mirror = jnp.where(across + down == last_tap, 1.0, 0.0).astype(BF16)
    taps[...] = dot(taps[...].astype(BF16), mirror)
    turn = LANES - last_tap - offset
    level = across - down >= turn

    def build(k, carry):
        for s in range(GROUP // 2):
            at = pl.ds(pl.multiple_of((k * (GROUP // 2) + s) * LANES, LANES), LANES)
            for parity in range(2):
                row = taps[pl.ds(k * GROUP + 2 * s + parity, 1), :]
                spread_row = jnp.broadcast_to(row, (LANES, LANES))
                turned = pltpu.roll(spread_row, turn, 1, stride=1, stride_axis=0)
                for block in range(2):
                    first = (2 * block + parity) * LANES
                    keep = jnp.logical_not(level) if block else level
                    bands[at, first : first + LANES] = jnp.where(keep, turned, 0.0).astype(BF16)
        return carry

    with jax.named_scope("bands"):
        lax.fori_loop(0, groups, build, 0)

    @pl.when(has_far & is_odd & not_last)
    def _():
        pl.semaphore_wait(ready_corner, 1 + not_first.astype(jnp.int32))
        corner_copy(1).start()

    @pl.when(has_far & is_odd & is_last)
    def _():
        pl.semaphore_wait(ready_corner, 1)
        corner_copy(1).start()

    @pl.when(has_far & is_odd & not_first)
    def _():
        corner_copy(0).start()

    span = coadd.shape[0]
    above = HALF + ROW_PAD
    row_id = lax.broadcasted_iota(jnp.int32, (span, 1), 0) - above + me_dec * rows
    inside = (row_id >= 0) & (row_id < n_dec * rows)
    deep, tall = shifts.shape[0], rows + GROUP
    top = MARGIN - above

    def spread(into, where):
        numer = tile[0, top : top + span, where]
        denom = tile[1, top : top + span, where]
        coadd[:, where] = jnp.where(inside, numer / jnp.maximum(denom, 1.0), 0.0).astype(BF16)
        for s in range(GROUP // 2):
            into[:, s * LANES : (s + 1) * LANES] = coadd[2 * s : 2 * s + deep, where]

    @pl.when(is_first)
    def _():
        pl.semaphore_wait(ready_wrap, 1 + has_far.astype(jnp.int32))
        own_start(0)
        near_copy(0).start()

    @pl.when(is_first & has_far)
    def _():
        corner_copy(0).start()

    with jax.named_scope("far_receive"):
        for part, present in ((0, has_prev), (1, has_next)):

            @pl.when(present)
            def _():
                dec_core_copy(1 - part).wait_recv()
                tile[:, edge_at(part), LANES : 2 * LANES] += dec_core_in[1 - part].astype(F32)

    with jax.named_scope("middle"):
        spread(shifts, slice(LANES, 2 * LANES))
        inner_sum[...] = product(shifts, bands, tall, slice(None))

    for part, present in ((0, has_prev & is_even), (1, has_next & is_odd)):

        @pl.when(present)
        def _():
            dec_copy(1 - part).wait_recv()
            add_band(1 - part, edge_at(part))

    weight_ref[:, MARGIN : MARGIN + LANES] = tile[1, MARGIN : MARGIN + rows, LANES : 2 * LANES]

    def finish_end(end):
        way = 1 - end

        @pl.when(has_far)
        def _():
            corner_copy(way).wait_recv()
            for plane, value in enumerate(unpacked(corner_in[way], way)):
                tile[plane, far_at, ends[end]] += value

        own_take(way, end)
        near_copy(way).wait_recv()
        for plane, value in enumerate(unpacked(near_in[way], way)):
            tile[plane, near_at, ends[end]] += value
        into = slice(end * (cols - MARGIN), end * (cols - MARGIN) + MARGIN)
        first = pcols - LANES if end else MARGIN
        weight_ref[:, into] = tile[1, MARGIN : MARGIN + rows, first : first + MARGIN]
        spread(end_shifts.at[end], ends[end])

    late = late_end(n_ra)
    with jax.named_scope("early_end"):
        for end in range(2):

            @pl.when(late == 1 - end)
            def _():
                finish_end(end)
                matched_ref[:, end * LANES : (end + 1) * LANES] = end_sums(
                    end, inner_sum, end_shifts, bands, rows
                )

    def way_sent(way):
        own_each(lambda at, size: own_copy(way, size).wait_send())
        near_copy(way).wait_send()

        @pl.when(has_far)
        def _():
            corner_copy(way).wait_send()

    with jax.named_scope("sent"):
        for way, present in ((0, has_prev), (1, has_next)):

            @pl.when(present)
            def _():
                dec_copy(way).wait_send()
                dec_core_copy(way).wait_send()

        way_sent(1)

        @pl.when(not_first)
        def _():
            way_sent(0)

    with jax.named_scope("late_end"):
        for end in range(2):

            @pl.when(late == end)
            def _():
                finish_end(end)

    @pl.when(is_first)
    def _():
        way_sent(0)


def finish(
    n_ra, matched_in, weight_in, bands, inner_sum, end_shifts, matched_out, weight_out, held, sems
):
    weight = pltpu.make_async_copy(weight_in, weight_out, sems.at[0])
    weight.start()
    late = late_end(n_ra)
    for end in range(2):

        @pl.when(late == end)
        def _():
            early_at = slice((1 - end) * LANES, (2 - end) * LANES)
            early = pltpu.make_async_copy(
                matched_in.at[:, early_at], matched_out.at[:, early_at], sems.at[1]
            )
            early.start()
            held[...] = end_sums(end, inner_sum, end_shifts, bands, held.shape[0])
            last = pltpu.make_async_copy(
                held, matched_out.at[:, end * LANES : (end + 1) * LANES], sems.at[2]
            )
            last.start()
            early.wait()
            last.wait()

    weight.wait()


def solution(mesh):
    n_ra, n_dec = mesh.shape["ra"], mesh.shape["dec"]

    def shards(exposures, inv_variance, pixel_valid, correlation, pixel_offset, subpixel, psf_match):
        epochs, prows, pcols = exposures.shape
        rows, cols = prows - 2 * MARGIN, pcols - 2 * MARGIN
        groups = -(-psf_match.shape[0] // GROUP)
        deep = rows + GROUP * groups
        result = jax.ShapeDtypeStruct((rows, cols), F32)
        hbm = pl.BlockSpec(memory_space=pltpu.HBM)
        vmem = pl.BlockSpec(memory_space=pltpu.VMEM)
        sums = pl.pallas_call(
            functools.partial(kernel, (epochs, prows, pcols, n_ra, n_dec)),
            out_shape=(
                result,
                result,
                jax.ShapeDtypeStruct((groups * GROUP // 2 * LANES, 4 * LANES), BF16),
                jax.ShapeDtypeStruct((rows + GROUP, 4 * LANES), F32),
                jax.ShapeDtypeStruct((2, deep, GROUP // 2 * LANES), BF16),
            ),
            in_specs=[hbm] * 7,
            out_specs=(vmem,) * 5,
            scratch_shapes=[
                pltpu.VMEM((epochs, prows, pcols), F32),
                pltpu.VMEM((epochs, prows, pcols), F32),
                pltpu.VMEM((epochs, prows, pcols), jnp.int32),
                pltpu.SMEM(correlation.shape, jnp.int32),
                pltpu.SMEM(pixel_offset.shape, jnp.int32),
                pltpu.SMEM(subpixel.shape, F32),
                pltpu.VMEM(psf_match.shape, BF16),
                pltpu.VMEM((2, prows, pcols), F32),
                pltpu.VMEM((epochs, prows, 2 * pcols), BF16),
                pltpu.VMEM((2, 2, BAND, 2 * LANES), BF16),
                pltpu.VMEM((2, 2, BAND, 2 * LANES), BF16),
                pltpu.VMEM((2, 2, BAND, LANES), BF16),
                pltpu.VMEM((2, 2, BAND, LANES), BF16),
                pltpu.VMEM((2, (OWN + HALO) * 3 // 2, LANES), BF16),
                pltpu.VMEM((2, (OWN + HALO) * 3 // 2, LANES), BF16),
                pltpu.VMEM((2, BAND * 3 // 2, LANES), BF16),
                pltpu.VMEM((2, BAND * 3 // 2, LANES), BF16),
                pltpu.VMEM((2, BAND * 3 // 2, LANES), BF16),
                pltpu.VMEM((2, BAND * 3 // 2, LANES), BF16),
                pltpu.VMEM((groups * GROUP, LANES), F32),
                pltpu.VMEM((deep + GROUP, pcols), BF16),
                pltpu.VMEM((deep, GROUP // 2 * LANES), BF16),
                pltpu.SemaphoreType.DMA((11,)),
                pltpu.SemaphoreType.DMA((2,)),
                pltpu.SemaphoreType.DMA((2,)),
                pltpu.SemaphoreType.DMA((2,)),
                pltpu.SemaphoreType.DMA((2,)),
                pltpu.SemaphoreType.DMA((2,)),
                pltpu.SemaphoreType.REGULAR,
                pltpu.SemaphoreType.REGULAR,
            ],
            compiler_params=pltpu.CompilerParams(
                collective_id=0, has_side_effects=True, vmem_limit_bytes=24 * 1024 * 1024
            ),
            name="coadd",
        )(*[pltpu.with_memory_space_constraint(x, pltpu.HBM) for x in (exposures, inv_variance, pixel_valid, correlation, pixel_offset, subpixel, psf_match)])
        return pl.pallas_call(
            functools.partial(finish, n_ra),
            out_shape=(result, result),
            in_specs=[vmem] * 5,
            out_specs=(hbm, hbm),
            scratch_shapes=[pltpu.VMEM((rows, LANES), F32), pltpu.SemaphoreType.DMA((3,))],
            compiler_params=pltpu.CompilerParams(vmem_limit_bytes=8 * 1024 * 1024),
            name="finish",
        )(*sums)

    return jax.shard_map(
        shards,
        mesh=mesh,
        in_specs=(
            P(None, "dec", "ra"),
            P(None, "dec", "ra"),
            P(None, "dec", "ra"),
            P("dec", "ra", None),
            P("dec", "ra", None, None),
            P("dec", "ra", None, None),
            P(),
        ),
        out_specs=(P("dec", "ra"), P("dec", "ra")),
        check_vma=False,
    )
```

```python
import functools
import math

import jax
import jax.numpy as jnp
from jax import lax
from jax.experimental import pallas as pl
from jax.experimental.pallas import tpu as pltpu
from jax.sharding import PartitionSpec as P

MARGIN = 64
HALF = 31
LANES = 128
BAND = 96
GROUP = 16
RIM = 112
OWN = 128
HALO = 32
WINDOW = 160
ROW_PAD = 1
F32 = jnp.float32
BF16 = jnp.bfloat16
MESH = pl.DeviceIdType.MESH
SERIES = tuple((-1.0) ** k / math.factorial(2 * k + 1) for k in range(12))


def dot(a, b):
    return jnp.dot(a, b, preferred_element_type=F32)


def lanczos(x):
    angle = (jnp.pi / 3.0) * x
    square = angle * angle
    ratio = jnp.full_like(x, SERIES[-1])
    for term in SERIES[-2::-1]:
        ratio = ratio * square + term
    both = ratio * ratio
    return jnp.where(jnp.abs(x) < 3.0, both * (1.0 - (4.0 / 3.0) * square * both), 0.0)


def toeplitz(row, count, width, shift, first, last):
    spread = jnp.broadcast_to(row, (count, LANES))
    turned = pltpu.roll(spread, (LANES // 2 - shift) % LANES, 1, stride=1, stride_axis=0)
    lanes = lax.broadcasted_iota(jnp.int32, (count, LANES), 1)
    down = lax.broadcasted_iota(jnp.int32, (count, LANES), 0)
    blocks = []
    for block in range(width // LANES):
        lane = lanes + block * LANES
        inside = jnp.abs(lane - down + shift) < LANES // 2
        inside = inside & (lane >= first) & (lane < last)
        blocks.append(jnp.where(inside, turned, 0.0))
    return blocks[0] if len(blocks) == 1 else jnp.concatenate(blocks, axis=1)


def lane_ids(value):
    return lax.broadcasted_iota(jnp.int32, value.shape, 1)


def packed(planes, way):
    first, second = planes[0], planes[1]
    if way:
        first, second = pltpu.roll(first, BAND, 1), pltpu.roll(second, BAND, 1)
    half = first.shape[0] // 2
    upper = jnp.where(lane_ids(first) < BAND, first, pltpu.roll(second, LANES - BAND, 1))
    low, high = second[:half], second[half:]
    lower = jnp.where(lane_ids(low) < LANES // 2, low, pltpu.roll(high, LANES // 2, 1))
    return jnp.concatenate([upper, lower], axis=0).astype(BF16)


def unpacked(value, way):
    value = value.astype(F32)
    half = value.shape[0] // 3
    upper, lower = value[: 2 * half], value[2 * half :]
    lanes = lane_ids(upper)
    first = jnp.where(lanes < BAND, upper, 0.0)
    low = jnp.concatenate([lower, pltpu.roll(lower, LANES // 2, 1)], axis=0)
    high = jnp.where(lanes < BAND, pltpu.roll(upper, BAND, 1), 0.0)
    second = jnp.where(lanes < LANES // 2, low, high)
    if way:
        first, second = pltpu.roll(first, LANES - BAND, 1), pltpu.roll(second, LANES - BAND, 1)
    return first, second


def product(shifts, bands, first, tall, chosen):
    groups = bands.shape[0] // shifts.shape[1]
    stacked = jnp.concatenate(
        [shifts[first + k * GROUP : first + k * GROUP + tall, :] for k in range(groups)], axis=1
    )
    return dot(stacked, bands[:, chosen])


def end_sums(end, inner_sum, end_shifts, bands, first, rows):
    picked = slice((1 - end) * 2 * LANES, (2 - end) * 2 * LANES)
    tall = rows + GROUP
    total = inner_sum[first : first + tall, end * 2 * LANES : (end + 1) * 2 * LANES] + product(
        end_shifts.at[end], bands, first, tall, picked
    )
    return total[:rows, :LANES] + total[1 : rows + 1, LANES:]


def late_end(n_ra):
    me = lax.axis_index("ra")
    left_last = (me == 0) | ((lax.rem(me, 2) == 1) & (me < n_ra - 1))
    return jnp.where(left_last, 0, 1)


def kernel(
    dims,
    exp_hbm,
    inv_hbm,
    val_hbm,
    cor_hbm,
    off_hbm,
    sub_hbm,
    psf_hbm,
    matched_ref,
    weight_ref,
    bands,
    inner_sum,
    end_shifts,
    exp_ref,
    inv_ref,
    val_ref,
    cor_ref,
    off_ref,
    sub_ref,
    psf_ref,
    tile,
    slab,
    dec_out,
    dec_in,
    dec_core_out,
    dec_core_in,
    own_out,
    own_in,
    near_out,
    near_in,
    corner_out,
    corner_in,
    taps,
    coadd,
    shifts,
    local_sem,
    dec_recv,
    dec_core_recv,
    own_recv,
    near_recv,
    corner_recv,
    ready_wrap,
    ready_corner,
):
    epochs, prows, pcols, n_ra, n_dec = dims
    rows, cols = prows - 2 * MARGIN, pcols - 2 * MARGIN
    me_ra, me_dec = lax.axis_index("ra"), lax.axis_index("dec")
    prev_ra, next_ra = lax.rem(me_ra + n_ra - 1, n_ra), lax.rem(me_ra + 1, n_ra)
    has_prev, has_next = me_dec > 0, me_dec < n_dec - 1
    is_first, not_first = me_ra == 0, me_ra > 0
    is_last, not_last = me_ra == n_ra - 1, me_ra < n_ra - 1
    odd = lax.rem(me_dec, 2)
    is_odd, is_even = odd == 1, odd == 0
    far = me_dec - 1 + 2 * odd
    has_far = (far >= 0) & (far < n_dec)
    has_near = jnp.where(is_odd, has_prev, has_next)

    small = [
        pltpu.make_async_copy(src, dst, local_sem.at[i % 3])
        for i, (src, dst) in enumerate(
            ((off_hbm, off_ref), (sub_hbm, sub_ref), (cor_hbm, cor_ref), (psf_hbm, psf_ref))
        )
    ]
    top_first = prows - RIM
    segments = (
        pl.ds(pl.multiple_of((1 - odd) * top_first, GROUP), RIM),
        pl.ds(pl.multiple_of(odd * RIM, GROUP), top_first),
    )

    def load(segment, which):
        src, dst = ((inv_hbm, inv_ref), (val_hbm, val_ref), (exp_hbm, exp_ref))[which]
        return pltpu.make_async_copy(
            src.at[:, segments[segment]], dst.at[:, segments[segment]], local_sem.at[3 + 3 * segment + which]
        )

    loads = [load(segment, which) for segment in range(2) for which in range(3)]
    for copy in small[:3] + loads:
        copy.start()

    barrier = pltpu.get_barrier_semaphore()
    pl.semaphore_signal(barrier, inc=1, device_id=(prev_ra, me_dec), device_id_type=MESH)

    @pl.when(not_last)
    def _():
        pl.semaphore_signal(barrier, inc=1, device_id=(next_ra, me_dec), device_id_type=MESH)

    @pl.when(has_far & (is_odd | is_first))
    def _():
        pl.semaphore_signal(barrier, inc=1, device_id=(prev_ra, far), device_id_type=MESH)

    @pl.when(has_far & is_odd & not_last)
    def _():
        pl.semaphore_signal(barrier, inc=1, device_id=(next_ra, far), device_id_type=MESH)

    @pl.when(has_prev)
    def _():
        pl.semaphore_signal(barrier, inc=1, device_id=(me_ra, me_dec - 1), device_id_type=MESH)

    @pl.when(has_next)
    def _():
        pl.semaphore_signal(barrier, inc=1, device_id=(me_ra, me_dec + 1), device_id_type=MESH)

    for copy in small[:3]:
        copy.wait()
    small[3].start()
    inner = prows - 2 * BAND
    groups = taps.shape[0] // GROUP
    side = 2 * LANES
    reach = RIM - (WINDOW - (prows - 2 * RIM)) // 2
    with jax.named_scope("maps"):
        lane = lax.broadcasted_iota(jnp.int32, (8, LANES), 1).astype(F32) - LANES // 2
        which_map = lax.broadcasted_iota(jnp.int32, (8, LANES), 0)
        place = lane
        for e in range(epochs):
            shift_r = off_ref[0, 0, e, 0].astype(F32) + sub_ref[0, 0, e, 0]
            shift_c = off_ref[0, 0, e, 1].astype(F32) + sub_ref[0, 0, e, 1]
            place = jnp.where(which_map == 2 * e, shift_r - lane, place)
            place = jnp.where(which_map == 2 * e + 1, shift_c + lane, place)
        wave = lanczos(place)
        kept = wave.astype(BF16).astype(F32)
        scale = jnp.sum(wave, axis=1, keepdims=True) / jnp.sum(kept, axis=1, keepdims=True)
        def scaled_map(line, count, width, spans):
            parts = [toeplitz(kept[line(e)], count, width, *span) for e, span in spans]
            return functools.reduce(jnp.add, parts)

        def row_line(e):
            return slice(2 * e, 2 * e + 1)

        def col_line(e):
            return slice(2 * e + 1, 2 * e + 2)

        width = -(-epochs * RIM // LANES) * LANES
        upper, lower = [
            scaled_map(
                row_line,
                BAND,
                width,
                [(e, (shift - e * RIM, e * RIM, (e + 1) * RIM)) for e in range(epochs)],
            )
            for shift in (0, BAND - RIM)
        ]
        rim_maps = [
            jnp.where(is_odd, *pair).astype(BF16)[:, : epochs * RIM]
            for pair in ((upper, lower), (lower, upper))
        ]
        inner_maps, lefts, rights, gains = [], [], [], []
        for e in range(epochs):
            gains.append(scale[row_line(e)] * scale[col_line(e)] * cor_ref[0, 0, e].astype(F32))
            inner_maps.append(
                scaled_map(row_line, inner, side, [(e, (reach - BAND, 0, WINDOW))])
                .astype(BF16)[:, :WINDOW]
            )
            turned = kept[col_line(e)]
            same, behind, ahead = (
                toeplitz(turned, LANES, LANES, shift, 0, LANES).astype(BF16)
                for shift in (0, -LANES, LANES)
            )
            zero = jnp.zeros_like(same)
            lower = jnp.concatenate([behind, same], axis=1)
            lefts.append(jnp.concatenate([jnp.concatenate([same, ahead], axis=1), lower], axis=0))
            rights.append(jnp.concatenate([jnp.concatenate([zero, ahead], axis=1), lower], axis=0))

    def pixels(e, segment):
        at = segments[segment]
        masked = inv_ref[e, at] * val_ref[e, at].astype(F32) * gains[e]
        return jnp.concatenate([(masked * exp_ref[e, at]).astype(BF16), masked.astype(BF16)], axis=0)

    def columns(part, e):
        left = dot(part[:, :side], lefts[e])
        right = dot(part[:, pcols - side :], rights[e])
        wide = jnp.concatenate(
            [left[:, :LANES], left[:, LANES:] + right[:, :LANES], right[:, LANES:]], axis=1
        ).astype(BF16)
        half = wide.shape[0] // 2
        return jnp.concatenate([wide[:half], wide[half:]], axis=1)

    ends = (slice(0, LANES), slice(pcols - LANES, pcols))

    def arrive(segment):
        for which in range(3):
            load(segment, which).wait()

    ways = (1 - odd, odd)

    def warp_columns(segment):
        warped = [columns(pixels(e, segment), e) for e in range(epochs)]
        for e in range(epochs):
            slab[e, segments[segment]] = warped[e]
        return warped

    def warp_rim(slot, warped):
        value = dot(rim_maps[slot], jnp.concatenate(warped, axis=0))
        into = pl.ds(pl.multiple_of(ways[slot] * (prows - BAND), 8), BAND)
        for plane in range(2):
            tile[plane, into, :] = value[:, plane * pcols : (plane + 1) * pcols]

    def dec_give(slot):
        way = ways[slot]
        rim_at = pl.ds(pl.multiple_of(way * (prows - BAND), 8), BAND)
        for plane in range(2):
            for end in range(2):
                dec_out[way, plane, :, end * LANES : (end + 1) * LANES] = tile[
                    plane, rim_at, ends[end]
                ].astype(BF16)
            dec_core_out[way, plane] = tile[plane, rim_at, LANES : 2 * LANES].astype(BF16)

    with jax.named_scope("near_rim"):
        arrive(0)
        warp_rim(0, warp_columns(0))
        dec_give(0)
    with jax.named_scope("barrier"):
        pl.semaphore_wait(
            barrier,
            1
            + not_first.astype(jnp.int32)
            + has_prev.astype(jnp.int32)
            + has_next.astype(jnp.int32)
            + (has_far & (is_even | is_last)).astype(jnp.int32)
            + (has_far & is_even & not_first).astype(jnp.int32),
        )

    def dec_copy(way):
        return pltpu.make_async_remote_copy(
            src_ref=dec_out.at[way],
            dst_ref=dec_in.at[way],
            send_sem=local_sem.at[3 + way],
            recv_sem=dec_recv.at[way],
            device_id=(me_ra, me_dec + (1 if way else -1)),
            device_id_type=MESH,
        )

    def dec_core_copy(way):
        return pltpu.make_async_remote_copy(
            src_ref=dec_core_out.at[way],
            dst_ref=dec_core_in.at[way],
            send_sem=local_sem.at[(5, 1)[way]],
            recv_sem=dec_core_recv.at[way],
            device_id=(me_ra, me_dec + (1 if way else -1)),
            device_id_type=MESH,
        )

    def ra_copy(out, into, send, recv, way, to_dec):
        return pltpu.make_async_remote_copy(
            src_ref=out.at[way],
            dst_ref=into.at[way],
            send_sem=local_sem.at[send[way]],
            recv_sem=recv.at[way],
            device_id=(next_ra if way else prev_ra, to_dec),
            device_id_type=MESH,
        )

    def own_copy(way, size):
        return pltpu.make_async_remote_copy(
            src_ref=own_out.at[way, 0:size],
            dst_ref=own_in.at[way, 0:size],
            send_sem=local_sem.at[7 + way],
            recv_sem=own_recv.at[way],
            device_id=(next_ra if way else prev_ra, me_dec),
            device_id_type=MESH,
        )

    def own_each(action):
        @pl.when(has_far)
        def _():
            action(wide_at, (OWN + HALO) * 3 // 2)

        @pl.when(jnp.logical_not(has_far))
        def _():
            action(own_at, OWN * 3 // 2)

    def own_start(way):
        own_each(lambda at, size: own_copy(way, size).start())

    def own_take(way, end):
        def take(at, size):
            own_copy(way, size).wait_recv()
            for plane, value in enumerate(unpacked(own_in[way, :size], way)):
                tile[plane, at, ends[end]] += value

        own_each(take)

    def near_copy(way):
        return ra_copy(near_out, near_in, (2, 6), near_recv, way, me_dec)

    def corner_copy(way):
        return ra_copy(corner_out, corner_in, (9, 10), corner_recv, way, far)

    def dec_send(way):
        dec_copy(way).start()
        dec_core_copy(way).start()

    def far_dec_send(way):
        dec_core_copy(way).start()
        dec_copy(way).start()

    pl.when(is_odd)(functools.partial(dec_send, 0))
    pl.when(is_even & has_next)(functools.partial(dec_send, 1))

    def edge_at(part):
        first = 2 * MARGIN - BAND + part * (prows - 4 * MARGIN + BAND)
        return pl.ds(pl.multiple_of(first, 8), BAND)

    far_rim = pl.ds(pl.multiple_of(odd * (prows - BAND), 8), BAND)
    own_at = pl.ds(pl.multiple_of(MARGIN + odd * MARGIN, 8), OWN)
    wide_at = pl.ds(pl.multiple_of(MARGIN - HALO + odd * BAND, 8), OWN + HALO)
    far_at, near_at = edge_at(odd), edge_at(1 - odd)

    @pl.when(has_far & is_even & not_first)
    def _():
        pl.semaphore_signal(ready_corner, inc=1, device_id=(prev_ra, far), device_id_type=MESH)

    @pl.when(has_far & is_even & not_last)
    def _():
        pl.semaphore_signal(ready_corner, inc=1, device_id=(next_ra, far), device_id_type=MESH)

    @pl.when(is_last)
    def _():
        pl.semaphore_signal(ready_wrap, inc=1, device_id=(next_ra, me_dec), device_id_type=MESH)

    @pl.when(is_last & has_far)
    def _():
        pl.semaphore_signal(ready_wrap, inc=1, device_id=(next_ra, far), device_id_type=MESH)

    with jax.named_scope("inner"):
        arrive(1)
        warp_columns(1)
        far_in = pl.ds(pl.multiple_of(odd * top_first, GROUP), RIM)
        warp_rim(1, [slab[e, far_in] for e in range(epochs)])
        value = functools.reduce(
            jnp.add,
            [dot(inner_maps[e], slab[e, reach : reach + WINDOW]) for e in range(epochs)],
        )
        for plane in range(2):
            tile[plane, BAND : BAND + inner, :] = value[:, plane * pcols : (plane + 1) * pcols]

    def corner_give(way):
        corner_out[way] = packed(tile[:, far_rim, ends[way]], way)

    def own_give(way):
        def give(at, size):
            own_out[way, :size] = packed(tile[:, at, ends[way]], way)
            if way:
                own_copy(1, size).start()
            else:

                @pl.when(not_first)
                def _():
                    own_copy(0, size).start()

        own_each(give)

    def add_band(way, at):
        for end in range(2):
            tile[:, at, ends[end]] += dec_in[way, :, :, end * LANES : (end + 1) * LANES].astype(F32)

    with jax.named_scope("corner_send"):

        @pl.when(has_far & is_even)
        def _():
            corner_give(1)
            corner_copy(1).start()
            corner_give(0)

            @pl.when(not_first)
            def _():
                corner_copy(0).start()

    with jax.named_scope("own_send"):
        own_give(1)

    with jax.named_scope("near_send"):
        for part, present in ((0, is_odd), (1, has_next & is_even)):

            @pl.when(present)
            def _():
                dec_copy(1 - part).wait_recv()
                add_band(1 - part, edge_at(part))

        near_out[1] = packed(tile[:, near_at, ends[1]], 1)

        @pl.when(not_last | is_even)
        def _():
            near_copy(1).start()

    with jax.named_scope("far_send"):
        own_give(0)
        near_out[0] = packed(tile[:, near_at, ends[0]], 0)

        @pl.when(not_first)
        def _():
            near_copy(0).start()

        @pl.when(has_far)
        def _():
            dec_give(1)
            pl.when(is_even)(functools.partial(far_dec_send, 0))
            pl.when(is_odd)(functools.partial(far_dec_send, 1))

        @pl.when(has_far & is_odd)
        def _():
            for way in (1, 0):
                corner_give(way)

        @pl.when(is_last & is_odd)
        def _():
            near_copy(1).start()

    small[3].wait()
    side_k = psf_ref.shape[0]
    taps[...] = jnp.zeros_like(taps)
    taps[ROW_PAD : ROW_PAD + side_k, 0:side_k] = psf_ref[...].astype(F32)
    offset = MARGIN - HALF
    across = lax.broadcasted_iota(jnp.int32, (LANES, LANES), 1)
    down = lax.broadcasted_iota(jnp.int32, (LANES, LANES), 0)
    last_tap = taps.shape[0] - 1
    mirror = jnp.where(across + down == last_tap, 1.0, 0.0).astype(BF16)
    taps[...] = dot(taps[...].astype(BF16), mirror)
    turn = LANES - last_tap - offset
    level = across - down >= turn

    def build(k, carry):
        for s in range(GROUP // 2):
            at = pl.ds(pl.multiple_of((k * (GROUP // 2) + s) * LANES, LANES), LANES)
            for parity in range(2):
                row = taps[pl.ds(k * GROUP + 2 * s + parity, 1), :]
                spread_row = jnp.broadcast_to(row, (LANES, LANES))
                turned = pltpu.roll(spread_row, turn, 1, stride=1, stride_axis=0)
                for block in range(2):
                    first = (2 * block + parity) * LANES
                    keep = jnp.logical_not(level) if block else level
                    bands[at, first : first + LANES] = jnp.where(keep, turned, 0.0).astype(BF16)
        return carry

    with jax.named_scope("bands"):
        lax.fori_loop(0, groups, build, 0)

    @pl.when(has_far & is_odd & not_last)
    def _():
        pl.semaphore_wait(ready_corner, 1 + not_first.astype(jnp.int32))
        corner_copy(1).start()

    @pl.when(has_far & is_odd & is_last)
    def _():
        pl.semaphore_wait(ready_corner, 1)
        corner_copy(1).start()

    @pl.when(has_far & is_odd & not_first)
    def _():
        corner_copy(0).start()

    span = coadd.shape[0]
    above = HALF + ROW_PAD
    deep, tall = shifts.shape[0], rows + GROUP
    top = MARGIN - above

    def spread(into, where, held=(0, span), kept_rows=(0, deep)):
        first, last = held
        numer = tile[0, top + first : top + last, where]
        denom = tile[1, top + first : top + last, where]
        row_id = lax.broadcasted_iota(jnp.int32, (last - first, 1), 0) + (me_dec * rows + first - above)
        inside = (row_id >= 0) & (row_id < n_dec * rows)
        coadd[first:last, where] = jnp.where(inside, numer / jnp.maximum(denom, 1.0), 0.0).astype(BF16)
        first, last = kept_rows
        for s in range(GROUP // 2):
            into[first:last, s * LANES : (s + 1) * LANES] = coadd[
                2 * s + first : 2 * s + last, where
            ]

    @pl.when(is_first)
    def _():
        pl.semaphore_wait(ready_wrap, 1 + has_far.astype(jnp.int32))
        own_start(0)
        near_copy(0).start()

    @pl.when(is_first & has_far)
    def _():
        corner_copy(0).start()

    with jax.named_scope("far_receive"):
        for part, present in ((0, has_prev), (1, has_next)):

            @pl.when(present)
            def _():
                dec_core_copy(1 - part).wait_recv()
                tile[:, edge_at(part), LANES : 2 * LANES] += dec_core_in[1 - part].astype(F32)

    with jax.named_scope("middle"):
        spread(shifts, slice(LANES, 2 * LANES))
        inner_sum[...] = product(shifts, bands, 0, tall, slice(None))

    for part, present in ((0, has_prev & is_even), (1, has_next & is_odd)):

        @pl.when(present)
        def _():
            dec_copy(1 - part).wait_recv()
            add_band(1 - part, edge_at(part))

    weight_ref[:, MARGIN : MARGIN + LANES] = tile[1, MARGIN : MARGIN + rows, LANES : 2 * LANES]

    half = rows // 2
    reached = half + groups * GROUP

    def far_own(end):
        way = 1 - end

        @pl.when(has_far)
        def _():
            corner_copy(way).wait_recv()
            for plane, value in enumerate(unpacked(corner_in[way], way)):
                tile[plane, far_at, ends[end]] += value

        own_take(way, end)

    def near_weight(end):
        way = 1 - end
        near_copy(way).wait_recv()
        for plane, value in enumerate(unpacked(near_in[way], way)):
            tile[plane, near_at, ends[end]] += value
        into = slice(end * (cols - MARGIN), end * (cols - MARGIN) + MARGIN)
        first = pcols - LANES if end else MARGIN
        weight_ref[:, into] = tile[1, MARGIN : MARGIN + rows, first : first + MARGIN]

    late = late_end(n_ra)
    with jax.named_scope("early_end"):
        for end in range(2):

            @pl.when(late == 1 - end)
            def _():
                far_own(end)
                near_weight(end)
                spread(end_shifts.at[end], ends[end])
                matched_ref[:, end * LANES : (end + 1) * LANES] = end_sums(
                    end, inner_sum, end_shifts, bands, 0, rows
                )

    def way_sent(way):
        own_each(lambda at, size: own_copy(way, size).wait_send())
        near_copy(way).wait_send()

        @pl.when(has_far)
        def _():
            corner_copy(way).wait_send()

    with jax.named_scope("sent"):
        for way, present in ((0, has_prev), (1, has_next)):

            @pl.when(present)
            def _():
                dec_copy(way).wait_send()
                dec_core_copy(way).wait_send()

        way_sent(1)

        @pl.when(not_first)
        def _():
            way_sent(0)

    with jax.named_scope("late_end"):
        for end in range(2):

            @pl.when((late == end) & is_odd)
            def _():
                far_own(end)
                near_weight(end)
                spread(end_shifts.at[end], ends[end])

            @pl.when((late == end) & is_even)
            def _():
                far_own(end)
                spread(end_shifts.at[end], ends[end], (0, reached), (0, reached))
                matched_ref[:half, end * LANES : (end + 1) * LANES] = end_sums(
                    end, inner_sum, end_shifts, bands, 0, half
                )
                near_weight(end)
                spread(
                    end_shifts.at[end], ends[end], (reached, reached + half), (reached - GROUP, deep)
                )

    @pl.when(is_first)
    def _():
        way_sent(0)


def finish(
    n_ra, matched_in, weight_in, bands, inner_sum, end_shifts, matched_out, weight_out, held, sems
):
    weight = pltpu.make_async_copy(weight_in, weight_out, sems.at[0])
    weight.start()
    late = late_end(n_ra)
    rows = held.shape[0]
    odd = lax.rem(lax.axis_index("dec"), 2)
    for end in range(2):
        for parity, first in ((1, 0), (0, rows // 2)):

            @pl.when((late == end) & (odd == parity))
            def _():
                early_at = slice((1 - end) * LANES, (2 - end) * LANES)
                late_at = slice(end * LANES, (end + 1) * LANES)
                copies = [
                    pltpu.make_async_copy(
                        matched_in.at[:, early_at], matched_out.at[:, early_at], sems.at[1]
                    ),
                    pltpu.make_async_copy(
                        held.at[first:rows], matched_out.at[first:rows, late_at], sems.at[2]
                    ),
                ]
                if first:
                    copies.append(
                        pltpu.make_async_copy(
                            matched_in.at[0:first, late_at],
                            matched_out.at[0:first, late_at],
                            sems.at[3],
                        )
                    )
                    copies[2].start()
                copies[0].start()
                held[first:rows] = end_sums(
                    end, inner_sum, end_shifts, bands, first, rows - first
                )
                copies[1].start()
                for copy in copies:
                    copy.wait()

    weight.wait()


def solution(mesh):
    n_ra, n_dec = mesh.shape["ra"], mesh.shape["dec"]

    def shards(exposures, inv_variance, pixel_valid, correlation, pixel_offset, subpixel, psf_match):
        epochs, prows, pcols = exposures.shape
        rows, cols = prows - 2 * MARGIN, pcols - 2 * MARGIN
        groups = -(-psf_match.shape[0] // GROUP)
        deep = rows + GROUP * groups
        result = jax.ShapeDtypeStruct((rows, cols), F32)
        hbm = pl.BlockSpec(memory_space=pltpu.HBM)
        vmem = pl.BlockSpec(memory_space=pltpu.VMEM)
        sums = pl.pallas_call(
            functools.partial(kernel, (epochs, prows, pcols, n_ra, n_dec)),
            out_shape=(
                result,
                result,
                jax.ShapeDtypeStruct((groups * GROUP // 2 * LANES, 4 * LANES), BF16),
                jax.ShapeDtypeStruct((rows + GROUP, 4 * LANES), F32),
                jax.ShapeDtypeStruct((2, deep, GROUP // 2 * LANES), BF16),
            ),
            in_specs=[hbm] * 7,
            out_specs=(vmem,) * 5,
            scratch_shapes=[
                pltpu.VMEM((epochs, prows, pcols), F32),
                pltpu.VMEM((epochs, prows, pcols), F32),
                pltpu.VMEM((epochs, prows, pcols), jnp.int32),
                pltpu.SMEM(correlation.shape, jnp.int32),
                pltpu.SMEM(pixel_offset.shape, jnp.int32),
                pltpu.SMEM(subpixel.shape, F32),
                pltpu.VMEM(psf_match.shape, BF16),
                pltpu.VMEM((2, prows, pcols), F32),
                pltpu.VMEM((epochs, prows, 2 * pcols), BF16),
                pltpu.VMEM((2, 2, BAND, 2 * LANES), BF16),
                pltpu.VMEM((2, 2, BAND, 2 * LANES), BF16),
                pltpu.VMEM((2, 2, BAND, LANES), BF16),
                pltpu.VMEM((2, 2, BAND, LANES), BF16),
                pltpu.VMEM((2, (OWN + HALO) * 3 // 2, LANES), BF16),
                pltpu.VMEM((2, (OWN + HALO) * 3 // 2, LANES), BF16),
                pltpu.VMEM((2, BAND * 3 // 2, LANES), BF16),
                pltpu.VMEM((2, BAND * 3 // 2, LANES), BF16),
                pltpu.VMEM((2, BAND * 3 // 2, LANES), BF16),
                pltpu.VMEM((2, BAND * 3 // 2, LANES), BF16),
                pltpu.VMEM((groups * GROUP, LANES), F32),
                pltpu.VMEM((deep + GROUP, pcols), BF16),
                pltpu.VMEM((deep, GROUP // 2 * LANES), BF16),
                pltpu.SemaphoreType.DMA((11,)),
                pltpu.SemaphoreType.DMA((2,)),
                pltpu.SemaphoreType.DMA((2,)),
                pltpu.SemaphoreType.DMA((2,)),
                pltpu.SemaphoreType.DMA((2,)),
                pltpu.SemaphoreType.DMA((2,)),
                pltpu.SemaphoreType.REGULAR,
                pltpu.SemaphoreType.REGULAR,
            ],
            compiler_params=pltpu.CompilerParams(
                collective_id=0, has_side_effects=True, vmem_limit_bytes=24 * 1024 * 1024
            ),
            name="coadd",
        )(*[pltpu.with_memory_space_constraint(x, pltpu.HBM) for x in (exposures, inv_variance, pixel_valid, correlation, pixel_offset, subpixel, psf_match)])
        return pl.pallas_call(
            functools.partial(finish, n_ra),
            out_shape=(result, result),
            in_specs=[vmem] * 5,
            out_specs=(hbm, hbm),
            scratch_shapes=[pltpu.VMEM((rows, LANES), F32), pltpu.SemaphoreType.DMA((4,))],
            compiler_params=pltpu.CompilerParams(vmem_limit_bytes=8 * 1024 * 1024),
            name="finish",
        )(*sums)

    return jax.shard_map(
        shards,
        mesh=mesh,
        in_specs=(
            P(None, "dec", "ra"),
            P(None, "dec", "ra"),
            P(None, "dec", "ra"),
            P("dec", "ra", None),
            P("dec", "ra", None, None),
            P("dec", "ra", None, None),
            P(),
        ),
        out_specs=(P("dec", "ra"), P("dec", "ra")),
        check_vma=False,
    )
```

```python
import functools
import math

import jax
import jax.numpy as jnp
from jax import lax
from jax.experimental import pallas as pl
from jax.experimental.pallas import tpu as pltpu
from jax.sharding import PartitionSpec as P

MARGIN = 64
HALF = 31
LANES = 128
BAND = 96
GROUP = 16
RIM = 112
OWN = 128
HALO = 32
WINDOW = 160
ROW_PAD = 1
F32 = jnp.float32
BF16 = jnp.bfloat16
MESH = pl.DeviceIdType.MESH
SERIES = tuple((-1.0) ** k / math.factorial(2 * k + 1) for k in range(12))


def dot(a, b):
    return jnp.dot(a, b, preferred_element_type=F32)


def lanczos(x):
    angle = (jnp.pi / 3.0) * x
    square = angle * angle
    ratio = jnp.full_like(x, SERIES[-1])
    for term in SERIES[-2::-1]:
        ratio = ratio * square + term
    both = ratio * ratio
    return jnp.where(jnp.abs(x) < 3.0, both * (1.0 - (4.0 / 3.0) * square * both), 0.0)


def toeplitz(row, count, width, shift, first, last):
    spread = jnp.broadcast_to(row, (count, LANES))
    turned = pltpu.roll(spread, (LANES // 2 - shift) % LANES, 1, stride=1, stride_axis=0)
    lanes = lax.broadcasted_iota(jnp.int32, (count, LANES), 1)
    down = lax.broadcasted_iota(jnp.int32, (count, LANES), 0)
    blocks = []
    for block in range(width // LANES):
        lane = lanes + block * LANES
        inside = jnp.abs(lane - down + shift) < LANES // 2
        inside = inside & (lane >= first) & (lane < last)
        blocks.append(jnp.where(inside, turned, 0.0))
    return blocks[0] if len(blocks) == 1 else jnp.concatenate(blocks, axis=1)


def lane_ids(value):
    return lax.broadcasted_iota(jnp.int32, value.shape, 1)


def packed(planes, way):
    first, second = planes[0], planes[1]
    if way:
        first, second = pltpu.roll(first, BAND, 1), pltpu.roll(second, BAND, 1)
    half = first.shape[0] // 2
    upper = jnp.where(lane_ids(first) < BAND, first, pltpu.roll(second, LANES - BAND, 1))
    low, high = second[:half], second[half:]
    lower = jnp.where(lane_ids(low) < LANES // 2, low, pltpu.roll(high, LANES // 2, 1))
    return jnp.concatenate([upper, lower], axis=0).astype(BF16)


def unpacked(value, way):
    value = value.astype(F32)
    half = value.shape[0] // 3
    upper, lower = value[: 2 * half], value[2 * half :]
    lanes = lane_ids(upper)
    first = jnp.where(lanes < BAND, upper, 0.0)
    low = jnp.concatenate([lower, pltpu.roll(lower, LANES // 2, 1)], axis=0)
    high = jnp.where(lanes < BAND, pltpu.roll(upper, BAND, 1), 0.0)
    second = jnp.where(lanes < LANES // 2, low, high)
    if way:
        first, second = pltpu.roll(first, LANES - BAND, 1), pltpu.roll(second, LANES - BAND, 1)
    return first, second


def product(shifts, bands, first, tall, chosen):
    groups = bands.shape[0] // shifts.shape[1]
    stacked = jnp.concatenate(
        [shifts[first + k * GROUP : first + k * GROUP + tall, :] for k in range(groups)], axis=1
    )
    return dot(stacked, bands[:, chosen])


def end_sums(end, inner_sum, end_shifts, bands, first, rows):
    picked = slice((1 - end) * 2 * LANES, (2 - end) * 2 * LANES)
    tall = rows + GROUP
    total = inner_sum[first : first + tall, end * 2 * LANES : (end + 1) * 2 * LANES] + product(
        end_shifts.at[end], bands, first, tall, picked
    )
    return total[:rows, :LANES] + total[1 : rows + 1, LANES:]


def late_end(n_ra):
    me = lax.axis_index("ra")
    left_last = (me == 0) | ((lax.rem(me, 2) == 1) & (me < n_ra - 1))
    return jnp.where(left_last, 0, 1)


def kernel(
    dims,
    exp_hbm,
    inv_hbm,
    val_hbm,
    cor_hbm,
    off_hbm,
    sub_hbm,
    psf_hbm,
    matched_ref,
    weight_ref,
    bands,
    inner_sum,
    end_shifts,
    exp_ref,
    inv_ref,
    val_ref,
    cor_ref,
    off_ref,
    sub_ref,
    psf_ref,
    tile,
    slab,
    dec_out,
    dec_in,
    dec_core_out,
    dec_core_in,
    own_out,
    own_in,
    near_out,
    near_in,
    corner_out,
    corner_in,
    taps,
    coadd,
    shifts,
    local_sem,
    dec_recv,
    dec_core_recv,
    own_recv,
    near_recv,
    corner_recv,
    ready_wrap,
    ready_corner,
):
    epochs, prows, pcols, n_ra, n_dec = dims
    rows, cols = prows - 2 * MARGIN, pcols - 2 * MARGIN
    me_ra, me_dec = lax.axis_index("ra"), lax.axis_index("dec")
    prev_ra, next_ra = lax.rem(me_ra + n_ra - 1, n_ra), lax.rem(me_ra + 1, n_ra)
    has_prev, has_next = me_dec > 0, me_dec < n_dec - 1
    is_first, not_first = me_ra == 0, me_ra > 0
    is_last, not_last = me_ra == n_ra - 1, me_ra < n_ra - 1
    odd = lax.rem(me_dec, 2)
    is_odd, is_even = odd == 1, odd == 0
    far = me_dec - 1 + 2 * odd
    has_far = (far >= 0) & (far < n_dec)
    has_near = jnp.where(is_odd, has_prev, has_next)

    small = [
        pltpu.make_async_copy(src, dst, local_sem.at[i % 3])
        for i, (src, dst) in enumerate(
            ((off_hbm, off_ref), (sub_hbm, sub_ref), (cor_hbm, cor_ref), (psf_hbm, psf_ref))
        )
    ]
    top_first = prows - RIM
    segments = (
        pl.ds(pl.multiple_of((1 - odd) * top_first, GROUP), RIM),
        pl.ds(pl.multiple_of(odd * RIM, GROUP), top_first),
    )

    def load(segment, which):
        src, dst = ((inv_hbm, inv_ref), (val_hbm, val_ref), (exp_hbm, exp_ref))[which]
        return pltpu.make_async_copy(
            src.at[:, segments[segment]], dst.at[:, segments[segment]], local_sem.at[3 + 3 * segment + which]
        )

    loads = [load(segment, which) for segment in range(2) for which in range(3)]
    for copy in small[:3] + loads:
        copy.start()

    barrier = pltpu.get_barrier_semaphore()
    pl.semaphore_signal(barrier, inc=1, device_id=(prev_ra, me_dec), device_id_type=MESH)

    @pl.when(not_last)
    def _():
        pl.semaphore_signal(barrier, inc=1, device_id=(next_ra, me_dec), device_id_type=MESH)

    @pl.when(has_far & (is_odd | is_first))
    def _():
        pl.semaphore_signal(barrier, inc=1, device_id=(prev_ra, far), device_id_type=MESH)

    @pl.when(has_far & is_odd & not_last)
    def _():
        pl.semaphore_signal(barrier, inc=1, device_id=(next_ra, far), device_id_type=MESH)

    @pl.when(has_prev)
    def _():
        pl.semaphore_signal(barrier, inc=1, device_id=(me_ra, me_dec - 1), device_id_type=MESH)

    @pl.when(has_next)
    def _():
        pl.semaphore_signal(barrier, inc=1, device_id=(me_ra, me_dec + 1), device_id_type=MESH)

    for copy in small[:3]:
        copy.wait()
    small[3].start()
    inner = prows - 2 * BAND
    groups = taps.shape[0] // GROUP
    side = 2 * LANES
    reach = RIM - (WINDOW - (prows - 2 * RIM)) // 2
    with jax.named_scope("maps"):
        lane = lax.broadcasted_iota(jnp.int32, (8, LANES), 1).astype(F32) - LANES // 2
        which_map = lax.broadcasted_iota(jnp.int32, (8, LANES), 0)
        place = lane
        for e in range(epochs):
            shift_r = off_ref[0, 0, e, 0].astype(F32) + sub_ref[0, 0, e, 0]
            shift_c = off_ref[0, 0, e, 1].astype(F32) + sub_ref[0, 0, e, 1]
            place = jnp.where(which_map == 2 * e, shift_r - lane, place)
            place = jnp.where(which_map == 2 * e + 1, shift_c + lane, place)
        wave = lanczos(place)
        kept = wave.astype(BF16).astype(F32)
        scale = jnp.sum(wave, axis=1, keepdims=True) / jnp.sum(kept, axis=1, keepdims=True)
        def scaled_map(line, count, width, spans):
            parts = [toeplitz(kept[line(e)], count, width, *span) for e, span in spans]
            return functools.reduce(jnp.add, parts)

        def row_line(e):
            return slice(2 * e, 2 * e + 1)

        def col_line(e):
            return slice(2 * e + 1, 2 * e + 2)

        width = -(-epochs * RIM // LANES) * LANES
        upper, lower = [
            scaled_map(
                row_line,
                BAND,
                width,
                [(e, (shift - e * RIM, e * RIM, (e + 1) * RIM)) for e in range(epochs)],
            )
            for shift in (0, BAND - RIM)
        ]
        rim_maps = [
            jnp.where(is_odd, *pair).astype(BF16)[:, : epochs * RIM]
            for pair in ((upper, lower), (lower, upper))
        ]
        inner_maps, lefts, rights, gains = [], [], [], []
        for e in range(epochs):
            gains.append(scale[row_line(e)] * scale[col_line(e)] * cor_ref[0, 0, e].astype(F32))
            inner_maps.append(
                scaled_map(row_line, inner, side, [(e, (reach - BAND, 0, WINDOW))])
                .astype(BF16)[:, :WINDOW]
            )
            turned = kept[col_line(e)]
            same, behind, ahead = (
                toeplitz(turned, LANES, LANES, shift, 0, LANES).astype(BF16)
                for shift in (0, -LANES, LANES)
            )
            zero = jnp.zeros_like(same)
            lower = jnp.concatenate([behind, same], axis=1)
            lefts.append(jnp.concatenate([jnp.concatenate([same, ahead], axis=1), lower], axis=0))
            rights.append(jnp.concatenate([jnp.concatenate([zero, ahead], axis=1), lower], axis=0))

    def pixels(e, segment):
        at = segments[segment]
        masked = inv_ref[e, at] * val_ref[e, at].astype(F32) * gains[e]
        return jnp.concatenate([(masked * exp_ref[e, at]).astype(BF16), masked.astype(BF16)], axis=0)

    def columns(part, e):
        left = dot(part[:, :side], lefts[e])
        right = dot(part[:, pcols - side :], rights[e])
        wide = jnp.concatenate(
            [left[:, :LANES], left[:, LANES:] + right[:, :LANES], right[:, LANES:]], axis=1
        ).astype(BF16)
        half = wide.shape[0] // 2
        return jnp.concatenate([wide[:half], wide[half:]], axis=1)

    ends = (slice(0, LANES), slice(pcols - LANES, pcols))

    def arrive(segment):
        for which in range(3):
            load(segment, which).wait()

    ways = (1 - odd, odd)

    def warp_columns(segment):
        warped = [columns(pixels(e, segment), e) for e in range(epochs)]
        for e in range(epochs):
            slab[e, segments[segment]] = warped[e]
        return warped

    def warp_rim(slot, warped):
        value = dot(rim_maps[slot], jnp.concatenate(warped, axis=0))
        into = pl.ds(pl.multiple_of(ways[slot] * (prows - BAND), 8), BAND)
        for plane in range(2):
            tile[plane, into, :] = value[:, plane * pcols : (plane + 1) * pcols]

    def dec_give(slot):
        way = ways[slot]
        rim_at = pl.ds(pl.multiple_of(way * (prows - BAND), 8), BAND)
        for plane in range(2):
            for end in range(2):
                dec_out[way, plane, :, end * LANES : (end + 1) * LANES] = tile[
                    plane, rim_at, ends[end]
                ].astype(BF16)
            dec_core_out[way, plane] = tile[plane, rim_at, LANES : 2 * LANES].astype(BF16)

    with jax.named_scope("near_rim"):
        arrive(0)
        warp_rim(0, warp_columns(0))
        dec_give(0)
    with jax.named_scope("barrier"):
        pl.semaphore_wait(
            barrier,
            1
            + not_first.astype(jnp.int32)
            + has_prev.astype(jnp.int32)
            + has_next.astype(jnp.int32)
            + (has_far & (is_even | is_last)).astype(jnp.int32)
            + (has_far & is_even & not_first).astype(jnp.int32),
        )

    def dec_copy(way):
        return pltpu.make_async_remote_copy(
            src_ref=dec_out.at[way],
            dst_ref=dec_in.at[way],
            send_sem=local_sem.at[3 + way],
            recv_sem=dec_recv.at[way],
            device_id=(me_ra, me_dec + (1 if way else -1)),
            device_id_type=MESH,
        )

    def dec_core_copy(way):
        return pltpu.make_async_remote_copy(
            src_ref=dec_core_out.at[way],
            dst_ref=dec_core_in.at[way],
            send_sem=local_sem.at[(5, 1)[way]],
            recv_sem=dec_core_recv.at[way],
            device_id=(me_ra, me_dec + (1 if way else -1)),
            device_id_type=MESH,
        )

    def ra_copy(out, into, send, recv, way, to_dec):
        return pltpu.make_async_remote_copy(
            src_ref=out.at[way],
            dst_ref=into.at[way],
            send_sem=local_sem.at[send[way]],
            recv_sem=recv.at[way],
            device_id=(next_ra if way else prev_ra, to_dec),
            device_id_type=MESH,
        )

    def own_copy(way, size):
        return pltpu.make_async_remote_copy(
            src_ref=own_out.at[way, 0:size],
            dst_ref=own_in.at[way, 0:size],
            send_sem=local_sem.at[7 + way],
            recv_sem=own_recv.at[way],
            device_id=(next_ra if way else prev_ra, me_dec),
            device_id_type=MESH,
        )

    def own_each(action):
        @pl.when(has_far)
        def _():
            action(wide_at, (OWN + HALO) * 3 // 2)

        @pl.when(jnp.logical_not(has_far))
        def _():
            action(own_at, OWN * 3 // 2)

    def own_start(way):
        own_each(lambda at, size: own_copy(way, size).start())

    def own_take(way, end):
        def take(at, size):
            own_copy(way, size).wait_recv()
            for plane, value in enumerate(unpacked(own_in[way, :size], way)):
                tile[plane, at, ends[end]] += value

        own_each(take)

    def near_copy(way):
        return ra_copy(near_out, near_in, (2, 6), near_recv, way, me_dec)

    def corner_copy(way):
        return ra_copy(corner_out, corner_in, (9, 10), corner_recv, way, far)

    def dec_send(way):
        dec_copy(way).start()
        dec_core_copy(way).start()

    def far_dec_send(way):
        dec_core_copy(way).start()
        dec_copy(way).start()

    pl.when(is_odd)(functools.partial(dec_send, 0))
    pl.when(is_even & has_next)(functools.partial(dec_send, 1))

    def edge_at(part):
        first = 2 * MARGIN - BAND + part * (prows - 4 * MARGIN + BAND)
        return pl.ds(pl.multiple_of(first, 8), BAND)

    far_rim = pl.ds(pl.multiple_of(odd * (prows - BAND), 8), BAND)
    own_at = pl.ds(pl.multiple_of(MARGIN + odd * MARGIN, 8), OWN)
    wide_at = pl.ds(pl.multiple_of(MARGIN - HALO + odd * BAND, 8), OWN + HALO)
    far_at, near_at = edge_at(odd), edge_at(1 - odd)

    @pl.when(has_far & is_even & not_first)
    def _():
        pl.semaphore_signal(ready_corner, inc=1, device_id=(prev_ra, far), device_id_type=MESH)

    @pl.when(has_far & is_even & not_last)
    def _():
        pl.semaphore_signal(ready_corner, inc=1, device_id=(next_ra, far), device_id_type=MESH)

    @pl.when(is_last)
    def _():
        pl.semaphore_signal(ready_wrap, inc=1, device_id=(next_ra, me_dec), device_id_type=MESH)

    @pl.when(is_last & has_far)
    def _():
        pl.semaphore_signal(ready_wrap, inc=1, device_id=(next_ra, far), device_id_type=MESH)

    with jax.named_scope("inner"):
        arrive(1)
        warp_columns(1)
        far_in = pl.ds(pl.multiple_of(odd * top_first, GROUP), RIM)
        warp_rim(1, [slab[e, far_in] for e in range(epochs)])
        value = functools.reduce(
            jnp.add,
            [dot(inner_maps[e], slab[e, reach : reach + WINDOW]) for e in range(epochs)],
        )
        for plane in range(2):
            tile[plane, BAND : BAND + inner, :] = value[:, plane * pcols : (plane + 1) * pcols]

    def corner_give(way):
        corner_out[way] = packed(tile[:, far_rim, ends[way]], way)

    def own_give(way):
        def give(at, size):
            own_out[way, :size] = packed(tile[:, at, ends[way]], way)
            if way:
                own_copy(1, size).start()
            else:

                @pl.when(not_first)
                def _():
                    own_copy(0, size).start()

        own_each(give)

    def add_band(way, at):
        for end in range(2):
            tile[:, at, ends[end]] += dec_in[way, :, :, end * LANES : (end + 1) * LANES].astype(F32)

    with jax.named_scope("corner_send"):

        @pl.when(has_far & is_even)
        def _():
            corner_give(1)
            corner_copy(1).start()
            corner_give(0)

            @pl.when(not_first)
            def _():
                corner_copy(0).start()

    with jax.named_scope("own_send"):
        own_give(1)

    with jax.named_scope("near_send"):
        for part, present in ((0, is_odd), (1, has_next & is_even)):

            @pl.when(present)
            def _():
                dec_copy(1 - part).wait_recv()
                add_band(1 - part, edge_at(part))

        near_out[1] = packed(tile[:, near_at, ends[1]], 1)

        @pl.when(not_last | is_even)
        def _():
            near_copy(1).start()

    with jax.named_scope("far_send"):
        own_give(0)
        near_out[0] = packed(tile[:, near_at, ends[0]], 0)

        @pl.when(not_first)
        def _():
            near_copy(0).start()

        @pl.when(has_far)
        def _():
            dec_give(1)
            pl.when(is_even)(functools.partial(far_dec_send, 0))
            pl.when(is_odd)(functools.partial(far_dec_send, 1))

        @pl.when(has_far & is_odd)
        def _():
            for way in (1, 0):
                corner_give(way)

        @pl.when(is_last & is_odd)
        def _():
            near_copy(1).start()

    small[3].wait()
    side_k = psf_ref.shape[0]
    taps[...] = jnp.zeros_like(taps)
    taps[ROW_PAD : ROW_PAD + side_k, 0:side_k] = psf_ref[...].astype(F32)
    offset = MARGIN - HALF
    across = lax.broadcasted_iota(jnp.int32, (LANES, LANES), 1)
    down = lax.broadcasted_iota(jnp.int32, (LANES, LANES), 0)
    last_tap = taps.shape[0] - 1
    mirror = jnp.where(across + down == last_tap, 1.0, 0.0).astype(BF16)
    taps[...] = dot(taps[...].astype(BF16), mirror)
    turn = LANES - last_tap - offset
    level = across - down >= turn

    def build(k, carry):
        for s in range(GROUP // 2):
            at = pl.ds(pl.multiple_of((k * (GROUP // 2) + s) * LANES, LANES), LANES)
            for parity in range(2):
                row = taps[pl.ds(k * GROUP + 2 * s + parity, 1), :]
                spread_row = jnp.broadcast_to(row, (LANES, LANES))
                turned = pltpu.roll(spread_row, turn, 1, stride=1, stride_axis=0)
                for block in range(2):
                    first = (2 * block + parity) * LANES
                    keep = jnp.logical_not(level) if block else level
                    bands[at, first : first + LANES] = jnp.where(keep, turned, 0.0).astype(BF16)
        return carry

    with jax.named_scope("bands"):
        lax.fori_loop(0, groups, build, 0)

    @pl.when(has_far & is_odd & not_last)
    def _():
        pl.semaphore_wait(ready_corner, 1 + not_first.astype(jnp.int32))
        corner_copy(1).start()

    @pl.when(has_far & is_odd & is_last)
    def _():
        pl.semaphore_wait(ready_corner, 1)
        corner_copy(1).start()

    @pl.when(has_far & is_odd & not_first)
    def _():
        corner_copy(0).start()

    span = coadd.shape[0]
    above = HALF + ROW_PAD
    deep, tall = shifts.shape[0], rows + GROUP
    top = MARGIN - above

    def spread(into, where, held=(0, span), kept_rows=(0, deep)):
        first, last = held
        numer = tile[0, top + first : top + last, where]
        denom = tile[1, top + first : top + last, where]
        row_id = lax.broadcasted_iota(jnp.int32, (last - first, 1), 0) + (me_dec * rows + first - above)
        inside = (row_id >= 0) & (row_id < n_dec * rows)
        coadd[first:last, where] = jnp.where(inside, numer / jnp.maximum(denom, 1.0), 0.0).astype(BF16)
        first, last = kept_rows
        for s in range(GROUP // 2):
            into[first:last, s * LANES : (s + 1) * LANES] = coadd[
                2 * s + first : 2 * s + last, where
            ]

    @pl.when(is_first)
    def _():
        pl.semaphore_wait(ready_wrap, 1 + has_far.astype(jnp.int32))
        own_start(0)
        near_copy(0).start()

    @pl.when(is_first & has_far)
    def _():
        corner_copy(0).start()

    with jax.named_scope("far_receive"):
        for part, present in ((0, has_prev), (1, has_next)):

            @pl.when(present)
            def _():
                dec_core_copy(1 - part).wait_recv()
                tile[:, edge_at(part), LANES : 2 * LANES] += dec_core_in[1 - part].astype(F32)

    with jax.named_scope("middle"):
        spread(shifts, slice(LANES, 2 * LANES))
        inner_sum[...] = product(shifts, bands, 0, tall, slice(None))

    for part, present in ((0, has_prev & is_even), (1, has_next & is_odd)):

        @pl.when(present)
        def _():
            dec_copy(1 - part).wait_recv()
            add_band(1 - part, edge_at(part))

    weight_ref[:, MARGIN : MARGIN + LANES] = tile[1, MARGIN : MARGIN + rows, LANES : 2 * LANES]

    half = rows // 2
    reached = half + groups * GROUP

    def far_own(end):
        way = 1 - end

        @pl.when(has_far)
        def _():
            corner_copy(way).wait_recv()
            for plane, value in enumerate(unpacked(corner_in[way], way)):
                tile[plane, far_at, ends[end]] += value

        own_take(way, end)

    def weigh(end, first, last):
        into = slice(end * (cols - MARGIN), end * (cols - MARGIN) + MARGIN)
        lane = pcols - LANES if end else MARGIN
        weight_ref[first:last, into] = tile[
            1, MARGIN + first : MARGIN + last, lane : lane + MARGIN
        ]

    def near_weight(end, first, last):
        way = 1 - end
        near_copy(way).wait_recv()
        for plane, value in enumerate(unpacked(near_in[way], way)):
            tile[plane, near_at, ends[end]] += value
        weigh(end, first, last)

    late = late_end(n_ra)
    with jax.named_scope("early_end"):
        for end in range(2):

            @pl.when(late == 1 - end)
            def _():
                far_own(end)
                near_weight(end, 0, rows)
                spread(end_shifts.at[end], ends[end])
                matched_ref[:, end * LANES : (end + 1) * LANES] = end_sums(
                    end, inner_sum, end_shifts, bands, 0, rows
                )

    def way_sent(way):
        own_each(lambda at, size: own_copy(way, size).wait_send())
        near_copy(way).wait_send()

        @pl.when(has_far)
        def _():
            corner_copy(way).wait_send()

    with jax.named_scope("sent"):
        for way, present in ((0, has_prev), (1, has_next)):

            @pl.when(present)
            def _():
                dec_copy(way).wait_send()
                dec_core_copy(way).wait_send()

        way_sent(1)

        @pl.when(not_first)
        def _():
            way_sent(0)

    with jax.named_scope("late_end"):
        for end in range(2):

            @pl.when((late == end) & is_odd)
            def _():
                far_own(end)
                weigh(end, rows - OWN, rows)
                near_weight(end, 0, rows - OWN)
                spread(end_shifts.at[end], ends[end])

            @pl.when((late == end) & is_even)
            def _():
                far_own(end)
                weigh(end, 0, OWN)
                spread(end_shifts.at[end], ends[end], (0, reached), (0, reached))
                matched_ref[:half, end * LANES : (end + 1) * LANES] = end_sums(
                    end, inner_sum, end_shifts, bands, 0, half
                )
                near_weight(end, OWN, rows)
                spread(
                    end_shifts.at[end], ends[end], (reached, reached + half), (reached - GROUP, deep)
                )

    @pl.when(is_first)
    def _():
        way_sent(0)


def finish(
    n_ra, matched_in, weight_in, bands, inner_sum, end_shifts, matched_out, weight_out, held, sems
):
    weight = pltpu.make_async_copy(weight_in, weight_out, sems.at[0])
    weight.start()
    late = late_end(n_ra)
    rows = held.shape[0]
    odd = lax.rem(lax.axis_index("dec"), 2)
    for end in range(2):
        for parity, first in ((1, 0), (0, rows // 2)):

            @pl.when((late == end) & (odd == parity))
            def _():
                early_at = slice((1 - end) * LANES, (2 - end) * LANES)
                late_at = slice(end * LANES, (end + 1) * LANES)
                copies = [
                    pltpu.make_async_copy(
                        matched_in.at[:, early_at], matched_out.at[:, early_at], sems.at[1]
                    ),
                    pltpu.make_async_copy(
                        held.at[first:rows], matched_out.at[first:rows, late_at], sems.at[2]
                    ),
                ]
                if first:
                    copies.append(
                        pltpu.make_async_copy(
                            matched_in.at[0:first, late_at],
                            matched_out.at[0:first, late_at],
                            sems.at[3],
                        )
                    )
                    copies[2].start()
                copies[0].start()
                held[first:rows] = end_sums(
                    end, inner_sum, end_shifts, bands, first, rows - first
                )
                copies[1].start()
                for copy in copies:
                    copy.wait()

    weight.wait()


def solution(mesh):
    n_ra, n_dec = mesh.shape["ra"], mesh.shape["dec"]

    def shards(exposures, inv_variance, pixel_valid, correlation, pixel_offset, subpixel, psf_match):
        epochs, prows, pcols = exposures.shape
        rows, cols = prows - 2 * MARGIN, pcols - 2 * MARGIN
        groups = -(-psf_match.shape[0] // GROUP)
        deep = rows + GROUP * groups
        result = jax.ShapeDtypeStruct((rows, cols), F32)
        hbm = pl.BlockSpec(memory_space=pltpu.HBM)
        vmem = pl.BlockSpec(memory_space=pltpu.VMEM)
        sums = pl.pallas_call(
            functools.partial(kernel, (epochs, prows, pcols, n_ra, n_dec)),
            out_shape=(
                result,
                result,
                jax.ShapeDtypeStruct((groups * GROUP // 2 * LANES, 4 * LANES), BF16),
                jax.ShapeDtypeStruct((rows + GROUP, 4 * LANES), F32),
                jax.ShapeDtypeStruct((2, deep, GROUP // 2 * LANES), BF16),
            ),
            in_specs=[hbm] * 7,
            out_specs=(vmem,) * 5,
            scratch_shapes=[
                pltpu.VMEM((epochs, prows, pcols), F32),
                pltpu.VMEM((epochs, prows, pcols), F32),
                pltpu.VMEM((epochs, prows, pcols), jnp.int32),
                pltpu.SMEM(correlation.shape, jnp.int32),
                pltpu.SMEM(pixel_offset.shape, jnp.int32),
                pltpu.SMEM(subpixel.shape, F32),
                pltpu.VMEM(psf_match.shape, BF16),
                pltpu.VMEM((2, prows, pcols), F32),
                pltpu.VMEM((epochs, prows, 2 * pcols), BF16),
                pltpu.VMEM((2, 2, BAND, 2 * LANES), BF16),
                pltpu.VMEM((2, 2, BAND, 2 * LANES), BF16),
                pltpu.VMEM((2, 2, BAND, LANES), BF16),
                pltpu.VMEM((2, 2, BAND, LANES), BF16),
                pltpu.VMEM((2, (OWN + HALO) * 3 // 2, LANES), BF16),
                pltpu.VMEM((2, (OWN + HALO) * 3 // 2, LANES), BF16),
                pltpu.VMEM((2, BAND * 3 // 2, LANES), BF16),
                pltpu.VMEM((2, BAND * 3 // 2, LANES), BF16),
                pltpu.VMEM((2, BAND * 3 // 2, LANES), BF16),
                pltpu.VMEM((2, BAND * 3 // 2, LANES), BF16),
                pltpu.VMEM((groups * GROUP, LANES), F32),
                pltpu.VMEM((deep + GROUP, pcols), BF16),
                pltpu.VMEM((deep, GROUP // 2 * LANES), BF16),
                pltpu.SemaphoreType.DMA((11,)),
                pltpu.SemaphoreType.DMA((2,)),
                pltpu.SemaphoreType.DMA((2,)),
                pltpu.SemaphoreType.DMA((2,)),
                pltpu.SemaphoreType.DMA((2,)),
                pltpu.SemaphoreType.DMA((2,)),
                pltpu.SemaphoreType.REGULAR,
                pltpu.SemaphoreType.REGULAR,
            ],
            compiler_params=pltpu.CompilerParams(
                collective_id=0, has_side_effects=True, vmem_limit_bytes=24 * 1024 * 1024
            ),
            name="coadd",
        )(*[pltpu.with_memory_space_constraint(x, pltpu.HBM) for x in (exposures, inv_variance, pixel_valid, correlation, pixel_offset, subpixel, psf_match)])
        return pl.pallas_call(
            functools.partial(finish, n_ra),
            out_shape=(result, result),
            in_specs=[vmem] * 5,
            out_specs=(hbm, hbm),
            scratch_shapes=[pltpu.VMEM((rows, LANES), F32), pltpu.SemaphoreType.DMA((4,))],
            compiler_params=pltpu.CompilerParams(vmem_limit_bytes=8 * 1024 * 1024),
            name="finish",
        )(*sums)

    return jax.shard_map(
        shards,
        mesh=mesh,
        in_specs=(
            P(None, "dec", "ra"),
            P(None, "dec", "ra"),
            P(None, "dec", "ra"),
            P("dec", "ra", None),
            P("dec", "ra", None, None),
            P("dec", "ra", None, None),
            P(),
        ),
        out_specs=(P("dec", "ra"), P("dec", "ra")),
        check_vma=False,
    )
```

```python
import functools
import math

import jax
import jax.numpy as jnp
from jax import lax
from jax.experimental import pallas as pl
from jax.experimental.pallas import tpu as pltpu
from jax.sharding import PartitionSpec as P

MARGIN = 64
HALF = 31
LANES = 128
BAND = 96
GROUP = 16
RIM = 112
OWN = 128
HALO = 32
WINDOW = 160
ROW_PAD = 1
F32 = jnp.float32
BF16 = jnp.bfloat16
MESH = pl.DeviceIdType.MESH
SERIES = tuple((-1.0) ** k / math.factorial(2 * k + 1) for k in range(12))


def dot(a, b):
    return jnp.dot(a, b, preferred_element_type=F32)


def lanczos(x):
    angle = (jnp.pi / 3.0) * x
    square = angle * angle
    ratio = jnp.full_like(x, SERIES[-1])
    for term in SERIES[-2::-1]:
        ratio = ratio * square + term
    both = ratio * ratio
    return jnp.where(jnp.abs(x) < 3.0, both * (1.0 - (4.0 / 3.0) * square * both), 0.0)


def toeplitz(row, count, width, shift, first, last):
    spread = jnp.broadcast_to(row, (count, LANES))
    turned = pltpu.roll(spread, (LANES // 2 - shift) % LANES, 1, stride=1, stride_axis=0)
    lanes = lax.broadcasted_iota(jnp.int32, (count, LANES), 1)
    down = lax.broadcasted_iota(jnp.int32, (count, LANES), 0)
    blocks = []
    for block in range(width // LANES):
        lane = lanes + block * LANES
        inside = jnp.abs(lane - down + shift) < LANES // 2
        inside = inside & (lane >= first) & (lane < last)
        blocks.append(jnp.where(inside, turned, 0.0))
    return blocks[0] if len(blocks) == 1 else jnp.concatenate(blocks, axis=1)


def lane_ids(value):
    return lax.broadcasted_iota(jnp.int32, value.shape, 1)


def packed(planes, way):
    first, second = planes[0], planes[1]
    if way:
        first, second = pltpu.roll(first, BAND, 1), pltpu.roll(second, BAND, 1)
    half = first.shape[0] // 2
    upper = jnp.where(lane_ids(first) < BAND, first, pltpu.roll(second, LANES - BAND, 1))
    low, high = second[:half], second[half:]
    lower = jnp.where(lane_ids(low) < LANES // 2, low, pltpu.roll(high, LANES // 2, 1))
    return jnp.concatenate([upper, lower], axis=0).astype(BF16)


def unpacked(value, way):
    value = value.astype(F32)
    half = value.shape[0] // 3
    upper, lower = value[: 2 * half], value[2 * half :]
    lanes = lane_ids(upper)
    first = jnp.where(lanes < BAND, upper, 0.0)
    low = jnp.concatenate([lower, pltpu.roll(lower, LANES // 2, 1)], axis=0)
    high = jnp.where(lanes < BAND, pltpu.roll(upper, BAND, 1), 0.0)
    second = jnp.where(lanes < LANES // 2, low, high)
    if way:
        first, second = pltpu.roll(first, LANES - BAND, 1), pltpu.roll(second, LANES - BAND, 1)
    return first, second


def product(shifts, bands, first, tall, chosen):
    groups = bands.shape[0] // shifts.shape[1]
    stacked = jnp.concatenate(
        [shifts[first + k * GROUP : first + k * GROUP + tall, :] for k in range(groups)], axis=1
    )
    return dot(stacked, bands[:, chosen])


def end_sums(end, inner_sum, end_shifts, bands, first, rows):
    picked = slice((1 - end) * 2 * LANES, (2 - end) * 2 * LANES)
    tall = rows + GROUP
    total = inner_sum[first : first + tall, end * 2 * LANES : (end + 1) * 2 * LANES] + product(
        end_shifts.at[end], bands, first, tall, picked
    )
    return total[:rows, :LANES] + total[1 : rows + 1, LANES:]


def late_end(n_ra):
    me = lax.axis_index("ra")
    left_last = (me == 0) | ((lax.rem(me, 2) == 1) & (me < n_ra - 1))
    return jnp.where(left_last, 0, 1)


def kernel(
    dims,
    exp_hbm,
    inv_hbm,
    val_hbm,
    cor_hbm,
    off_hbm,
    sub_hbm,
    psf_hbm,
    matched_ref,
    weight_ref,
    bands,
    inner_sum,
    end_shifts,
    exp_ref,
    inv_ref,
    val_ref,
    cor_ref,
    off_ref,
    sub_ref,
    psf_ref,
    tile,
    slab,
    dec_out,
    dec_in,
    dec_core_out,
    dec_core_in,
    own_out,
    own_in,
    near_out,
    near_in,
    corner_out,
    corner_in,
    taps,
    coadd,
    shifts,
    local_sem,
    dec_recv,
    dec_core_recv,
    own_recv,
    near_recv,
    corner_recv,
    ready_wrap,
    ready_corner,
):
    epochs, prows, pcols, n_ra, n_dec = dims
    rows, cols = prows - 2 * MARGIN, pcols - 2 * MARGIN
    me_ra, me_dec = lax.axis_index("ra"), lax.axis_index("dec")
    prev_ra, next_ra = lax.rem(me_ra + n_ra - 1, n_ra), lax.rem(me_ra + 1, n_ra)
    has_prev, has_next = me_dec > 0, me_dec < n_dec - 1
    is_first, not_first = me_ra == 0, me_ra > 0
    is_last, not_last = me_ra == n_ra - 1, me_ra < n_ra - 1
    odd = lax.rem(me_dec, 2)
    is_odd, is_even = odd == 1, odd == 0
    far = me_dec - 1 + 2 * odd
    has_far = (far >= 0) & (far < n_dec)
    has_near = jnp.where(is_odd, has_prev, has_next)

    small = [
        pltpu.make_async_copy(src, dst, local_sem.at[i % 3])
        for i, (src, dst) in enumerate(
            ((off_hbm, off_ref), (sub_hbm, sub_ref), (cor_hbm, cor_ref), (psf_hbm, psf_ref))
        )
    ]
    top_first = prows - RIM
    segments = (
        pl.ds(pl.multiple_of((1 - odd) * top_first, GROUP), RIM),
        pl.ds(pl.multiple_of(odd * RIM, GROUP), top_first),
    )

    def load(segment, which):
        src, dst = ((inv_hbm, inv_ref), (val_hbm, val_ref), (exp_hbm, exp_ref))[which]
        return pltpu.make_async_copy(
            src.at[:, segments[segment]], dst.at[:, segments[segment]], local_sem.at[3 + 3 * segment + which]
        )

    loads = [load(segment, which) for segment in range(2) for which in range(3)]
    for copy in small[:3] + loads:
        copy.start()

    barrier = pltpu.get_barrier_semaphore()
    pl.semaphore_signal(barrier, inc=1, device_id=(prev_ra, me_dec), device_id_type=MESH)

    @pl.when(not_last)
    def _():
        pl.semaphore_signal(barrier, inc=1, device_id=(next_ra, me_dec), device_id_type=MESH)

    @pl.when(has_far & (is_odd | is_first))
    def _():
        pl.semaphore_signal(barrier, inc=1, device_id=(prev_ra, far), device_id_type=MESH)

    @pl.when(has_far & is_odd & not_last)
    def _():
        pl.semaphore_signal(barrier, inc=1, device_id=(next_ra, far), device_id_type=MESH)

    @pl.when(has_prev)
    def _():
        pl.semaphore_signal(barrier, inc=1, device_id=(me_ra, me_dec - 1), device_id_type=MESH)

    @pl.when(has_next)
    def _():
        pl.semaphore_signal(barrier, inc=1, device_id=(me_ra, me_dec + 1), device_id_type=MESH)

    for copy in small[:3]:
        copy.wait()
    small[3].start()
    inner = prows - 2 * BAND
    groups = taps.shape[0] // GROUP
    side = 2 * LANES
    reach = RIM - (WINDOW - (prows - 2 * RIM)) // 2
    with jax.named_scope("maps"):
        lane = lax.broadcasted_iota(jnp.int32, (8, LANES), 1).astype(F32) - LANES // 2
        which_map = lax.broadcasted_iota(jnp.int32, (8, LANES), 0)
        place = lane
        for e in range(epochs):
            shift_r = off_ref[0, 0, e, 0].astype(F32) + sub_ref[0, 0, e, 0]
            shift_c = off_ref[0, 0, e, 1].astype(F32) + sub_ref[0, 0, e, 1]
            place = jnp.where(which_map == 2 * e, shift_r - lane, place)
            place = jnp.where(which_map == 2 * e + 1, shift_c + lane, place)
        wave = lanczos(place)
        kept = wave.astype(BF16).astype(F32)
        scale = jnp.sum(wave, axis=1, keepdims=True) / jnp.sum(kept, axis=1, keepdims=True)
        def scaled_map(line, count, width, spans):
            parts = [toeplitz(kept[line(e)], count, width, *span) for e, span in spans]
            return functools.reduce(jnp.add, parts)

        def row_line(e):
            return slice(2 * e, 2 * e + 1)

        def col_line(e):
            return slice(2 * e + 1, 2 * e + 2)

        width = -(-epochs * RIM // LANES) * LANES
        upper, lower = [
            scaled_map(
                row_line,
                BAND,
                width,
                [(e, (shift - e * RIM, e * RIM, (e + 1) * RIM)) for e in range(epochs)],
            )
            for shift in (0, BAND - RIM)
        ]
        rim_maps = [
            jnp.where(is_odd, *pair).astype(BF16)[:, : epochs * RIM]
            for pair in ((upper, lower), (lower, upper))
        ]
        inner_maps, lefts, rights, gains = [], [], [], []
        for e in range(epochs):
            gains.append(scale[row_line(e)] * scale[col_line(e)] * cor_ref[0, 0, e].astype(F32))
            inner_maps.append(
                scaled_map(row_line, inner, side, [(e, (reach - BAND, 0, WINDOW))])
                .astype(BF16)[:, :WINDOW]
            )
            turned = kept[col_line(e)]
            same, behind, ahead = (
                toeplitz(turned, LANES, LANES, shift, 0, LANES).astype(BF16)
                for shift in (0, -LANES, LANES)
            )
            zero = jnp.zeros_like(same)
            lower = jnp.concatenate([behind, same], axis=1)
            lefts.append(jnp.concatenate([jnp.concatenate([same, ahead], axis=1), lower], axis=0))
            rights.append(jnp.concatenate([jnp.concatenate([zero, ahead], axis=1), lower], axis=0))

    def pixels(e, segment):
        at = segments[segment]
        masked = inv_ref[e, at] * val_ref[e, at].astype(F32) * gains[e]
        return jnp.concatenate([(masked * exp_ref[e, at]).astype(BF16), masked.astype(BF16)], axis=0)

    def columns(part, e):
        left = dot(part[:, :side], lefts[e])
        right = dot(part[:, pcols - side :], rights[e])
        wide = jnp.concatenate(
            [left[:, :LANES], left[:, LANES:] + right[:, :LANES], right[:, LANES:]], axis=1
        ).astype(BF16)
        half = wide.shape[0] // 2
        return jnp.concatenate([wide[:half], wide[half:]], axis=1)

    ends = (slice(0, LANES), slice(pcols - LANES, pcols))

    def arrive(segment):
        for which in range(3):
            load(segment, which).wait()

    ways = (1 - odd, odd)

    def warp_columns(segment):
        warped = [columns(pixels(e, segment), e) for e in range(epochs)]
        for e in range(epochs):
            slab[e, segments[segment]] = warped[e]
        return warped

    def warp_rim(slot, warped):
        value = dot(rim_maps[slot], jnp.concatenate(warped, axis=0))
        into = pl.ds(pl.multiple_of(ways[slot] * (prows - BAND), 8), BAND)
        for plane in range(2):
            tile[plane, into, :] = value[:, plane * pcols : (plane + 1) * pcols]

    def dec_give(slot):
        way = ways[slot]
        rim_at = pl.ds(pl.multiple_of(way * (prows - BAND), 8), BAND)
        for plane in range(2):
            for end in range(2):
                dec_out[way, plane, :, end * LANES : (end + 1) * LANES] = tile[
                    plane, rim_at, ends[end]
                ].astype(BF16)
            dec_core_out[way, plane] = tile[plane, rim_at, LANES : 2 * LANES].astype(BF16)

    with jax.named_scope("near_rim"):
        arrive(0)
        warp_rim(0, warp_columns(0))
        dec_give(0)
    with jax.named_scope("barrier"):
        pl.semaphore_wait(
            barrier,
            1
            + not_first.astype(jnp.int32)
            + has_prev.astype(jnp.int32)
            + has_next.astype(jnp.int32)
            + (has_far & (is_even | is_last)).astype(jnp.int32)
            + (has_far & is_even & not_first).astype(jnp.int32),
        )

    def dec_copy(way):
        return pltpu.make_async_remote_copy(
            src_ref=dec_out.at[way],
            dst_ref=dec_in.at[way],
            send_sem=local_sem.at[3 + way],
            recv_sem=dec_recv.at[way],
            device_id=(me_ra, me_dec + (1 if way else -1)),
            device_id_type=MESH,
        )

    def dec_core_copy(way):
        return pltpu.make_async_remote_copy(
            src_ref=dec_core_out.at[way],
            dst_ref=dec_core_in.at[way],
            send_sem=local_sem.at[(5, 1)[way]],
            recv_sem=dec_core_recv.at[way],
            device_id=(me_ra, me_dec + (1 if way else -1)),
            device_id_type=MESH,
        )

    def ra_copy(out, into, send, recv, way, to_dec):
        return pltpu.make_async_remote_copy(
            src_ref=out.at[way],
            dst_ref=into.at[way],
            send_sem=local_sem.at[send[way]],
            recv_sem=recv.at[way],
            device_id=(next_ra if way else prev_ra, to_dec),
            device_id_type=MESH,
        )

    def own_copy(way, size):
        return pltpu.make_async_remote_copy(
            src_ref=own_out.at[way, 0:size],
            dst_ref=own_in.at[way, 0:size],
            send_sem=local_sem.at[7 + way],
            recv_sem=own_recv.at[way],
            device_id=(next_ra if way else prev_ra, me_dec),
            device_id_type=MESH,
        )

    def own_each(action):
        @pl.when(has_far)
        def _():
            action(wide_at, (OWN + HALO) * 3 // 2)

        @pl.when(jnp.logical_not(has_far))
        def _():
            action(own_at, OWN * 3 // 2)

    def own_start(way):
        own_each(lambda at, size: own_copy(way, size).start())

    def own_take(way, end):
        def take(at, size):
            own_copy(way, size).wait_recv()
            for plane, value in enumerate(unpacked(own_in[way, :size], way)):
                tile[plane, at, ends[end]] += value

        own_each(take)

    def near_copy(way):
        return ra_copy(near_out, near_in, (2, 6), near_recv, way, me_dec)

    def corner_copy(way):
        return ra_copy(corner_out, corner_in, (9, 10), corner_recv, way, far)

    def dec_send(way):
        dec_copy(way).start()
        dec_core_copy(way).start()

    def far_dec_send(way):
        dec_core_copy(way).start()
        dec_copy(way).start()

    pl.when(is_odd)(functools.partial(dec_send, 0))
    pl.when(is_even & has_next)(functools.partial(dec_send, 1))

    def edge_at(part):
        first = 2 * MARGIN - BAND + part * (prows - 4 * MARGIN + BAND)
        return pl.ds(pl.multiple_of(first, 8), BAND)

    far_rim = pl.ds(pl.multiple_of(odd * (prows - BAND), 8), BAND)
    own_at = pl.ds(pl.multiple_of(MARGIN + odd * MARGIN, 8), OWN)
    wide_at = pl.ds(pl.multiple_of(MARGIN - HALO + odd * BAND, 8), OWN + HALO)
    far_at, near_at = edge_at(odd), edge_at(1 - odd)

    @pl.when(has_far & is_even & not_first)
    def _():
        pl.semaphore_signal(ready_corner, inc=1, device_id=(prev_ra, far), device_id_type=MESH)

    @pl.when(has_far & is_even & not_last)
    def _():
        pl.semaphore_signal(ready_corner, inc=1, device_id=(next_ra, far), device_id_type=MESH)

    @pl.when(is_last)
    def _():
        pl.semaphore_signal(ready_wrap, inc=1, device_id=(next_ra, me_dec), device_id_type=MESH)

    @pl.when(is_last & has_far)
    def _():
        pl.semaphore_signal(ready_wrap, inc=1, device_id=(next_ra, far), device_id_type=MESH)

    with jax.named_scope("inner"):
        arrive(1)
        warp_columns(1)
        far_in = pl.ds(pl.multiple_of(odd * top_first, GROUP), RIM)
        warp_rim(1, [slab[e, far_in] for e in range(epochs)])
        value = functools.reduce(
            jnp.add,
            [dot(inner_maps[e], slab[e, reach : reach + WINDOW]) for e in range(epochs)],
        )
        for plane in range(2):
            tile[plane, BAND : BAND + inner, :] = value[:, plane * pcols : (plane + 1) * pcols]

    def corner_give(way):
        corner_out[way] = packed(tile[:, far_rim, ends[way]], way)

    def own_give(way):
        def give(at, size):
            own_out[way, :size] = packed(tile[:, at, ends[way]], way)
            if way:
                own_copy(1, size).start()
            else:

                @pl.when(not_first)
                def _():
                    own_copy(0, size).start()

        own_each(give)

    def add_band(way, at):
        for end in range(2):
            tile[:, at, ends[end]] += dec_in[way, :, :, end * LANES : (end + 1) * LANES].astype(F32)

    with jax.named_scope("corner_send"):

        @pl.when(has_far & is_even)
        def _():
            corner_give(1)
            corner_copy(1).start()
            corner_give(0)

            @pl.when(not_first)
            def _():
                corner_copy(0).start()

    with jax.named_scope("own_send"):
        own_give(1)

    with jax.named_scope("near_send"):
        for part, present in ((0, is_odd), (1, has_next & is_even)):

            @pl.when(present)
            def _():
                dec_copy(1 - part).wait_recv()
                add_band(1 - part, edge_at(part))

        near_out[1] = packed(tile[:, near_at, ends[1]], 1)

        @pl.when(not_last | is_even)
        def _():
            near_copy(1).start()

    with jax.named_scope("far_send"):
        own_give(0)
        near_out[0] = packed(tile[:, near_at, ends[0]], 0)

        @pl.when(not_first)
        def _():
            near_copy(0).start()

        @pl.when(has_far)
        def _():
            dec_give(1)
            pl.when(is_even)(functools.partial(far_dec_send, 0))
            pl.when(is_odd)(functools.partial(far_dec_send, 1))

        @pl.when(has_far & is_odd)
        def _():
            for way in (1, 0):
                corner_give(way)

        @pl.when(is_last & is_odd)
        def _():
            near_copy(1).start()

    small[3].wait()
    side_k = psf_ref.shape[0]
    taps[...] = jnp.zeros_like(taps)
    taps[ROW_PAD : ROW_PAD + side_k, 0:side_k] = psf_ref[...].astype(F32)
    offset = MARGIN - HALF
    across = lax.broadcasted_iota(jnp.int32, (LANES, LANES), 1)
    down = lax.broadcasted_iota(jnp.int32, (LANES, LANES), 0)
    last_tap = taps.shape[0] - 1
    mirror = jnp.where(across + down == last_tap, 1.0, 0.0).astype(BF16)
    taps[...] = dot(taps[...].astype(BF16), mirror)
    turn = LANES - last_tap - offset
    level = across - down >= turn

    def build(k, carry):
        for s in range(GROUP // 2):
            at = pl.ds(pl.multiple_of((k * (GROUP // 2) + s) * LANES, LANES), LANES)
            for parity in range(2):
                row = taps[pl.ds(k * GROUP + 2 * s + parity, 1), :]
                spread_row = jnp.broadcast_to(row, (LANES, LANES))
                turned = pltpu.roll(spread_row, turn, 1, stride=1, stride_axis=0)
                for block in range(2):
                    first = (2 * block + parity) * LANES
                    keep = jnp.logical_not(level) if block else level
                    bands[at, first : first + LANES] = jnp.where(keep, turned, 0.0).astype(BF16)
        return carry

    with jax.named_scope("bands"):
        lax.fori_loop(0, groups, build, 0)

    @pl.when(has_far & is_odd & not_last)
    def _():
        pl.semaphore_wait(ready_corner, 1 + not_first.astype(jnp.int32))
        corner_copy(1).start()

    @pl.when(has_far & is_odd & is_last)
    def _():
        pl.semaphore_wait(ready_corner, 1)
        corner_copy(1).start()

    @pl.when(has_far & is_odd & not_first)
    def _():
        corner_copy(0).start()

    span = coadd.shape[0]
    above = HALF + ROW_PAD
    deep, tall = shifts.shape[0], rows + GROUP
    top = MARGIN - above

    def spread(into, where, held=(0, span), kept_rows=(0, deep)):
        first, last = held
        numer = tile[0, top + first : top + last, where]
        denom = tile[1, top + first : top + last, where]
        row_id = lax.broadcasted_iota(jnp.int32, (last - first, 1), 0) + (me_dec * rows + first - above)
        inside = (row_id >= 0) & (row_id < n_dec * rows)
        coadd[first:last, where] = jnp.where(inside, numer / jnp.maximum(denom, 1.0), 0.0).astype(BF16)
        first, last = kept_rows
        for s in range(GROUP // 2):
            into[first:last, s * LANES : (s + 1) * LANES] = coadd[
                2 * s + first : 2 * s + last, where
            ]

    @pl.when(is_first)
    def _():
        pl.semaphore_wait(ready_wrap, 1 + has_far.astype(jnp.int32))
        own_start(0)
        near_copy(0).start()

    @pl.when(is_first & has_far)
    def _():
        corner_copy(0).start()

    with jax.named_scope("far_receive"):
        for part, present in ((0, has_prev), (1, has_next)):

            @pl.when(present)
            def _():
                dec_core_copy(1 - part).wait_recv()
                tile[:, edge_at(part), LANES : 2 * LANES] += dec_core_in[1 - part].astype(F32)

    with jax.named_scope("middle"):
        spread(shifts, slice(LANES, 2 * LANES))
        inner_sum[...] = product(shifts, bands, 0, tall, slice(None))

    for part, present in ((0, has_prev & is_even), (1, has_next & is_odd)):

        @pl.when(present)
        def _():
            dec_copy(1 - part).wait_recv()
            add_band(1 - part, edge_at(part))

    weight_ref[:, MARGIN : MARGIN + LANES] = tile[1, MARGIN : MARGIN + rows, LANES : 2 * LANES]

    half = rows // 2
    reached = half + groups * GROUP

    def far_own(end):
        way = 1 - end

        @pl.when(has_far)
        def _():
            corner_copy(way).wait_recv()
            for plane, value in enumerate(unpacked(corner_in[way], way)):
                tile[plane, far_at, ends[end]] += value

        own_take(way, end)

    def near_weight(end):
        way = 1 - end
        near_copy(way).wait_recv()
        for plane, value in enumerate(unpacked(near_in[way], way)):
            tile[plane, near_at, ends[end]] += value
        into = slice(end * (cols - MARGIN), end * (cols - MARGIN) + MARGIN)
        first = pcols - LANES if end else MARGIN
        weight_ref[:, into] = tile[1, MARGIN : MARGIN + rows, first : first + MARGIN]

    late = late_end(n_ra)
    with jax.named_scope("early_end"):
        for end in range(2):

            @pl.when(late == 1 - end)
            def _():
                far_own(end)
                near_weight(end)
                spread(end_shifts.at[end], ends[end])
                matched_ref[:, end * LANES : (end + 1) * LANES] = end_sums(
                    end, inner_sum, end_shifts, bands, 0, rows
                )

    def way_sent(way):
        own_each(lambda at, size: own_copy(way, size).wait_send())
        near_copy(way).wait_send()

        @pl.when(has_far)
        def _():
            corner_copy(way).wait_send()

    with jax.named_scope("sent"):
        for way, present in ((0, has_prev), (1, has_next)):

            @pl.when(present)
            def _():
                dec_copy(way).wait_send()
                dec_core_copy(way).wait_send()

        way_sent(1)

        @pl.when(not_first)
        def _():
            way_sent(0)

    with jax.named_scope("late_end"):
        for end in range(2):

            @pl.when((late == end) & is_odd)
            def _():
                far_own(end)
                near_weight(end)
                spread(end_shifts.at[end], ends[end])

            @pl.when((late == end) & is_even)
            def _():
                far_own(end)
                spread(end_shifts.at[end], ends[end], (0, reached), (0, reached))
                matched_ref[:half, end * LANES : (end + 1) * LANES] = end_sums(
                    end, inner_sum, end_shifts, bands, 0, half
                )
                near_weight(end)
                spread(
                    end_shifts.at[end], ends[end], (reached, reached + half), (reached - GROUP, deep)
                )

    @pl.when(is_first)
    def _():
        way_sent(0)


def finish(
    n_ra, matched_in, weight_in, bands, inner_sum, end_shifts, matched_out, weight_out, held, sems
):
    weight = pltpu.make_async_copy(weight_in, weight_out, sems.at[0])
    weight.start()
    late = late_end(n_ra)
    rows = held.shape[0]
    odd = lax.rem(lax.axis_index("dec"), 2)
    for end in range(2):
        for parity, first in ((1, 0), (0, rows // 2)):

            @pl.when((late == end) & (odd == parity))
            def _():
                early_at = slice((1 - end) * LANES, (2 - end) * LANES)
                late_at = slice(end * LANES, (end + 1) * LANES)
                copies = [
                    pltpu.make_async_copy(
                        matched_in.at[:, early_at], matched_out.at[:, early_at], sems.at[1]
                    ),
                    pltpu.make_async_copy(
                        held.at[first:rows], matched_out.at[first:rows, late_at], sems.at[2]
                    ),
                ]
                if first:
                    copies.append(
                        pltpu.make_async_copy(
                            matched_in.at[0:first, late_at],
                            matched_out.at[0:first, late_at],
                            sems.at[3],
                        )
                    )

                held[first:rows] = end_sums(
                    end, inner_sum, end_shifts, bands, first, rows - first
                )
                copies[1].start()
                copies[0].start()
                if first:
                    copies[2].start()
                for copy in copies:
                    copy.wait()

    weight.wait()


def solution(mesh):
    n_ra, n_dec = mesh.shape["ra"], mesh.shape["dec"]

    def shards(exposures, inv_variance, pixel_valid, correlation, pixel_offset, subpixel, psf_match):
        epochs, prows, pcols = exposures.shape
        rows, cols = prows - 2 * MARGIN, pcols - 2 * MARGIN
        groups = -(-psf_match.shape[0] // GROUP)
        deep = rows + GROUP * groups
        result = jax.ShapeDtypeStruct((rows, cols), F32)
        hbm = pl.BlockSpec(memory_space=pltpu.HBM)
        vmem = pl.BlockSpec(memory_space=pltpu.VMEM)
        sums = pl.pallas_call(
            functools.partial(kernel, (epochs, prows, pcols, n_ra, n_dec)),
            out_shape=(
                result,
                result,
                jax.ShapeDtypeStruct((groups * GROUP // 2 * LANES, 4 * LANES), BF16),
                jax.ShapeDtypeStruct((rows + GROUP, 4 * LANES), F32),
                jax.ShapeDtypeStruct((2, deep, GROUP // 2 * LANES), BF16),
            ),
            in_specs=[hbm] * 7,
            out_specs=(vmem,) * 5,
            scratch_shapes=[
                pltpu.VMEM((epochs, prows, pcols), F32),
                pltpu.VMEM((epochs, prows, pcols), F32),
                pltpu.VMEM((epochs, prows, pcols), jnp.int32),
                pltpu.SMEM(correlation.shape, jnp.int32),
                pltpu.SMEM(pixel_offset.shape, jnp.int32),
                pltpu.SMEM(subpixel.shape, F32),
                pltpu.VMEM(psf_match.shape, BF16),
                pltpu.VMEM((2, prows, pcols), F32),
                pltpu.VMEM((epochs, prows, 2 * pcols), BF16),
                pltpu.VMEM((2, 2, BAND, 2 * LANES), BF16),
                pltpu.VMEM((2, 2, BAND, 2 * LANES), BF16),
                pltpu.VMEM((2, 2, BAND, LANES), BF16),
                pltpu.VMEM((2, 2, BAND, LANES), BF16),
                pltpu.VMEM((2, (OWN + HALO) * 3 // 2, LANES), BF16),
                pltpu.VMEM((2, (OWN + HALO) * 3 // 2, LANES), BF16),
                pltpu.VMEM((2, BAND * 3 // 2, LANES), BF16),
                pltpu.VMEM((2, BAND * 3 // 2, LANES), BF16),
                pltpu.VMEM((2, BAND * 3 // 2, LANES), BF16),
                pltpu.VMEM((2, BAND * 3 // 2, LANES), BF16),
                pltpu.VMEM((groups * GROUP, LANES), F32),
                pltpu.VMEM((deep + GROUP, pcols), BF16),
                pltpu.VMEM((deep, GROUP // 2 * LANES), BF16),
                pltpu.SemaphoreType.DMA((11,)),
                pltpu.SemaphoreType.DMA((2,)),
                pltpu.SemaphoreType.DMA((2,)),
                pltpu.SemaphoreType.DMA((2,)),
                pltpu.SemaphoreType.DMA((2,)),
                pltpu.SemaphoreType.DMA((2,)),
                pltpu.SemaphoreType.REGULAR,
                pltpu.SemaphoreType.REGULAR,
            ],
            compiler_params=pltpu.CompilerParams(
                collective_id=0, has_side_effects=True, vmem_limit_bytes=24 * 1024 * 1024
            ),
            name="coadd",
        )(*[pltpu.with_memory_space_constraint(x, pltpu.HBM) for x in (exposures, inv_variance, pixel_valid, correlation, pixel_offset, subpixel, psf_match)])
        return pl.pallas_call(
            functools.partial(finish, n_ra),
            out_shape=(result, result),
            in_specs=[vmem] * 5,
            out_specs=(hbm, hbm),
            scratch_shapes=[pltpu.VMEM((rows, LANES), F32), pltpu.SemaphoreType.DMA((4,))],
            compiler_params=pltpu.CompilerParams(vmem_limit_bytes=8 * 1024 * 1024),
            name="finish",
        )(*sums)

    return jax.shard_map(
        shards,
        mesh=mesh,
        in_specs=(
            P(None, "dec", "ra"),
            P(None, "dec", "ra"),
            P(None, "dec", "ra"),
            P("dec", "ra", None),
            P("dec", "ra", None, None),
            P("dec", "ra", None, None),
            P(),
        ),
        out_specs=(P("dec", "ra"), P("dec", "ra")),
        check_vma=False,
    )
```
